32 devices in a mesh: dp: 8 (over y, x, core), seq: 4 (over z).
Axes of the slice: x: 2, y: 2, z: 4, core: 2. Of those that a mesh axis runs over, the one named last changes fastest.
Arguments:
- tokens: bfloat16 [2, 8, 1024, 768], P(None, 'dp', 'seq'), may hold values from -6 to 6
- lengths: int32 [2, 8], P(None, 'dp'), may hold values from 256 to 1024, as said below
- dealing: int32 [2, 8], P(None, 'dp'), may hold values from 0 to 7, each once within a row
- cotangent: bfloat16 [2, 8, 1024, 768], P(None, 'dp', 'seq'), may hold values from -6 to 6
- in_weight: bfloat16 [768, 3352], P(('dp', 'seq')), may hold values from -0.21875 to 0.21875
- out_weight: bfloat16 [1536, 768], P(('dp', 'seq')), may hold values from -0.15625 to 0.15625
- norm_gain: bfloat16 [768], P(('dp', 'seq')), may hold values from 0.5 to 1.5
- gate_gain: bfloat16 [1536], P(('dp', 'seq')), may hold values from 0.5 to 1.5
- conv_weight: float32 [4, 1792], replicated, may hold values from -3 to 3
- conv_bias: float32 [1792], replicated, may hold values from -0.5 to 0.5
- decay_log: float32 [24], replicated, may hold values from -5 to 1
- step_bias: float32 [24], replicated, may hold values from -4 to -2
- skip_gain: float32 [24], replicated, may hold values from 0.5 to 1.5
Outputs:
- outputs: bfloat16 [2, 8, 1024, 768], P(None, 'dp', 'seq')
- grad_tokens: bfloat16 [2, 8, 1024, 768], P(None, 'dp', 'seq')
- grad_in_weight: float32 [768, 3352], P(('dp', 'seq'))
- grad_out_weight: float32 [1536, 768], P(('dp', 'seq'))
- grad_norm_gain: float32 [768], P(('dp', 'seq'))
- grad_gate_gain: float32 [1536], P(('dp', 'seq'))
- grad_conv_weight: float32 [4, 1792], replicated
- grad_conv_bias: float32 [1792], replicated
- grad_decay_log: float32 [24], replicated
- grad_step_bias: float32 [24], replicated
- grad_skip_gain: float32 [24], replicated
The draws below stay inside these ranges and needn't reach their ends.
Inputs may be any that keep to these rules, and one draw needn't show every extreme that they name: `lengths`: in every draw one sequence has exactly 1024 valid tokens and one exactly 256. Each row of dealing names every slot of its micro-batch once.
All inputs are finite; a program needn't handle non-finite values.
Results may differ from the reference program's by a relative error of at most 0.0075.
Values may be sent and summed in bfloat16 or wider, within the bound.
No kernel may reach another device: no remote copies, remote signals or barrier semaphores. Data moves between devices by JAX's collectives and lax.ppermute only.
A program may use at most 192 MiB of HBM per device.

```python
from functools import partial
import jax
import jax.numpy as jnp
from jax import lax

D = 768
INNER = 1536
HEADS = 24
HDIM = 64
STATE = 128
KCONV = 4
GROUP = 256
MICRO = 2
CONVCH = 1792
PROJ = 3352
SEQS = 8
LEN = 1024


def draw_lengths(key, part):
    total_count = MICRO * SEQS
    first_key, second_key = jax.random.split(jax.random.fold_in(key, 11))
    flat_lengths = jax.random.randint(first_key, (total_count,), LEN // 4, LEN + 1)
    chosen = jax.random.permutation(second_key, total_count)
    flat_lengths = flat_lengths.at[chosen[0]].set(LEN).at[chosen[1]].set(LEN // 4)
    return flat_lengths.reshape(MICRO, SEQS).astype(jnp.int32)


def block_levels(stream_key, dims, cuts, smallest, largest):
    def one(position, parts):
        heights = jax.random.uniform(jax.random.fold_in(jax.random.fold_in(stream_key, 6), position), (parts,), jnp.float32, smallest / len(cuts), largest / len(cuts))
        return jnp.repeat(jnp.exp(heights), dims[position] // parts).reshape((-1,) + (1,) * (len(dims) - position - 1))

    gain = one(*cuts[0])
    for cut in cuts[1:]:
        gain = gain * one(*cut)
    return gain


def noise(own_key, dims, spread, reach, shards=(), kind=jnp.bfloat16):
    result = jax.random.normal(own_key, dims, jnp.float32) * spread
    if len(shards) > 0:
        result = block_levels(own_key, dims, shards, -0.22, 0.18) * result
    return jnp.clip(result, min=-reach, max=reach).astype(kind)


def setup_inputs(seed: int = 0) -> dict:
    keys = jax.random.split(jax.random.key(seed), 14)
    return {
        "tokens": noise(keys[0], (MICRO, SEQS, LEN, D), 1.0, 6.0, ((1, 8), (2, 4))),
        "lengths": draw_lengths(jax.random.fold_in(keys[13], 71), 0),
        "dealing": jax.vmap(lambda own: jax.random.permutation(own, SEQS))(jax.random.split(keys[2], MICRO)).reshape((MICRO, SEQS)).astype(jnp.int32),
        "cotangent": noise(keys[3], (MICRO, SEQS, LEN, D), 1.0, 6.0, ((1, 8), (2, 4))),
        "in_weight": noise(keys[4], (D, PROJ), D ** -0.5, 0.21875, ((0, 32),)),
        "out_weight": noise(keys[5], (INNER, D), INNER ** -0.5, 0.15625, ((0, 32),)),
        "norm_gain": jnp.clip(1.0 + 0.1 * jax.random.normal(keys[6], (D,), jnp.float32), 0.5, 1.5).astype(jnp.bfloat16),
        "gate_gain": jnp.clip(1.0 + 0.1 * jax.random.normal(keys[7], (INNER,), jnp.float32), 0.5, 1.5).astype(jnp.bfloat16),
        "conv_weight": noise(keys[8], (KCONV, CONVCH), KCONV ** -0.5, 3.0, (), jnp.float32),
        "conv_bias": jnp.clip(jax.random.uniform(keys[9], (CONVCH,), jnp.float32, -0.5, 0.5), -0.5, 0.5),
        "decay_log": jnp.clip(jax.random.uniform(keys[10], (HEADS,), jnp.float32, -5.0, 1.0), -5.0, 1.0),
        "step_bias": jnp.clip(jax.random.uniform(keys[11], (HEADS,), jnp.float32, -4.0, -2.0), -4.0, -2.0),
        "skip_gain": jnp.clip(jax.random.uniform(keys[12], (HEADS,), jnp.float32, 0.5, 1.5), 0.5, 1.5),
    }


EPSILON = 1e-05
PRECISE = lax.Precision.HIGHEST

@jax.custom_vjp
def low(v):
    return lax.optimization_barrier(v.astype(jnp.bfloat16)).astype(jnp.float32)

@jax.custom_vjp
def low_back(v):
    return v

def low_keep(v):
    return (low(v), None)

def low_pass(kept, grad):
    return (grad,)

def back_keep(v):
    return (v, None)

def back_low(kept, grad):
    return (low(grad),)
low.defvjp(low_keep, low_pass)
low_back.defvjp(back_keep, back_low)

def norm_rows(values, gain_row):
    return values * lax.rsqrt(lax.optimization_barrier(jnp.mean(values * values, axis=-1, keepdims=True)) + EPSILON) * gain_row

def block_step(skip_gain, state_in, pieces):
    values, in_keys, out_keys, step_size, log_decay = pieces
    cumulative = jnp.cumsum(log_decay, axis=0)
    causal = (jnp.arange(GROUP)[:, None] >= jnp.arange(GROUP)[None, :])[:, :, None]
    spread_diff = cumulative[:, None, :] - cumulative[None, :, :]
    segment = jnp.where(causal, jnp.exp(jnp.where(causal, spread_diff, 0.0)), 0.0)
    affinity = low_back(jnp.dot(out_keys, in_keys.T, precision=PRECISE))
    mixing = low(affinity[:, :, None] * segment * step_size[None, :, :])
    local_part = jnp.einsum('tsh,shp->thp', mixing, values, precision=PRECISE)
    carried_part = jnp.exp(cumulative)[:, :, None] * jnp.einsum('tn,hpn->thp', out_keys, state_in, precision=PRECISE)
    core_out = low_back(local_part + carried_part)
    mixed_out = core_out + skip_gain[None, :, None] * values
    weights_in = jnp.exp(cumulative[-1][None, :] - cumulative) * step_size
    update = jnp.einsum('thp,tn->hpn', weights_in[:, :, None] * values, in_keys, precision=PRECISE)
    new_state = jnp.exp(cumulative[-1])[:, None, None] * state_in + update
    return (new_state, mixed_out)

def sequence_forward(weights, inputs, length):
    in_weight, out_weight, norm_gain, gate_gain, conv_weight, conv_bias, decay_log, step_bias, skip_gain = weights
    channels = INNER + 2 * STATE
    normed = low(norm_rows(inputs, norm_gain))
    projected = low_back(jnp.dot(normed, in_weight, precision=PRECISE))
    gate_in = projected[:, :INNER]
    conv_in = projected[:, INNER:INNER + channels]
    step_raw = projected[:, INNER + channels:]
    padded = jnp.pad(conv_in, ((KCONV - 1, 0), (0, 0)))
    conv_out = conv_bias[None, :] + jnp.zeros((LEN, channels), jnp.float32)
    for offset in range(KCONV):
        conv_out = conv_out + conv_weight[offset][None, :] * padded[offset:offset + LEN]
    activated = jax.nn.silu(conv_out)
    values = low(activated[:, :INNER]).reshape(LEN, HEADS, HDIM)
    in_keys = low(activated[:, INNER:INNER + STATE])
    out_keys = low(activated[:, INNER + STATE:])
    valid_mask = (jnp.arange(LEN, dtype=jnp.int32) < length).astype(jnp.float32)
    step_size = jax.nn.softplus(step_raw + step_bias[None, :]) * valid_mask[:, None]
    log_decay = -jnp.exp(decay_log)[None, :] * step_size
    blocks = LEN // GROUP
    pieces = (values.reshape(blocks, GROUP, HEADS, HDIM), in_keys.reshape(blocks, GROUP, STATE), out_keys.reshape(blocks, GROUP, STATE), step_size.reshape(blocks, GROUP, HEADS), log_decay.reshape(blocks, GROUP, HEADS))
    step_fn = jax.checkpoint(partial(block_step, skip_gain))
    final_state, mixed_out = lax.scan(step_fn, jnp.zeros((HEADS, HDIM, STATE), jnp.float32), pieces)
    mixed_out = mixed_out.reshape(LEN, INNER)
    gated = mixed_out * jax.nn.silu(gate_in)
    normed_out = low(norm_rows(gated, gate_gain))
    branch = jnp.dot(normed_out, out_weight, precision=PRECISE)
    return inputs + valid_mask[:, None] * branch

def reference(tokens, lengths, dealing, cotangent, in_weight, out_weight, norm_gain, gate_gain, conv_weight, conv_bias, decay_log, step_bias, skip_gain):
    weights = tuple((weight.astype(jnp.float32) for weight in (in_weight, out_weight, norm_gain, gate_gain, conv_weight, conv_bias, decay_log, step_bias, skip_gain)))
    micro_index = jnp.arange(MICRO, dtype=jnp.int32)[:, None]
    slots = dealing.astype(jnp.int32)
    dealt_tokens = jnp.zeros_like(tokens).at[micro_index, slots].set(tokens)
    dealt_lengths = jnp.zeros_like(lengths).at[micro_index, slots].set(lengths)
    sequence_count = MICRO * SEQS
    inputs = dealt_tokens.reshape(sequence_count, LEN, D).astype(jnp.float32)
    length_list = dealt_lengths.reshape(sequence_count).astype(jnp.int32)
    cot_rows = cotangent.reshape(sequence_count, LEN, D).astype(jnp.float32)

    def forward(weights, inputs):

        def visit_one(carried, element):
            return (carried, jax.checkpoint(sequence_forward)(weights, element[0], element[1]))
        return lax.scan(visit_one, None, (inputs, length_list))[1]
    outputs, pullback = jax.vjp(forward, weights, inputs)
    grad_weights, grad_inputs = pullback(cot_rows)
    grad_dealt = grad_inputs.reshape(MICRO, SEQS, LEN, D)
    grad_given = jnp.take_along_axis(grad_dealt, slots[:, :, None, None], axis=1)
    return (outputs.reshape(tokens.shape).astype(jnp.bfloat16), grad_given.astype(jnp.bfloat16), grad_weights[0], grad_weights[1], grad_weights[2], grad_weights[3], grad_weights[4], grad_weights[5], grad_weights[6], grad_weights[7], grad_weights[8])
```

```python
import functools

import jax
import jax.numpy as jnp
from jax import lax
from jax.experimental import pallas as pl
from jax.experimental.pallas import tpu as pltpu
from jax.sharding import PartitionSpec as P

INNER = 1536
HEADS = 24
HDIM = 64
STATE = 128
KCONV = 4
CHANNELS = INNER + 2 * STATE
LANES = 128
CHUNK = 128
HALO = 16
EPSILON = 1e-05
WIDTH = CHANNELS + LANES
SPLIT = 1024
F32 = jnp.float32
BF16 = jnp.bfloat16
BOTH = ("dp", "seq")
VMEM_LIMIT = 60 * 1024 * 1024


def flip_dp(value, mask):
    pairs = [(i, i ^ mask) for i in range(lax.axis_size("dp"))]
    return lax.ppermute(value, "dp", pairs)


def shift_seq(value, step):
    size = lax.axis_size("seq")
    return lax.ppermute(value, "seq", [(i, (i + step) % size) for i in range(size)])


def column_place(dp_even, lin):
    return (dp_even + lin % 2) * lax.axis_size("seq") + lin // 2


def unit_pairs(parity):
    size = lax.axis_size("seq")
    pairs = []
    for dp in range(lax.axis_size("dp")):
        core = dp % 2
        for block in range(size):
            micro = (block % 2) ^ parity
            lin = (2 * micro + core) * (size // 2) + block // 2
            pairs.append((dp * size + block, column_place(dp - core, lin)))
    return pairs


def neighbour_pairs(step):
    size = lax.axis_size("seq")
    group = size // 2
    pairs = []
    for dp_even in range(0, lax.axis_size("dp"), 2):
        for lin in range(2 * size):
            if 0 <= lin % group + step < group:
                pairs.append((column_place(dp_even, lin), column_place(dp_even, lin + step)))
    return pairs


def reversed_pairs(pairs):
    return [(target, source) for source, target in pairs]


def to_stretch(blocks, place):
    odd = place["seq"] % 2 == 1
    late = place["micro"] == 1
    first = lax.ppermute(jnp.where(odd, blocks[1], blocks[0]), BOTH, unit_pairs(0))
    second = lax.ppermute(jnp.where(odd, blocks[0], blocks[1]), BOTH, unit_pairs(1))
    return jnp.where(late, second, first), jnp.where(late, first, second)


def from_stretch(first, second, place):
    odd = place["seq"] % 2 == 1
    late = place["micro"] == 1
    one = lax.ppermute(jnp.where(late, second, first), BOTH, reversed_pairs(unit_pairs(0)))
    two = lax.ppermute(jnp.where(late, first, second), BOTH, reversed_pairs(unit_pairs(1)))
    return jnp.where(odd, two, one), jnp.where(odd, one, two)


def seq_gather(shard, place):
    size = lax.axis_size("seq")
    got = [shard] + [shift_seq(shard, j) for j in range(1, size)]
    rows = []
    for i in range(size):
        row = got[0]
        for j in range(1, size):
            row = jnp.where((place["seq"] - i) % size == j, got[j], row)
        rows.append(row)
    return jnp.stack(rows)


def spread(block, bits):
    masks, held = (0,), block[None]
    last = None
    for bit in bits:
        if last is not None:
            masks, held = masks + last[0], jnp.concatenate([held, last[1]])
        last = (tuple(m ^ (1 << bit) for m in masks), flip_dp(held, 1 << bit))
    pieces = [(masks, held)] + ([last] if last is not None else [])
    return pieces + [(tuple(m ^ 1 for m in part[0]), flip_dp(part[1], 1)) for part in pieces]


def fold(parts, bits):
    order = {bit: i for i, bit in enumerate(sorted(bits, reverse=True))}
    shape = (2,) * len(bits) + parts.shape[1:]
    parts = parts.reshape(shape)
    axes = sorted(bits, reverse=True)
    for bit in bits:
        axis = axes.index(bit)
        axes.pop(axis)
        keep = lax.index_in_dim(parts, 0, axis, keepdims=False)
        give = lax.index_in_dim(parts, 1, axis, keepdims=False).astype(BF16)
        parts = keep + flip_dp(give, 1 << bit).astype(F32)
    del order
    return parts


def seq_scatter(parts, place):
    size = lax.axis_size("seq")
    total = lax.dynamic_index_in_dim(parts, place["seq"], 0, keepdims=False)
    for j in range(1, size):
        give = lax.dynamic_index_in_dim(parts, (place["seq"] + j) % size, 0, keepdims=False)
        total = total + shift_seq(give.astype(BF16), j).astype(F32)
    return total


def sum_everywhere(value):
    for bit in range(lax.axis_size("dp").bit_length() - 1):
        value = value + flip_dp(value, 1 << bit)
    size = lax.axis_size("seq")
    apart = 1
    while apart < size:
        pairs = [(i, i ^ apart) for i in range(size)]
        value = value + lax.ppermute(value, "seq", pairs)
        apart *= 2
    return value


def dp_table(row):
    table = row[None]
    for bit in range(lax.axis_size("dp").bit_length() - 1):
        table = jnp.concatenate([table, flip_dp(table, 1 << bit)])
    return table


def route_kernel(place_ref, table_ref, out_ref):
    dp = place_ref[0]
    size = table_ref.shape[0]
    for way in range(2):
        for micro in range(2):
            first_bit, second_bit = ((2, 4), (4, 2))[micro]
            goal = []
            for r in range(size):
                if way == 1:
                    goal.append(table_ref[r, micro])
                else:
                    found = jnp.int32(0)
                    for other in range(size):
                        hit = table_ref[other, micro] == jnp.bitwise_xor(dp, r)
                        found = jnp.where(hit, jnp.bitwise_xor(dp, other), found)
                    goal.append(found)
            held = [0, 1, first_bit, first_bit | 1]

            def chosen(base):
                low = jnp.int32(0)
                high = jnp.int32(0)
                for n in range(3, -1, -1):
                    away = jnp.bitwise_xor(goal[base ^ held[n]], jnp.bitwise_xor(dp, base))
                    cross = (jnp.bitwise_and(away, second_bit) != 0) & (
                        jnp.bitwise_and(away, first_bit) == 0
                    )
                    low = jnp.where(cross, n, low)
                for n in range(4):
                    away = jnp.bitwise_xor(goal[base ^ held[n]], jnp.bitwise_xor(dp, base))
                    cross = (jnp.bitwise_and(away, second_bit) != 0) & (
                        jnp.bitwise_and(away, first_bit) == 0
                    )
                    high = jnp.where(cross, n, high)
                return low, high

            low, high = chosen(0)
            other_low, _ = chosen(second_bit)
            row = way * 2 + micro
            out_ref[row, 0] = low
            out_ref[row, 1] = high
            for side in range(2):
                pick = jnp.int32(0)
                target = jnp.bitwise_xor(dp, side)
                for n in range(4):
                    pick = jnp.where(goal[held[n]] == target, n, pick)
                    far = jnp.where(other_low == n, 4, 5)
                    pick = jnp.where(goal[held[n] ^ second_bit] == target, far, pick)
                out_ref[row, 2 + side] = pick
    core = jnp.bitwise_and(dp, 1)
    column = jnp.bitwise_xor(core, place_ref[2])
    micro = place_ref[1]
    own = jnp.where(micro == 0, table_ref[0, 2], table_ref[0, 3])
    other = jnp.where(micro == 0, table_ref[1, 2], table_ref[1, 3])
    out_ref[4, 0] = jnp.where(column == 0, own, other)
    for n in range(1, 4):
        out_ref[4, n] = jnp.int32(0)


def make_routes(place, table):
    return pl.pallas_call(
        route_kernel,
        out_shape=jax.ShapeDtypeStruct((5, 4), jnp.int32),
        in_specs=[pl.BlockSpec(memory_space=pltpu.SMEM)] * 2,
        out_specs=pl.BlockSpec(memory_space=pltpu.SMEM),
    )(jnp.stack([place["dp"], place["micro"], place["column"]]), table)


def pick_of(entries, index):
    out = entries[0]
    for n in range(1, len(entries)):
        out = jnp.where(index == n, entries[n], out)
    return out


def deal(items, routes, place):
    low_core = place["dp"] % 2 == 0
    half = items.shape[1] // 2
    top, bottom = items[:, :half], items[:, half:]
    mine = jnp.where(low_core, top, bottom)
    got = flip_dp(jnp.where(low_core, bottom, top), 1)
    own, partner = [], []
    for micro in range(2):
        first_bit, second_bit = ((2, 4), (4, 2))[micro]
        pair = jnp.stack([mine[micro], got[micro]])
        came = flip_dp(pair, first_bit)
        held = [mine[micro], got[micro], came[0], came[1]]
        route = routes[micro]
        sent = jnp.stack([pick_of(held, route[0]), pick_of(held, route[1])])
        far = flip_dp(sent, second_bit)
        held = held + [far[0], far[1]]
        own.append(pick_of(held, route[2]))
        partner.append(pick_of(held, route[3]))
    own = jnp.stack(own)
    back = flip_dp(jnp.stack(partner), 1)
    return jnp.concatenate(
        [jnp.where(low_core, own, back), jnp.where(low_core, back, own)], axis=1
    )


def deal_gathered(items, source):
    every = lax.all_gather(items, "dp", axis=0)
    picked = [
        lax.dynamic_index_in_dim(every[:, m], source[m], 0, keepdims=False) for m in range(2)
    ]
    return jnp.stack(picked)


def dot(a, b, ca=1, cb=0):
    return lax.dot_general(a, b, (((ca,), (cb,)), ((), ())), preferred_element_type=F32)


def two_parts(x):
    high = x.astype(BF16)
    return high, (x - high.astype(F32)).astype(BF16)


def running_sum(x, reverse=False):
    rows = lax.broadcasted_iota(jnp.int32, (CHUNK, CHUNK), 0)
    cols = lax.broadcasted_iota(jnp.int32, (CHUNK, CHUNK), 1)
    reach = (rows <= cols) if reverse else (rows >= cols)
    reach = jnp.where(reach, 1.0, 0.0).astype(BF16)
    high, rest = two_parts(x)
    middle, low = two_parts(x - high.astype(F32))
    del rest
    return dot(reach, high) + dot(reach, middle) + dot(reach, low)


def fill_expander(expand_ref):
    head = lax.broadcasted_iota(jnp.int32, (LANES, INNER), 0)
    col = lax.broadcasted_iota(jnp.int32, (LANES, INNER), 1)
    one = jnp.where(col // HDIM == head, 1.0, 0.0).astype(BF16)
    expand_ref[0:LANES, :] = one
    expand_ref[LANES : 2 * LANES, :] = one


def head_sums(prod, tile):
    lane = lax.broadcasted_iota(jnp.int32, (LANES, LANES), 0)
    head = lax.broadcasted_iota(jnp.int32, (LANES, LANES), 1)
    one = jnp.where(2 * tile + lane // HDIM == head, 1.0, 0.0).astype(BF16)
    high, low = two_parts(prod)
    return dot(jnp.concatenate([high, low], axis=1), jnp.concatenate([one, one], axis=0))


def start_pieces(dp, pieces, plan, target, sem, rows):
    copies = []
    for piece, (masks, spots) in zip(pieces, plan):
        for n, mask in enumerate(masks):
            for source, scale, col, width in spots:
                first = pl.multiple_of(jnp.bitwise_xor(dp, mask) * (rows * scale), 8)
                copy = pltpu.make_async_copy(
                    piece.at[n, pl.ds(source, rows * scale), :],
                    target.at[pl.ds(first, rows * scale), pl.ds(col, width)],
                    sem.at[len(copies)],
                )
                copy.start()
                copies.append(copy)
    return copies


def wait_all(copies):
    for copy in copies:
        copy.wait()


def piece_count(plan):
    return sum(len(masks) * len(spots) for masks, spots in plan)


def gain_row(w_ref):
    return w_ref[:, CHANNELS:].astype(F32).T[HEADS : HEADS + 1]


def project_kernel(plan, rows, scal, x_ref, cw_ref, cb_ref, dl_ref, sb_ref, *refs):
    count = len(plan)
    pieces = refs[:count]
    nh_ref, cext_ref, act_ref, step_ref, sig_ref, cum_ref, upd_ref, tot_ref = refs[count : count + 8]
    w_ref, proj_ref, expand_ref, sem = refs[count + 8 :]
    copies = start_pieces(scal[0], pieces, plan, w_ref, sem, rows)
    total = x_ref.shape[0]
    length = total - HALO
    chunks = length // CHUNK
    fill_expander(expand_ref)

    def norm(i, carry):
        at = pl.ds(pl.multiple_of(i * HALO, HALO), HALO)
        u = x_ref[at, :].astype(F32)
        scale = lax.rsqrt(jnp.mean(u * u, axis=1, keepdims=True) + EPSILON)
        nh_ref[at, :] = (u * scale * gain).astype(BF16)
        return carry

    wait_all(copies)
    gain = gain_row(w_ref)
    lax.fori_loop(0, total // HALO, norm, 0)

    def project(j, carry):
        at = pl.ds(pl.multiple_of(j * 384, 384), 384)
        proj_ref[:, at] = dot(nh_ref[...], w_ref[:, at])
        return carry

    lax.fori_loop(0, WIDTH // 384, project, 0)

    def conv(idx, carry):
        i, j = idx // (CHANNELS // LANES), idx % (CHANNELS // LANES)
        cols = pl.ds(pl.multiple_of(j * LANES, LANES), LANES)
        first = pl.multiple_of(i * CHUNK, CHUNK)
        part = proj_ref[pl.ds(first, CHUNK + HALO), cols]
        weights = cw_ref[:, cols]
        out = cb_ref[0:1, cols] + weights[KCONV - 1 : KCONV] * part[HALO:]
        for k in range(KCONV - 1):
            out = out + weights[k : k + 1] * pltpu.roll(part, KCONV - 1 - k, 0)[HALO:]
        act_ref[pl.ds(first, CHUNK), cols] = (out * jax.nn.sigmoid(out)).astype(BF16)
        cext_ref[pl.ds(first + HALO, CHUNK), cols] = part[HALO:].astype(BF16)
        return carry

    lax.fori_loop(0, chunks * (CHANNELS // LANES), conv, 0)
    cext_ref[0:HALO, :] = proj_ref[0:HALO, 0:CHANNELS].astype(BF16)
    lane = lax.broadcasted_iota(jnp.int32, (CHUNK, LANES), 1)
    row = lax.broadcasted_iota(jnp.int32, (CHUNK, LANES), 0)
    rate = -jnp.exp(dl_ref[0:1, :])
    lasts = []
    for i in range(chunks):
        at = pl.ds(i * CHUNK, CHUNK)
        pre = proj_ref[pl.ds(HALO + i * CHUNK, CHUNK), pl.ds(CHANNELS, LANES)] + sb_ref[0:1, :]
        live = (row + i * CHUNK < scal[1]) & (lane < HEADS)
        soft = jnp.maximum(pre, 0.0) + jnp.log1p(jnp.exp(-jnp.abs(pre)))
        step = jnp.where(live, soft, 0.0)
        step_ref[at, :] = step
        sig_ref[at, :] = jnp.where(live, jax.nn.sigmoid(pre), 0.0)
        cum = running_sum(rate * step)
        cum_ref[at, :] = cum
        lasts.append(cum[CHUNK - 1 : CHUNK])
    after = jnp.zeros_like(lasts[0])
    for i in range(chunks - 1, -1, -1):
        at = pl.ds(i * CHUNK, CHUNK)
        weight = jnp.exp(lasts[i] + after - cum_ref[at, :]) * step_ref[at, :]
        wide = dot(jnp.concatenate(two_parts(weight), axis=1), expand_ref[...])
        values = act_ref[at, 0:INNER].astype(F32)
        keys = act_ref[at, INNER : INNER + STATE]
        update = dot(keys, (wide * values).astype(BF16), 0, 0)
        proj_ref[0:STATE, 0:INNER] = (
            update if i == chunks - 1 else proj_ref[0:STATE, 0:INNER] + update
        )
        after = after + lasts[i]
    upd_ref[...] = proj_ref[0:STATE, 0:INNER].astype(BF16)
    tot_ref[...] = jnp.broadcast_to(after, tot_ref.shape)


def mixing_parts(cum, cum_rows, step_rows, head):
    gap = jnp.minimum(cum[:, head : head + 1] - cum_rows[head : head + 1, :], 0.0)
    return jnp.exp(gap) * step_rows[head : head + 1, :]


def causal_tile():
    rows = lax.broadcasted_iota(jnp.int32, (CHUNK, CHUNK), 0)
    cols = lax.broadcasted_iota(jnp.int32, (CHUNK, CHUNK), 1)
    return rows >= cols


def local_kernel(plan, rows, scal, nh_ref, act_ref, step_ref, cum_ref, *refs):
    count = len(plan)
    pieces = refs[:count]
    local_ref, gate_ref, w_ref, sem = refs[count:]
    copies = start_pieces(scal[0], pieces, plan, w_ref, sem, rows)
    chunks = act_ref.shape[0] // CHUNK
    left = lax.broadcasted_iota(jnp.int32, (CHUNK, LANES), 1) < HDIM

    def chunk(c, carry):
        at = pl.ds(pl.multiple_of(c * CHUNK, CHUNK), CHUNK)
        in_keys = act_ref[at, INNER : INNER + STATE]
        out_keys = act_ref[at, INNER + STATE : CHANNELS]
        affinity = jnp.where(causal_tile(), dot(out_keys, in_keys, 1, 1), 0.0)
        cum = cum_ref[at, :]
        cum_rows = cum.T
        step_rows = step_ref[at, :].T
        for tile in range(INNER // LANES):
            cols = slice(tile * LANES, (tile + 1) * LANES)
            mixing = [
                (affinity * mixing_parts(cum, cum_rows, step_rows, 2 * tile + n)).astype(BF16)
                for n in range(2)
            ]
            values = act_ref[at, cols]
            zero = jnp.zeros_like(values)
            apart = jnp.concatenate(
                [jnp.where(left, values, zero), jnp.where(left, zero, values)], axis=0
            )
            local_ref[at, cols] = dot(jnp.concatenate(mixing, axis=1), apart)
        return carry

    lax.fori_loop(0, chunks, chunk, 0)
    wait_all(copies)

    def project(j, carry):
        at = pl.ds(pl.multiple_of(j * 384, 384), 384)
        gate_ref[:, at] = dot(nh_ref[HALO:, :], w_ref[:, at])
        return carry

    lax.fori_loop(0, INNER // 384, project, 0)


def middle_kernel(plan, rows, scal, local_ref, act_ref, step_ref, cum_ref, gate_ref, state_ref, x_ref, c_ref,
                  skip_ref, *refs):
    count = len(plan)
    pieces = refs[:count]
    out_ref, gn_ref, dgate_ref, gcore_ref, rowq_ref, lsg_ref, states_ref, gskip_ref = refs[
        count : count + 8
    ]
    w_ref, gain_ref, mc_ref, gno_ref, state_s, wide_ref, core_ref, mixed_ref, acc_ref, expand_ref, sem = refs[
        count + 8 :
    ]
    copies = start_pieces(scal[0], pieces, plan, w_ref, sem, rows)
    length = act_ref.shape[0]
    chunks = length // CHUNK
    tiles = INNER // LANES
    model = c_ref.shape[1]
    fill_expander(expand_ref)

    def mask(i, carry):
        at = pl.ds(pl.multiple_of(i * CHUNK, CHUNK), CHUNK)
        row = lax.broadcasted_iota(jnp.int32, (CHUNK, model), 0) + i * CHUNK
        c = c_ref[at, :]
        mc_ref[at, :] = jnp.where(row < scal[1], c.astype(F32), 0.0).astype(BF16)
        return carry

    lax.fori_loop(0, chunks, mask, 0)
    wait_all(copies)

    def back_project(j, carry):
        at = pl.ds(pl.multiple_of(j * 384, 384), 384)
        gno_ref[:, at] = dot(mc_ref[...], w_ref[at, 0:model], 1, 1)
        return carry

    lax.fori_loop(0, INNER // 384, back_project, 0)
    gain_ref[...] = w_ref[:, model:].astype(F32).T[0:8]
    state_s[...] = state_ref[...].astype(F32)
    acc_ref[...] = jnp.zeros_like(acc_ref)
    gskip_ref[...] = jnp.zeros_like(gskip_ref)

    def chunk(c, before):
        at = pl.ds(pl.multiple_of(c * CHUNK, CHUNK), CHUNK)
        in_keys = act_ref[at, INNER : INNER + STATE]
        out_keys = act_ref[at, INNER + STATE : CHANNELS]
        cum = cum_ref[at, :]
        last = cum[CHUNK - 1 : CHUNK]
        growth = jnp.exp(cum)
        weight = jnp.exp(last - cum) * step_ref[at, :]
        small = jnp.concatenate(
            [growth, weight, jnp.exp(cum + before), jnp.broadcast_to(jnp.exp(last), (8, LANES))], axis=0
        )
        wide_ref[...] = dot(jnp.concatenate(two_parts(small), axis=1), expand_ref[...])
        state_b = state_s[...].astype(BF16)
        states_ref[c] = state_b
        squares = jnp.zeros((CHUNK, LANES), F32)
        for tile in range(tiles):
            cols = slice(tile * LANES, (tile + 1) * LANES)
            values = act_ref[at, cols].astype(F32)
            readout = dot(out_keys, state_b[:, cols])
            core = local_ref[at, cols] + wide_ref[0:CHUNK, cols] * readout
            mixed = core + skip_ref[0:1, cols] * values
            core_ref[:, cols] = core
            mixed_ref[:, cols] = mixed
            gate = gate_ref[at, cols]
            gated = mixed * (gate * jax.nn.sigmoid(gate))
            squares = squares + gated * gated
            weighted = (wide_ref[CHUNK : 2 * CHUNK, cols] * values).astype(BF16)
            state_s[:, cols] = wide_ref[3 * CHUNK : 3 * CHUNK + 1, cols] * state_s[:, cols] + dot(
                in_keys, weighted, 0, 0
            )
        scale = lax.rsqrt(jnp.sum(squares, axis=1, keepdims=True) / INNER + EPSILON)
        products = jnp.zeros((CHUNK, LANES), F32)
        for tile in range(tiles):
            cols = slice(tile * LANES, (tile + 1) * LANES)
            gate = gate_ref[at, cols]
            gn = mixed_ref[:, cols] * (gate * jax.nn.sigmoid(gate)) * scale
            gain = gain_ref[0:1, cols]
            gn_ref[at, cols] = (gn * gain).astype(BF16)
            products = products + gn * (gno_ref[at, cols] * gain)
        mean = jnp.sum(products, axis=1, keepdims=True) / INNER
        rowq = jnp.zeros((CHUNK, LANES), F32)
        for tile in range(tiles):
            cols = slice(tile * LANES, (tile + 1) * LANES)
            gate = gate_ref[at, cols]
            sig = jax.nn.sigmoid(gate)
            silu = gate * sig
            mixed = mixed_ref[:, cols]
            dgated = scale * (gno_ref[at, cols] * gain_ref[0:1, cols] - (mixed * silu * scale) * mean)
            g = dgated * silu
            dgate_ref[at, cols] = (dgated * mixed * (sig * (1.0 + gate * (1.0 - sig)))).astype(BF16)
            gcore = g.astype(BF16)
            gcore_ref[at, cols] = gcore
            values = act_ref[at, cols].astype(F32)
            gskip_ref[:, cols] = gskip_ref[:, cols] + jnp.sum(
                (g * values).reshape(CHUNK // 8, 8, LANES), axis=0
            )
            gcore_f = gcore.astype(F32)
            rowq = rowq + head_sums(gcore_f * core_ref[:, cols], tile)
            scaled = (wide_ref[2 * CHUNK : 3 * CHUNK, cols] * gcore_f).astype(BF16)
            acc_ref[:, cols] = acc_ref[:, cols] + dot(out_keys, scaled, 0, 0)
        rowq_ref[at, :] = rowq
        return before + last

    lax.fori_loop(0, chunks, chunk, jnp.zeros((1, LANES), F32))
    lsg_ref[...] = acc_ref[...].astype(BF16)

    def finish(i, carry):
        at = pl.ds(pl.multiple_of(i * CHUNK, CHUNK), CHUNK)
        row = lax.broadcasted_iota(jnp.int32, (CHUNK, model), 0) + i * CHUNK
        u = x_ref[pl.ds(pl.multiple_of(i * CHUNK + HALO, HALO), CHUNK), :].astype(F32)
        out_ref[at, :] = (u + jnp.where(row < scal[1], gno_ref[at, 0:model], 0.0)).astype(BF16)
        return carry

    for j in range(2):
        cols = slice(j * model // 2, (j + 1) * model // 2)
        gno_ref[:, cols] = dot(gn_ref[...], w_ref[:, cols])
    lax.fori_loop(0, chunks, finish, 0)


def put_block(dp, block, keep_ref, send_ref, start, cols, part):
    away = jnp.bitwise_xor(dp, block)
    slot = away // 2
    rows = part.shape[0]

    @pl.when(away % 2 == 0)
    def _():
        keep_ref[slot, start : start + rows, cols] = part

    @pl.when(away % 2 == 1)
    def _():
        send_ref[slot, start : start + rows, cols] = part


def early_kernel(plan, rows, devices, scal, act_ref, step_ref, cum_ref, gcore_ref, gn_ref, c_ref, nh_ref,
                 dgate_ref, *refs):
    count = len(plan)
    pieces = refs[:count]
    gvl_ref, gk_ref, gng_ref, keep_ref, send_ref = refs[count : count + 5]
    w_ref, mc_ref, sem = refs[count + 5 :]
    copies = start_pieces(scal[0], pieces, plan, w_ref, sem, rows)
    length, model = c_ref.shape
    chunks = length // CHUNK
    left = lax.broadcasted_iota(jnp.int32, (CHUNK, LANES), 1) < HDIM

    def mask(i, carry):
        at = pl.ds(pl.multiple_of(i * CHUNK, CHUNK), CHUNK)
        row = lax.broadcasted_iota(jnp.int32, (CHUNK, model), 0) + i * CHUNK
        mc_ref[at, :] = jnp.where(row < scal[1], c_ref[at, :].astype(F32), 0.0).astype(BF16)
        return carry

    lax.fori_loop(0, chunks, mask, 0)
    half = model // 2
    for j in range(2 * INNER // model):
        part = dot(nh_ref[HALO:, :], dgate_ref[:, j * half : (j + 1) * half], 0, 0).astype(BF16)
        start = (j // 2) * rows
        cols = slice((j % 2) * half, (j % 2 + 1) * half)
        for block in range(devices):
            put_block(
                scal[0], block, keep_ref, send_ref, start, cols, part[block * rows : (block + 1) * rows]
            )
    for j in range(INNER // half):
        part = dot(gn_ref[:, j * half : (j + 1) * half], mc_ref[...], 0, 0).astype(BF16)
        each = half // (2 * rows)
        for n in range(each):
            put_block(
                scal[0], j * each + n, keep_ref, send_ref, 2 * rows, slice(0, model),
                part[n * 2 * rows : (n + 1) * 2 * rows],
            )

    def chunk(c, carry):
        at = pl.ds(pl.multiple_of(c * CHUNK, CHUNK), CHUNK)
        in_keys = act_ref[at, INNER : INNER + STATE]
        out_keys = act_ref[at, INNER + STATE : CHANNELS]
        affinity = jnp.where(causal_tile(), dot(out_keys, in_keys, 1, 1), 0.0)
        cum = cum_ref[at, :]
        cum_rows = cum.T
        step_rows = step_ref[at, :].T
        gaff = jnp.zeros((CHUNK, CHUNK), F32)
        for tile in range(INNER // LANES):
            cols = slice(tile * LANES, (tile + 1) * LANES)
            values = act_ref[at, cols]
            grads = gcore_ref[at, cols]
            zero = jnp.zeros_like(grads)
            apart = jnp.concatenate(
                [jnp.where(left, grads, zero), jnp.where(left, zero, grads)], axis=0
            )
            gmix = dot(apart, values, 1, 1)
            mixing = []
            for n in range(2):
                weight = mixing_parts(cum, cum_rows, step_rows, 2 * tile + n)
                gaff = gaff + gmix[n * CHUNK : (n + 1) * CHUNK] * weight
                mixing.append((affinity * weight).astype(BF16))
            back = dot(jnp.concatenate(mixing, axis=1), grads, 0, 0)
            gvl_ref[at, cols] = jnp.where(left, back[0:CHUNK], back[CHUNK:])
        gaff = jnp.where(causal_tile(), gaff, 0.0).astype(BF16)
        gk_ref[at, 0:STATE] = dot(gaff, out_keys, 0, 0)
        gk_ref[at, STATE : 2 * STATE] = dot(gaff, in_keys)
        return carry

    lax.fori_loop(0, chunks, chunk, 0)
    wait_all(copies)
    for j in range(2):
        cols = slice(j * half, (j + 1) * half)
        gng_ref[:, cols] = dot(dgate_ref[...], w_ref[cols, :], 1, 1)


def late_kernel(plan, rows, devices, scal, act_ref, step_ref, sig_ref, cum_ref, gcore_ref, gvl_ref, gk_ref,
                gng_ref, rowq_ref, states_ref, gout_ref, gskip_ref, skip_ref, x_ref, c_ref, nh_ref,
                cext_ref, cw_ref, cb_ref, dl_ref, *refs):
    count = len(plan)
    pieces = refs[:count]
    gtok_ref, last_ref, ghalo_ref, keep_ref, send_ref, small_ref = refs[count : count + 6]
    w_ref, gstate_ref, wide_ref, gact_ref, gpad_ref, gproj_ref, acc_ref, expand_ref, sem = refs[
        count + 6 :
    ]
    copies = start_pieces(scal[0], pieces, plan, w_ref, sem, rows)
    length, model = c_ref.shape
    chunks = length // CHUNK
    tiles = INNER // LANES
    fill_expander(expand_ref)
    gstate_ref[...] = gout_ref[...].astype(F32)
    small_ref[...] = jnp.zeros_like(small_ref)
    small_ref[6:7, 0:INNER] = jnp.sum(gskip_ref[...], axis=0, keepdims=True)
    gpad_ref[0:HALO, :] = jnp.zeros((HALO, CHANNELS), F32)
    gpad_ref[HALO + length :, :] = jnp.zeros((HALO, CHANNELS), F32)
    gproj_ref[0:HALO, CHANNELS:] = jnp.zeros((HALO, LANES), BF16)
    rate = -jnp.exp(dl_ref[0:1, :])
    end = lax.broadcasted_iota(jnp.int32, (CHUNK, LANES), 0) == CHUNK - 1

    def chunk(n, carry):
        gdecay, gbias = carry
        c = chunks - 1 - n
        at = pl.ds(pl.multiple_of(c * CHUNK, CHUNK), CHUNK)
        in_keys = act_ref[at, INNER : INNER + STATE]
        out_keys = act_ref[at, INNER + STATE : CHANNELS]
        cum = cum_ref[at, :]
        step = step_ref[at, :]
        sig = sig_ref[at, :]
        last = cum[CHUNK - 1 : CHUNK]
        small = jnp.concatenate(
            [jnp.exp(cum), jnp.exp(last - cum) * step, jnp.broadcast_to(jnp.exp(last), (8, LANES))], axis=0
        )
        wide_ref[...] = dot(jnp.concatenate(two_parts(small), axis=1), expand_ref[...])
        colq = jnp.zeros((CHUNK, LANES), F32)
        ends = jnp.zeros((8, LANES), F32)
        gin = gk_ref[at, 0:STATE]
        gout = gk_ref[at, STATE : 2 * STATE]
        for tile in range(tiles):
            cols = slice(tile * LANES, (tile + 1) * LANES)
            values = act_ref[at, cols].astype(F32)
            grads = gcore_ref[at, cols].astype(F32)
            gstate = gstate_ref[:, cols]
            gstate_b = gstate.astype(BF16)
            state = states_ref[c, :, cols]
            weight = wide_ref[CHUNK : 2 * CHUNK, cols]
            decay = wide_ref[2 * CHUNK : 2 * CHUNK + 1, cols]
            gvs = weight * dot(in_keys, gstate_b)
            gvalues = gvl_ref[at, cols] + gvs
            colq = colq + head_sums(values * gvalues, tile)
            passed = jnp.sum((values * gvs).reshape(CHUNK // 8, 8, LANES), axis=0) + decay * jnp.sum(
                (gstate * state.astype(F32)).reshape(STATE // 8, 8, LANES), axis=0
            )
            ends = ends + head_sums(passed, tile)
            gin = gin + dot((weight * values).astype(BF16), gstate_b, 1, 1)
            scaled = (wide_ref[0:CHUNK, cols] * grads).astype(BF16)
            gout = gout + dot(scaled, state, 1, 1)
            gstate_ref[:, cols] = decay * gstate + dot(out_keys, scaled, 0, 0)
            gact_ref[:, cols] = gvalues + skip_ref[0:1, cols] * grads
        gact_ref[:, INNER : INNER + STATE] = gin
        gact_ref[:, INNER + STATE : CHANNELS] = gout
        gcum = rowq_ref[at, :] - colq
        gcum = gcum + jnp.where(end, jnp.sum(ends, axis=0, keepdims=True), 0.0)
        glog = running_sum(gcum, reverse=True)
        gdecay = gdecay + jnp.sum((glog * (rate * step)).reshape(CHUNK // 8, 8, LANES), axis=0)
        ratio = jnp.where(step > 0.0, sig / jnp.where(step > 0.0, step, 1.0), 0.0)
        graw = colq * ratio + rate * glog * sig
        gbias = gbias + jnp.sum(graw.reshape(CHUNK // 8, 8, LANES), axis=0)
        first = pl.multiple_of(c * CHUNK, CHUNK)
        gproj_ref[pl.ds(first + HALO, CHUNK), CHANNELS:] = graw.astype(BF16)
        for tile in range(CHANNELS // LANES):
            cols = slice(tile * LANES, (tile + 1) * LANES)
            part = cext_ref[pl.ds(first, CHUNK + HALO), cols].astype(F32)
            moved = [pltpu.roll(part, KCONV - 1 - k, 0)[HALO:] for k in range(KCONV - 1)] + [part[HALO:]]
            out = cb_ref[0:1, cols]
            for k in range(KCONV):
                out = out + cw_ref[k : k + 1, cols] * moved[k]
            sc = jax.nn.sigmoid(out)
            gconv = gact_ref[:, cols] * (sc * (1.0 + out * (1.0 - sc)))
            gpad_ref[pl.ds(first + HALO, CHUNK), cols] = gconv
            for k in range(KCONV):
                small_ref[k : k + 1, cols] = small_ref[k : k + 1, cols] + jnp.sum(
                    gconv * moved[k], axis=0, keepdims=True
                )
            small_ref[4:5, cols] = small_ref[4:5, cols] + jnp.sum(gconv, axis=0, keepdims=True)
        return gdecay, gbias

    zero = jnp.zeros((8, LANES), F32)
    gdecay, gbias = lax.fori_loop(0, chunks, chunk, (zero, zero))
    small_ref[5:6, 0:LANES] = jnp.sum(gdecay, axis=0, keepdims=True)
    small_ref[5:6, LANES : 2 * LANES] = jnp.sum(gbias, axis=0, keepdims=True)

    def conv_back(i, carry):
        first = pl.multiple_of(i * HALO, HALO)
        for tile in range(CHANNELS // LANES):
            cols = slice(tile * LANES, (tile + 1) * LANES)
            part = gpad_ref[pl.ds(first, 2 * HALO), cols]
            total = cw_ref[KCONV - 1 : KCONV, cols] * part[:HALO]
            for k in range(KCONV - 1):
                ahead = pltpu.roll(part, 2 * HALO - (KCONV - 1 - k), 0)[:HALO]
                total = total + cw_ref[k : k + 1, cols] * ahead
            gproj_ref[pl.ds(first, HALO), cols] = total.astype(BF16)
        return carry

    lax.fori_loop(0, (length + HALO) // HALO, conv_back, 0)
    for j in range(WIDTH // 384):
        cols = slice(j * 384, (j + 1) * 384)
        part = dot(nh_ref[...], gproj_ref[:, cols], 0, 0).astype(BF16)
        for block in range(devices):
            put_block(
                scal[0], block, keep_ref, send_ref, 0, cols, part[block * rows : (block + 1) * rows]
            )
    wait_all(copies)
    for j in range(2):
        cols = slice(j * model // 2, (j + 1) * model // 2)
        acc_ref[:, cols] = dot(gproj_ref[...], w_ref[cols, :], 1, 1)
    acc_ref[HALO:, :] = acc_ref[HALO:, :] + gng_ref[...]
    gain = gain_row(w_ref)

    def norm_back(i, carry):
        at = pl.ds(pl.multiple_of(i * HALO, HALO), HALO)
        u = x_ref[at, :].astype(F32)
        scale = lax.rsqrt(jnp.mean(u * u, axis=1, keepdims=True) + EPSILON)
        nh = u * scale
        g = acc_ref[at, :] * gain
        acc_ref[at, :] = scale * (g - nh * jnp.mean(g * nh, axis=1, keepdims=True))
        return carry

    lax.fori_loop(0, (length + HALO) // HALO, norm_back, 0)
    ghalo_ref[...] = acc_ref[0:HALO, :]
    last_ref[...] = acc_ref[length:, :] + c_ref[length - HALO :, :].astype(F32)

    def finish(i, carry):
        at = pl.ds(pl.multiple_of(i * HALO, HALO), HALO)
        grads = acc_ref[pl.ds(pl.multiple_of((i + 1) * HALO, HALO), HALO), :]
        gtok_ref[at, :] = (grads + c_ref[at, :].astype(F32)).astype(BF16)
        return carry

    lax.fori_loop(0, length // HALO, finish, 0)


def call(body, scal, whole, pieces, outs, scratch):
    smem = pl.BlockSpec(memory_space=pltpu.SMEM)
    vmem = pl.BlockSpec(memory_space=pltpu.VMEM)
    return pl.pallas_call(
        body,
        out_shape=[jax.ShapeDtypeStruct(shape, kind) for shape, kind in outs],
        in_specs=[smem] + [vmem] * len(whole) + [pl.BlockSpec(memory_space=pl.ANY)] * len(pieces),
        out_specs=[vmem] * len(outs),
        scratch_shapes=scratch,
        compiler_params=pltpu.CompilerParams(vmem_limit_bytes=VMEM_LIMIT),
    )(scal, *whole, *pieces)


def lane_row(vector):
    return jnp.pad(vector, (0, LANES - vector.shape[0]))[None]


def per_device(tokens, lengths, dealing, cotangent, in_weight, out_weight, norm_gain, gate_gain, conv_weight,
               conv_bias, decay_log, step_bias, skip_gain):
    dp, seq = lax.axis_index("dp"), lax.axis_index("seq")
    devices, size = lax.axis_size("dp"), lax.axis_size("seq")
    group = size // 2
    lin = seq * 2 + dp % 2
    holder = lin // group
    place = {"dp": dp, "seq": seq, "micro": holder // 2, "column": holder % 2, "turn": lin % group}
    block_len, model = tokens.shape[2:]
    length = 2 * block_len
    shard_rows = in_weight.shape[0]
    rows = shard_rows * size
    bits = list(range(1, devices.bit_length() - 1))
    tok = tokens[:, 0]
    cot = cotangent[:, 0]

    gains = jnp.concatenate(
        [norm_gain[:, None], jnp.swapaxes(gate_gain.reshape(2, shard_rows), 0, 1)], axis=1
    )
    conv_shard = jnp.concatenate([in_weight[:, INNER:], gains], axis=1)
    conv_shard = jnp.pad(conv_shard, ((0, 0), (0, WIDTH - conv_shard.shape[1])))
    rest_shard = jnp.concatenate([in_weight[:, :model], in_weight[:, model:INNER], out_weight], axis=0)
    conv_z = seq_gather(conv_shard, place)
    conv_block = conv_z.reshape(rows, WIDTH)
    gate_gains = jnp.swapaxes(conv_z[:, :, CHANNELS + HEADS + 1 : CHANNELS + HEADS + 3], 1, 2)
    gate_gains = jnp.pad(gate_gains.reshape(2 * rows, 1), ((0, 0), (0, LANES - 1)))
    conv_a = spread(conv_block[:, :SPLIT], bits)
    conv_b = spread(conv_block[:, SPLIT:], bits[::-1])
    rest_block = seq_gather(rest_shard, place)
    gate_block = jnp.swapaxes(rest_block[:, : 2 * shard_rows].reshape(size, 2, shard_rows, model), 0, 1)
    gate_p = spread(gate_block.reshape(2 * rows, model), bits)
    out_block = jnp.concatenate([rest_block[:, 2 * shard_rows :].reshape(2 * rows, model), gate_gains], axis=1)
    out_p = spread(out_block, bits[::-1])
    conv_pieces = [part for _, part in conv_a + conv_b]
    conv_plan = [(masks, [(0, 1, 0, SPLIT)]) for masks, _ in conv_a] + [
        (masks, [(0, 1, SPLIT, WIDTH - SPLIT)]) for masks, _ in conv_b
    ]
    gate_pieces = [part for _, part in gate_p]
    gate_plan = [(masks, [(0, 1, 0, model), (rows, 1, model, model)]) for masks, _ in gate_p]
    out_pieces = [part for _, part in out_p]
    out_plan = [(masks, [(0, 2, 0, model + LANES)]) for masks, _ in out_p]

    if devices == 8:
        table = dp_table(jnp.concatenate([dealing[:, 0], lengths[:, 0]]))
        routes = make_routes(place, table)
        own_length = routes[4, 0]
        cot_given = deal(cot, routes[0:2], place)
    else:
        every = lax.all_gather(jnp.concatenate([dealing, lengths], axis=0)[:, 0], "dp", axis=0)
        goals = every[:, :2]
        source_of_out = jnp.argmax(goals == dp, axis=0)
        cot_given = deal_gathered(cot, dealing[:, 0])
        mate = lax.dynamic_index_in_dim(every, dp - dp % 2 + place["column"], 0, keepdims=False)
        own_length = jnp.where(place["micro"] == 0, mate[2], mate[3])
    n_valid = jnp.clip(own_length - place["turn"] * length, 0, length)
    scal = jnp.stack([dp, n_valid])

    first, second = to_stretch(tok, place)
    halo = lax.ppermute(second[block_len - HALO :], BOTH, neighbour_pairs(1))
    x_ext = jnp.concatenate([halo, first, second])
    c_own = jnp.concatenate(to_stretch(cot_given, place))

    taps = jnp.pad(conv_weight, ((0, 8 - KCONV), (0, 0)))
    conv_bias_row = conv_bias[None]
    decay_row, bias_row = lane_row(decay_log), lane_row(step_bias)
    skip_row = jnp.repeat(skip_gain, HDIM)[None]

    def sems(plan):
        return pltpu.SemaphoreType.DMA((piece_count(plan),))

    wide = (length, INNER)
    nh, cext, act, step, sig, cum, update, total = call(
        functools.partial(project_kernel, conv_plan, rows),
        scal,
        [x_ext, taps, conv_bias_row, decay_row, bias_row],
        conv_pieces,
        [((length + HALO, model), BF16), ((length + HALO, CHANNELS), BF16), ((length, CHANNELS), BF16)]
        + [((length, LANES), F32)] * 3 + [((STATE, INNER), BF16), ((8, LANES), F32)],
        [pltpu.VMEM((model, WIDTH), BF16), pltpu.VMEM((length + HALO, WIDTH), F32),
         pltpu.VMEM((2 * LANES, INNER), BF16), sems(conv_plan)],
    )
    passing = jnp.repeat(jnp.exp(total[0, :HEADS]), HDIM)[None] if group > 2 else None

    def relay(own, pairs):
        carried = None
        for _ in range(group - 1):
            given = own if carried is None else (passing * carried.astype(F32) + own.astype(F32)).astype(BF16)
            carried = lax.ppermute(given, BOTH, pairs)
        return jnp.zeros_like(own) if carried is None else carried

    state_in = relay(update, neighbour_pairs(1))
    local, gate = call(
        functools.partial(local_kernel, gate_plan, rows),
        scal,
        [nh, act, step, cum],
        gate_pieces,
        [(wide, F32), (wide, F32)],
        [pltpu.VMEM((model, INNER), BF16), sems(gate_plan)],
    )
    out, gn, dgate, gcore, rowq, lsg, states, gskip = call(
        functools.partial(middle_kernel, out_plan, rows),
        scal,
        [local, act, step, cum, gate, state_in, x_ext, c_own, skip_row],
        out_pieces,
        [((length, model), BF16), (wide, BF16), (wide, BF16), (wide, BF16), ((length, LANES), F32),
         ((STATE, INNER), BF16), ((length // CHUNK, STATE, INNER), BF16), ((8, INNER), F32)],
        [pltpu.VMEM((INNER, model + LANES), BF16), pltpu.VMEM((8, INNER), F32),
         pltpu.VMEM((length, model), BF16), pltpu.VMEM(wide, F32), pltpu.VMEM((STATE, INNER), F32), pltpu.VMEM((3 * CHUNK + 8, INNER), F32),
         pltpu.VMEM((CHUNK, INNER), F32), pltpu.VMEM((CHUNK, INNER), F32), pltpu.VMEM((STATE, INNER), F32),
         pltpu.VMEM((2 * LANES, INNER), BF16), sems(out_plan)],
    )
    grad_out_state = relay(lsg, neighbour_pairs(-1))
    half_dp = devices // 2
    gvl, gk, gng, keep1, send1 = call(
        functools.partial(early_kernel, gate_plan, rows, devices),
        scal,
        [act, step, cum, gcore, gn, c_own, nh, dgate],
        gate_pieces,
        [(wide, F32), ((length, 2 * STATE), F32), ((length, model), F32)]
        + [((half_dp, 4 * rows, model), BF16)] * 2,
        [pltpu.VMEM((model, INNER), BF16), pltpu.VMEM((length, model), BF16), sems(gate_plan)],
    )
    gtok, last, ghalo, keep2, send2, small = call(
        functools.partial(late_kernel, conv_plan, rows, devices),
        scal,
        [act, step, sig, cum, gcore, gvl, gk, gng, rowq, states, grad_out_state, gskip, skip_row, x_ext,
         c_own, nh, cext, taps, conv_bias_row, decay_row],
        conv_pieces,
        [((length, model), BF16), ((HALO, model), F32), ((HALO, model), F32)]
        + [((half_dp, rows, WIDTH), BF16)] * 2 + [((8, WIDTH), F32)],
        [pltpu.VMEM((model, WIDTH), BF16), pltpu.VMEM((STATE, INNER), F32),
         pltpu.VMEM((2 * CHUNK + 8, INNER), F32), pltpu.VMEM((CHUNK, CHANNELS), F32),
         pltpu.VMEM((length + 2 * HALO, CHANNELS), F32), pltpu.VMEM((length + HALO, WIDTH), BF16),
         pltpu.VMEM((length + HALO, model), F32), pltpu.VMEM((2 * LANES, INNER), BF16), sems(conv_plan)],
    )

    out_blocks = jnp.stack(from_stretch(out[:block_len], out[block_len:], place))
    if devices == 8:
        outputs = deal(out_blocks, routes[2:4], place)
    else:
        outputs = deal_gathered(out_blocks, source_of_out)

    early = keep1.astype(F32) + flip_dp(send1, 1).astype(F32)
    early_gate = fold(early[:, : 2 * rows], bits[::-1]).reshape(2, size, shard_rows, model)
    early_out = fold(early[:, 2 * rows :], bits).reshape(size, 2 * shard_rows, model)
    early_all = jnp.concatenate([early_gate[0], early_gate[1], early_out], axis=1)
    early_sum = seq_scatter(early_all, place)
    late = keep2.astype(F32) + flip_dp(send2, 1).astype(F32)
    late_a = fold(late[:, :, :SPLIT], bits[::-1])
    late_b = fold(late[:, :, SPLIT:], bits)
    late_sum = seq_scatter(jnp.concatenate([late_a, late_b], axis=1).reshape(size, shard_rows, WIDTH), place)
    raw_in = jnp.concatenate(
        [early_sum[:shard_rows], early_sum[shard_rows : 2 * shard_rows],
         late_sum[:, : in_weight.shape[1] - INNER]], axis=1
    )
    raw_out = early_sum[2 * shard_rows :]
    grad_norm_gain = jnp.sum(raw_in * in_weight.astype(F32), axis=1) / norm_gain.astype(F32)
    grad_gate_gain = jnp.sum(raw_out * out_weight.astype(F32), axis=1) / gate_gain.astype(F32)

    from_next = lax.ppermute(ghalo, BOTH, neighbour_pairs(-1))
    tail = (last + from_next).astype(BF16)
    gtok_second = jnp.concatenate([gtok[block_len : length - HALO], tail])
    grad_tokens = jnp.stack(from_stretch(gtok[:block_len], gtok_second, place))

    sums = sum_everywhere(small)
    grad_skip = jnp.sum(sums[6, :INNER].reshape(HEADS, HDIM), axis=1)
    return (
        outputs[:, None],
        grad_tokens[:, None],
        raw_in,
        raw_out,
        grad_norm_gain,
        grad_gate_gain,
        sums[0:KCONV, :CHANNELS],
        sums[4, :CHANNELS],
        sums[5, :HEADS],
        sums[5, LANES : LANES + HEADS],
        grad_skip,
    )


def solution(mesh):
    in_specs = (
        P(None, "dp", "seq", None),
        P(None, "dp"),
        P(None, "dp"),
        P(None, "dp", "seq", None),
        P(BOTH, None),
        P(BOTH, None),
        P(BOTH),
        P(BOTH),
        P(),
        P(),
        P(),
        P(),
        P(),
    )
    out_specs = (
        P(None, "dp", "seq", None),
        P(None, "dp", "seq", None),
        P(BOTH, None),
        P(BOTH, None),
        P(BOTH),
        P(BOTH),
        P(),
        P(),
        P(),
        P(),
        P(),
    )
    return jax.shard_map(per_device, mesh=mesh, in_specs=in_specs, out_specs=out_specs, check_vma=False)
```

```python
import functools

import jax
import jax.numpy as jnp
from jax import lax
from jax.experimental import pallas as pl
from jax.experimental.pallas import tpu as pltpu
from jax.sharding import PartitionSpec as P

INNER = 1536
HEADS = 24
HDIM = 64
STATE = 128
KCONV = 4
CHANNELS = INNER + 2 * STATE
LANES = 128
CHUNK = 128
HALO = 16
EPSILON = 1e-05
WIDTH = CHANNELS + LANES
SPLIT = 1024
F32 = jnp.float32
BF16 = jnp.bfloat16
BOTH = ("dp", "seq")
VMEM_LIMIT = 60 * 1024 * 1024


def flip_dp(value, mask):
    pairs = [(i, i ^ mask) for i in range(lax.axis_size("dp"))]
    return lax.ppermute(value, "dp", pairs)


def shift_seq(value, step):
    size = lax.axis_size("seq")
    return lax.ppermute(value, "seq", [(i, (i + step) % size) for i in range(size)])


def column_place(dp_even, lin):
    return (dp_even + lin % 2) * lax.axis_size("seq") + lin // 2


def unit_pairs(parity):
    size = lax.axis_size("seq")
    pairs = []
    for dp in range(lax.axis_size("dp")):
        core = dp % 2
        for block in range(size):
            micro = (block % 2) ^ parity
            lin = (2 * micro + core) * (size // 2) + block // 2
            pairs.append((dp * size + block, column_place(dp - core, lin)))
    return pairs


def half_pairs(parity, other):
    size = lax.axis_size("seq")
    pairs = []
    for dp in range(lax.axis_size("dp")):
        core = dp % 2
        for block in range(size):
            micro = (block % 2) ^ parity
            lin = (2 * micro + (core ^ other)) * (size // 2) + block // 2
            pairs.append((dp * size + block, column_place(dp - core, lin)))
    return pairs


def neighbour_pairs(step):
    size = lax.axis_size("seq")
    group = size // 2
    pairs = []
    for dp_even in range(0, lax.axis_size("dp"), 2):
        for lin in range(2 * size):
            if 0 <= lin % group + step < group:
                pairs.append((column_place(dp_even, lin), column_place(dp_even, lin + step)))
    return pairs


def reversed_pairs(pairs):
    return [(target, source) for source, target in pairs]


def to_stretch(blocks, place):
    odd = place["seq"] % 2 == 1
    first = lax.ppermute(jnp.where(odd, blocks[1], blocks[0]), BOTH, unit_pairs(0))
    second = lax.ppermute(jnp.where(odd, blocks[0], blocks[1]), BOTH, unit_pairs(1))
    return first, second


def swapped(swap, pair):
    return jnp.where(swap, pair[1], pair[0]), jnp.where(swap, pair[0], pair[1])


def from_stretch(first, second, place):
    late = place["micro"] == 1
    one = lax.ppermute(jnp.where(late, second, first), BOTH, reversed_pairs(unit_pairs(0)))
    two = lax.ppermute(jnp.where(late, first, second), BOTH, reversed_pairs(unit_pairs(1)))
    return one, two


class Chain:
    def __init__(self, stages):
        self.stages = stages
        self.value = None
        self.pending = next(stages)

    def feed(self, arrived):
        try:
            self.pending = self.stages.send(arrived)
        except StopIteration as stop:
            self.pending = None
            self.value = stop.value


def advance(held, *chains):
    moving = [chain for chain in chains if chain.pending is not None]
    held, arrived = lax.optimization_barrier((held, [chain.pending for chain in moving]))
    for chain, got in zip(moving, arrived):
        chain.feed(got)
    return held


def seq_shifts(shard):
    return [shift_seq(shard, j) for j in range(1, lax.axis_size("seq"))]


def seq_order(shard, arrived, place):
    size = lax.axis_size("seq")
    got = [shard] + list(arrived)
    rows = []
    for i in range(size):
        row = got[0]
        for j in range(1, size):
            row = jnp.where((place["seq"] - i) % size == j, got[j], row)
        rows.append(row)
    return jnp.stack(rows)


def gather_stages(shard, place, streams_of):
    arrived = yield seq_shifts(shard)
    streams = streams_of(seq_order(shard, arrived, place))
    masks = [(0,) for _ in streams]
    held = [block[None] for block, _ in streams]
    last = None
    turned = None
    steps = len(streams[0][1])
    for step in range(steps):
        moved = []
        for n, (_, bits) in enumerate(streams):
            if last is not None:
                masks[n] = masks[n] + last[n][0]
                held[n] = jnp.concatenate([held[n], last[n][1]])
            moved.append(flip_dp(held[n], 1 << bits[step]))
        if step < steps - 1:
            moved = yield moved
        else:
            both = yield (moved, [flip_dp(h, 1) for h in held])
            moved, turned = both
        last = [
            (tuple(m ^ (1 << bits[step]) for m in masks[n]), moved[n]) for n, (_, bits) in enumerate(streams)
        ]
    ends = yield [flip_dp(array, 1) for _, array in last]
    out = []
    for n in range(len(streams)):
        pieces = [(masks[n], held[n]), last[n], (tuple(m ^ 1 for m in masks[n]), turned[n])]
        pieces.append((tuple(m ^ 1 for m in last[n][0]), ends[n]))
        out.append(pieces)
    return out


def reduce_stages(keep, send, place, streams_of, join):
    got = yield [flip_dp(send, 1)]
    streams = streams_of(keep.astype(F32) + got[0].astype(F32))
    parts, axes = [], []
    for part, bits in streams:
        parts.append(part.reshape((2,) * len(bits) + part.shape[1:]))
        axes.append(sorted(bits, reverse=True))
    for step in range(len(streams[0][1])):
        keeps, gives = [], []
        for n, (_, bits) in enumerate(streams):
            bit = bits[step]
            axis = axes[n].index(bit)
            axes[n].pop(axis)
            keeps.append(lax.index_in_dim(parts[n], 0, axis, keepdims=False))
            give = lax.index_in_dim(parts[n], 1, axis, keepdims=False).astype(BF16)
            gives.append(flip_dp(give, 1 << bit))
        gives = yield gives
        parts = [k + g.astype(F32) for k, g in zip(keeps, gives)]
    joined = join(parts)
    size = lax.axis_size("seq")
    total = lax.dynamic_index_in_dim(joined, place["seq"], 0, keepdims=False)
    moved = []
    for j in range(1, size):
        give = lax.dynamic_index_in_dim(joined, (place["seq"] + j) % size, 0, keepdims=False)
        moved.append(shift_seq(give.astype(BF16), j))
    moved = yield moved
    for got in moved:
        total = total + got.astype(F32)
    return total


def sum_stages(value):
    for bit in range(lax.axis_size("dp").bit_length() - 1):
        got = yield [flip_dp(value, 1 << bit)]
        value = value + got[0]
    size = lax.axis_size("seq")
    apart = 1
    while apart < size:
        got = yield [lax.ppermute(value, "seq", [(i, i ^ apart) for i in range(size)])]
        value = value + got[0]
        apart *= 2
    return value


def table_stages(row):
    table = row[None]
    for bit in range(lax.axis_size("dp").bit_length() - 1):
        got = yield [flip_dp(table, 1 << bit)]
        table = jnp.concatenate([table, got[0]])
    return table


def route_kernel(place_ref, table_ref, out_ref):
    dp = place_ref[0]
    size = table_ref.shape[0]
    for way in range(2):
        for micro in range(2):
            first_bit, second_bit = ((2, 4), (4, 2))[micro]
            goal = []
            for r in range(size):
                if way == 1:
                    goal.append(table_ref[r, micro])
                else:
                    found = jnp.int32(0)
                    for other in range(size):
                        hit = table_ref[other, micro] == jnp.bitwise_xor(dp, r)
                        found = jnp.where(hit, jnp.bitwise_xor(dp, other), found)
                    goal.append(found)
            held = [0, 1, first_bit, first_bit | 1]

            def chosen(base):
                low = jnp.int32(0)
                high = jnp.int32(0)
                for n in range(3, -1, -1):
                    away = jnp.bitwise_xor(goal[base ^ held[n]], jnp.bitwise_xor(dp, base))
                    cross = (jnp.bitwise_and(away, second_bit) != 0) & (
                        jnp.bitwise_and(away, first_bit) == 0
                    )
                    low = jnp.where(cross, n, low)
                for n in range(4):
                    away = jnp.bitwise_xor(goal[base ^ held[n]], jnp.bitwise_xor(dp, base))
                    cross = (jnp.bitwise_and(away, second_bit) != 0) & (
                        jnp.bitwise_and(away, first_bit) == 0
                    )
                    high = jnp.where(cross, n, high)
                return low, high

            low, high = chosen(0)
            other_low, _ = chosen(second_bit)
            row = way * 2 + micro
            out_ref[row, 0] = low
            out_ref[row, 1] = high
            for side in range(2):
                pick = jnp.int32(0)
                target = jnp.bitwise_xor(dp, side)
                for n in range(4):
                    pick = jnp.where(goal[held[n]] == target, n, pick)
                    far = jnp.where(other_low == n, 4, 5)
                    pick = jnp.where(goal[held[n] ^ second_bit] == target, far, pick)
                out_ref[row, 2 + side] = pick
    core = jnp.bitwise_and(dp, 1)
    column = jnp.bitwise_xor(core, place_ref[2])
    micro = place_ref[1]
    own = jnp.where(micro == 0, table_ref[0, 2], table_ref[0, 3])
    other = jnp.where(micro == 0, table_ref[1, 2], table_ref[1, 3])
    out_ref[4, 0] = jnp.where(column == 0, own, other)
    for n in range(1, 4):
        out_ref[4, n] = jnp.int32(0)


class Routes:
    def __init__(self, place, table):
        self.place, self.table, self.made = place, table, None

    @property
    def value(self):
        if self.made is None:
            self.made = make_routes(self.place, self.table.value)
        return self.made


def make_routes(place, table):
    return pl.pallas_call(
        route_kernel,
        out_shape=jax.ShapeDtypeStruct((5, 4), jnp.int32),
        in_specs=[pl.BlockSpec(memory_space=pltpu.SMEM)] * 2,
        out_specs=pl.BlockSpec(memory_space=pltpu.SMEM),
    )(jnp.stack([place["dp"], place["micro"], place["column"]]), table)


def pick_kernel(first, last, route_ref, *refs):
    pairs = len(refs) - 4
    mine_ref, got_ref = refs[0], refs[1]
    for micro in range(2):
        held = [mine_ref.at[micro], got_ref.at[micro]]
        for n in range(micro, pairs, 2):
            held += [refs[2 + n].at[0], refs[2 + n].at[1]]
        for k in range(2):
            index = route_ref[first + micro, last + k]
            out = refs[2 + pairs + micro].at[k] if last == 0 else refs[2 + pairs + k].at[micro]
            for n in range(len(held)):

                @pl.when(index == n)
                def _():
                    out[...] = held[n][...]


def pick(routes, first, last, mine, got, *pairs):
    vmem = pl.BlockSpec(memory_space=pltpu.VMEM)
    return pl.pallas_call(
        functools.partial(pick_kernel, first, last),
        out_shape=[jax.ShapeDtypeStruct(mine.shape, BF16)] * 2,
        in_specs=[pl.BlockSpec(memory_space=pltpu.SMEM)] + [vmem] * (2 + len(pairs)),
        out_specs=[vmem] * 2,
    )(routes, mine, got, *pairs)


def first_flips(mine, got):
    return [flip_dp(jnp.stack([mine[m], got[m]]), (2, 4)[m]) for m in range(2)]


def second_flips(sent):
    return [flip_dp(sent[m], (4, 2)[m]) for m in range(2)]


def cotangent_stages(items, routes, place):
    low_core = place["dp"] % 2 == 0
    half = items.shape[1] // 2
    mine, give = swapped(jnp.logical_not(low_core), (items[:, :half], items[:, half:]))
    got = (yield [flip_dp(give, 1)])[0]
    came = first_flips(mine, got)
    yield []
    came = yield came
    sent = pick(routes.value, 0, 0, mine, got, *came)
    far = second_flips(sent)
    yield []
    far = yield far
    parts = pick(routes.value, 0, 2, mine, got, *came, *far)
    odd = place["seq"] % 2 == 1
    moved = []
    for k in range(2):
        for parity, half_block in enumerate(swapped(odd, parts[k])):
            moved.append(lax.ppermute(half_block, BOTH, half_pairs(parity, k)))
    yield []
    moved = yield moved
    first = swapped(place["column"] == 1, (pick_late(moved[0:2], place, 0), pick_late(moved[2:4], place, 0)))
    second = swapped(place["column"] == 1, (pick_late(moved[0:2], place, 1), pick_late(moved[2:4], place, 1)))
    return jnp.concatenate(first + second)


def pick_late(pair, place, which):
    return swapped(place["micro"] == 1, pair)[which]


def output_stages(out, routes, place):
    half = out.shape[0] // 4
    moved = []
    for k in range(2):
        halves = []
        for block in range(2):
            top = out[2 * block * half : (2 * block + 1) * half]
            bottom = out[(2 * block + 1) * half : (2 * block + 2) * half]
            halves.append(swapped(place["column"] == 1, (top, bottom))[k])
        for parity in range(2):
            give = pick_late(halves, place, parity)
            moved.append(lax.ppermute(give, BOTH, reversed_pairs(half_pairs(parity, k))))
    yield []
    moved = yield moved
    odd = place["seq"] % 2 == 1
    mine = jnp.stack(swapped(odd, moved[0:2]))
    got = jnp.stack(swapped(odd, moved[2:4]))
    came = yield first_flips(mine, got)
    sent = pick(routes.value, 2, 0, mine, got, *came)
    far = yield second_flips(sent)
    own, partner = pick(routes.value, 2, 2, mine, got, *came, *far)
    back = (yield [flip_dp(partner, 1)])[0]
    return jnp.concatenate(swapped(place["dp"] % 2 == 1, (own, back)), axis=1)


def deal_gathered(items, source):
    every = lax.all_gather(items, "dp", axis=0)
    picked = [
        lax.dynamic_index_in_dim(every[:, m], source[m], 0, keepdims=False) for m in range(2)
    ]
    return jnp.stack(picked)


def dot(a, b, ca=1, cb=0):
    return lax.dot_general(a, b, (((ca,), (cb,)), ((), ())), preferred_element_type=F32)


def two_parts(x):
    high = x.astype(BF16)
    return high, (x - high.astype(F32)).astype(BF16)


def running_sum(x, reverse=False):
    rows = lax.broadcasted_iota(jnp.int32, (CHUNK, CHUNK), 0)
    cols = lax.broadcasted_iota(jnp.int32, (CHUNK, CHUNK), 1)
    reach = (rows <= cols) if reverse else (rows >= cols)
    reach = jnp.where(reach, 1.0, 0.0).astype(BF16)
    high, rest = two_parts(x)
    middle, low = two_parts(x - high.astype(F32))
    del rest
    return dot(reach, high) + dot(reach, middle) + dot(reach, low)


def fill_expander(expand_ref):
    head = lax.broadcasted_iota(jnp.int32, (LANES, INNER), 0)
    col = lax.broadcasted_iota(jnp.int32, (LANES, INNER), 1)
    one = jnp.where(col // HDIM == head, 1.0, 0.0).astype(BF16)
    expand_ref[0:LANES, :] = one
    expand_ref[LANES : 2 * LANES, :] = one


def head_sums(prod, tile):
    lane = lax.broadcasted_iota(jnp.int32, (LANES, LANES), 0)
    head = lax.broadcasted_iota(jnp.int32, (LANES, LANES), 1)
    one = jnp.where(2 * tile + lane // HDIM == head, 1.0, 0.0).astype(BF16)
    high, low = two_parts(prod)
    return dot(jnp.concatenate([high, low], axis=1), jnp.concatenate([one, one], axis=0))


def start_pieces(dp, pieces, plan, target, sem, rows):
    copies = []
    for piece, (masks, spots) in zip(pieces, plan):
        for n, mask in enumerate(masks):
            for source, scale, col, width in spots:
                first = pl.multiple_of(jnp.bitwise_xor(dp, mask) * (rows * scale), 8)
                copy = pltpu.make_async_copy(
                    piece.at[n, pl.ds(source, rows * scale), :],
                    target.at[pl.ds(first, rows * scale), pl.ds(col, width)],
                    sem.at[len(copies)],
                )
                copy.start()
                copies.append(copy)
    return copies


def wait_all(copies):
    for copy in copies:
        copy.wait()


def piece_count(plan):
    return sum(len(masks) * len(spots) for masks, spots in plan)


def gain_row(w_ref):
    return w_ref[:, CHANNELS:].astype(F32).T[HEADS : HEADS + 1]


def project_kernel(plan, rows, scal, x_ref, cw_ref, cb_ref, dl_ref, sb_ref, *refs):
    count = len(plan)
    pieces = refs[:count]
    nh_ref, cext_ref, act_ref, step_ref, sig_ref, cum_ref = refs[count : count + 6]
    w_ref, proj_ref, sem = refs[count + 6 :]
    copies = start_pieces(scal[0], pieces, plan, w_ref, sem, rows)
    total = x_ref.shape[0]
    length = total - HALO
    chunks = length // CHUNK

    def norm(i, carry):
        at = pl.ds(pl.multiple_of(i * HALO, HALO), HALO)
        u = x_ref[at, :].astype(F32)
        scale = lax.rsqrt(jnp.mean(u * u, axis=1, keepdims=True) + EPSILON)
        nh_ref[at, :] = (u * scale * gain).astype(BF16)
        return carry

    wait_all(copies)
    gain = gain_row(w_ref)
    lax.fori_loop(0, total // HALO, norm, 0)

    def project(j, carry):
        at = pl.ds(pl.multiple_of(j * 384, 384), 384)
        proj_ref[:, at] = dot(nh_ref[...], w_ref[:, at])
        return carry

    lax.fori_loop(0, WIDTH // 384, project, 0)

    def conv(idx, carry):
        i, j = idx // (CHANNELS // LANES), idx % (CHANNELS // LANES)
        cols = pl.ds(pl.multiple_of(j * LANES, LANES), LANES)
        first = pl.multiple_of(i * CHUNK, CHUNK)
        part = proj_ref[pl.ds(first, CHUNK + HALO), cols]
        weights = cw_ref[:, cols]
        out = cb_ref[0:1, cols] + weights[KCONV - 1 : KCONV] * part[HALO:]
        for k in range(KCONV - 1):
            out = out + weights[k : k + 1] * pltpu.roll(part, KCONV - 1 - k, 0)[HALO:]
        act_ref[pl.ds(first, CHUNK), cols] = (out * jax.nn.sigmoid(out)).astype(BF16)
        cext_ref[pl.ds(first + HALO, CHUNK), cols] = part[HALO:].astype(BF16)
        return carry

    lax.fori_loop(0, chunks * (CHANNELS // LANES), conv, 0)
    cext_ref[0:HALO, :] = proj_ref[0:HALO, 0:CHANNELS].astype(BF16)
    lane = lax.broadcasted_iota(jnp.int32, (CHUNK, LANES), 1)
    row = lax.broadcasted_iota(jnp.int32, (CHUNK, LANES), 0)
    rate = -jnp.exp(dl_ref[0:1, :])
    for i in range(chunks):
        at = pl.ds(i * CHUNK, CHUNK)
        pre = proj_ref[pl.ds(HALO + i * CHUNK, CHUNK), pl.ds(CHANNELS, LANES)] + sb_ref[0:1, :]
        live = (row + i * CHUNK < scal[1]) & (lane < HEADS)
        soft = jnp.maximum(pre, 0.0) + jnp.log1p(jnp.exp(-jnp.abs(pre)))
        step = jnp.where(live, soft, 0.0)
        step_ref[at, :] = step
        sig_ref[at, :] = jnp.where(live, jax.nn.sigmoid(pre), 0.0)
        cum_ref[at, :] = running_sum(rate * step)


def mixing_parts(cum, cum_rows, step_rows, head):
    gap = jnp.minimum(cum[:, head : head + 1] - cum_rows[head : head + 1, :], 0.0)
    return jnp.exp(gap) * step_rows[head : head + 1, :]


def causal_tile():
    rows = lax.broadcasted_iota(jnp.int32, (CHUNK, CHUNK), 0)
    cols = lax.broadcasted_iota(jnp.int32, (CHUNK, CHUNK), 1)
    return rows >= cols


def local_kernel(act_ref, step_ref, cum_ref, local_ref, upd_ref, tot_ref, sum_ref, expand_ref):
    chunks = act_ref.shape[0] // CHUNK
    left = lax.broadcasted_iota(jnp.int32, (CHUNK, LANES), 1) < HDIM
    fill_expander(expand_ref)
    after = jnp.zeros((1, LANES), F32)
    for i in range(chunks - 1, -1, -1):
        at = pl.ds(i * CHUNK, CHUNK)
        cum = cum_ref[at, :]
        last = cum[CHUNK - 1 : CHUNK]
        weight = jnp.exp(last + after - cum) * step_ref[at, :]
        wide = dot(jnp.concatenate(two_parts(weight), axis=1), expand_ref[...])
        values = act_ref[at, 0:INNER].astype(F32)
        keys = act_ref[at, INNER : INNER + STATE]
        update = dot(keys, (wide * values).astype(BF16), 0, 0)
        sum_ref[...] = update if i == chunks - 1 else sum_ref[...] + update
        after = after + last
    upd_ref[...] = sum_ref[...].astype(BF16)
    tot_ref[...] = jnp.broadcast_to(after, tot_ref.shape)

    def chunk(c, carry):
        at = pl.ds(pl.multiple_of(c * CHUNK, CHUNK), CHUNK)
        in_keys = act_ref[at, INNER : INNER + STATE]
        out_keys = act_ref[at, INNER + STATE : CHANNELS]
        affinity = jnp.where(causal_tile(), dot(out_keys, in_keys, 1, 1), 0.0)
        cum = cum_ref[at, :]
        cum_rows = cum.T
        step_rows = step_ref[at, :].T
        for tile in range(INNER // LANES):
            cols = slice(tile * LANES, (tile + 1) * LANES)
            mixing = [
                (affinity * mixing_parts(cum, cum_rows, step_rows, 2 * tile + n)).astype(BF16)
                for n in range(2)
            ]
            values = act_ref[at, cols]
            zero = jnp.zeros_like(values)
            apart = jnp.concatenate(
                [jnp.where(left, values, zero), jnp.where(left, zero, values)], axis=0
            )
            local_ref[at, cols] = dot(jnp.concatenate(mixing, axis=1), apart)
        return carry

    lax.fori_loop(0, chunks, chunk, 0)


def middle_kernel(gate_plan, plan, rows, scal, local_ref, act_ref, step_ref, cum_ref, nh_ref, state_ref, x_ref,
                  c_ref, skip_ref, *refs):
    gates = len(gate_plan)
    count = gates + len(plan)
    out_ref, gn_ref, dgate_ref, gcore_ref, rowq_ref, lsg_ref, states_ref, gskip_ref = refs[
        count : count + 8
    ]
    (w_ref, wg_ref, gate_ref, gain_ref, mc_ref, gno_ref, state_s, wide_ref, core_ref, mixed_ref, acc_ref, expand_ref,
     gate_sem, sem) = refs[count + 8 :]
    gate_copies = start_pieces(scal[0], refs[:gates], gate_plan, wg_ref, gate_sem, rows)
    copies = start_pieces(scal[0], refs[gates:count], plan, w_ref, sem, rows)
    length = act_ref.shape[0]
    chunks = length // CHUNK
    tiles = INNER // LANES
    model = c_ref.shape[1]
    fill_expander(expand_ref)

    def mask(i, carry):
        at = pl.ds(pl.multiple_of(i * CHUNK, CHUNK), CHUNK)
        row = lax.broadcasted_iota(jnp.int32, (CHUNK, model), 0) + i * CHUNK
        c = c_ref[at, :]
        mc_ref[at, :] = jnp.where(row < scal[1], c.astype(F32), 0.0).astype(BF16)
        return carry

    lax.fori_loop(0, chunks, mask, 0)
    wait_all(gate_copies)

    def project(j, carry):
        at = pl.ds(pl.multiple_of(j * 384, 384), 384)
        gate_ref[:, at] = dot(nh_ref[HALO:, :], wg_ref[:, at])
        return carry

    lax.fori_loop(0, INNER // 384, project, 0)
    wait_all(copies)

    def back_project(j, carry):
        at = pl.ds(pl.multiple_of(j * 384, 384), 384)
        gno_ref[:, at] = dot(mc_ref[...], w_ref[at, 0:model], 1, 1)
        return carry

    lax.fori_loop(0, INNER // 384, back_project, 0)
    gain_ref[...] = w_ref[:, model:].astype(F32).T[0:8]
    state_s[...] = state_ref[...].astype(F32)
    acc_ref[...] = jnp.zeros_like(acc_ref)
    gskip_ref[...] = jnp.zeros_like(gskip_ref)

    def chunk(c, before):
        at = pl.ds(pl.multiple_of(c * CHUNK, CHUNK), CHUNK)
        in_keys = act_ref[at, INNER : INNER + STATE]
        out_keys = act_ref[at, INNER + STATE : CHANNELS]
        cum = cum_ref[at, :]
        last = cum[CHUNK - 1 : CHUNK]
        growth = jnp.exp(cum)
        weight = jnp.exp(last - cum) * step_ref[at, :]
        small = jnp.concatenate(
            [growth, weight, jnp.exp(cum + before), jnp.broadcast_to(jnp.exp(last), (8, LANES))], axis=0
        )
        wide_ref[...] = dot(jnp.concatenate(two_parts(small), axis=1), expand_ref[...])
        state_b = state_s[...].astype(BF16)
        states_ref[c] = state_b
        squares = jnp.zeros((CHUNK, LANES), F32)
        for tile in range(tiles):
            cols = slice(tile * LANES, (tile + 1) * LANES)
            values = act_ref[at, cols].astype(F32)
            readout = dot(out_keys, state_b[:, cols])
            core = local_ref[at, cols] + wide_ref[0:CHUNK, cols] * readout
            mixed = core + skip_ref[0:1, cols] * values
            core_ref[:, cols] = core
            mixed_ref[:, cols] = mixed
            gate = gate_ref[at, cols]
            gated = mixed * (gate * jax.nn.sigmoid(gate))
            squares = squares + gated * gated
            weighted = (wide_ref[CHUNK : 2 * CHUNK, cols] * values).astype(BF16)
            state_s[:, cols] = wide_ref[3 * CHUNK : 3 * CHUNK + 1, cols] * state_s[:, cols] + dot(
                in_keys, weighted, 0, 0
            )
        scale = lax.rsqrt(jnp.sum(squares, axis=1, keepdims=True) / INNER + EPSILON)
        products = jnp.zeros((CHUNK, LANES), F32)
        for tile in range(tiles):
            cols = slice(tile * LANES, (tile + 1) * LANES)
            gate = gate_ref[at, cols]
            gn = mixed_ref[:, cols] * (gate * jax.nn.sigmoid(gate)) * scale
            gain = gain_ref[0:1, cols]
            gn_ref[at, cols] = (gn * gain).astype(BF16)
            products = products + gn * (gno_ref[at, cols] * gain)
        mean = jnp.sum(products, axis=1, keepdims=True) / INNER
        rowq = jnp.zeros((CHUNK, LANES), F32)
        for tile in range(tiles):
            cols = slice(tile * LANES, (tile + 1) * LANES)
            gate = gate_ref[at, cols]
            sig = jax.nn.sigmoid(gate)
            silu = gate * sig
            mixed = mixed_ref[:, cols]
            dgated = scale * (gno_ref[at, cols] * gain_ref[0:1, cols] - (mixed * silu * scale) * mean)
            g = dgated * silu
            dgate_ref[at, cols] = (dgated * mixed * (sig * (1.0 + gate * (1.0 - sig)))).astype(BF16)
            gcore = g.astype(BF16)
            gcore_ref[at, cols] = gcore
            values = act_ref[at, cols].astype(F32)
            gskip_ref[:, cols] = gskip_ref[:, cols] + jnp.sum(
                (g * values).reshape(CHUNK // 8, 8, LANES), axis=0
            )
            gcore_f = gcore.astype(F32)
            rowq = rowq + head_sums(gcore_f * core_ref[:, cols], tile)
            scaled = (wide_ref[2 * CHUNK : 3 * CHUNK, cols] * gcore_f).astype(BF16)
            acc_ref[:, cols] = acc_ref[:, cols] + dot(out_keys, scaled, 0, 0)
        rowq_ref[at, :] = rowq
        return before + last

    lax.fori_loop(0, chunks, chunk, jnp.zeros((1, LANES), F32))
    lsg_ref[...] = acc_ref[...].astype(BF16)

    def finish(i, carry):
        at = pl.ds(pl.multiple_of(i * CHUNK, CHUNK), CHUNK)
        row = lax.broadcasted_iota(jnp.int32, (CHUNK, model), 0) + i * CHUNK
        u = x_ref[pl.ds(pl.multiple_of(i * CHUNK + HALO, HALO), CHUNK), :].astype(F32)
        out_ref[at, :] = (u + jnp.where(row < scal[1], gno_ref[at, 0:model], 0.0)).astype(BF16)
        return carry

    for j in range(2):
        cols = slice(j * model // 2, (j + 1) * model // 2)
        gno_ref[:, cols] = dot(gn_ref[...], w_ref[:, cols])
    lax.fori_loop(0, chunks, finish, 0)


def put_block(dp, block, keep_ref, send_ref, start, cols, part):
    away = jnp.bitwise_xor(dp, block)
    slot = away // 2
    rows = part.shape[0]

    @pl.when(away % 2 == 0)
    def _():
        keep_ref[slot, start : start + rows, cols] = part

    @pl.when(away % 2 == 1)
    def _():
        send_ref[slot, start : start + rows, cols] = part


def early_kernel(rows, devices, scal, gn_ref, c_ref, nh_ref, dgate_ref, keep_ref, send_ref, mc_ref):
    length, model = c_ref.shape
    chunks = length // CHUNK

    def mask(i, carry):
        at = pl.ds(pl.multiple_of(i * CHUNK, CHUNK), CHUNK)
        row = lax.broadcasted_iota(jnp.int32, (CHUNK, model), 0) + i * CHUNK
        mc_ref[at, :] = jnp.where(row < scal[1], c_ref[at, :].astype(F32), 0.0).astype(BF16)
        return carry

    lax.fori_loop(0, chunks, mask, 0)
    half = model // 2
    for j in range(2 * INNER // model):
        part = dot(nh_ref[HALO:, :], dgate_ref[:, j * half : (j + 1) * half], 0, 0).astype(BF16)
        start = (j // 2) * rows
        cols = slice((j % 2) * half, (j % 2 + 1) * half)
        for block in range(devices):
            put_block(
                scal[0], block, keep_ref, send_ref, start, cols, part[block * rows : (block + 1) * rows]
            )
    for j in range(INNER // half):
        part = dot(gn_ref[:, j * half : (j + 1) * half], mc_ref[...], 0, 0).astype(BF16)
        each = half // (2 * rows)
        for n in range(each):
            put_block(
                scal[0], j * each + n, keep_ref, send_ref, 2 * rows, slice(0, model),
                part[n * 2 * rows : (n + 1) * 2 * rows],
            )


def local_back_kernel(plan, rows, scal, act_ref, step_ref, cum_ref, gcore_ref, dgate_ref, *refs):
    count = len(plan)
    pieces = refs[:count]
    gvl_ref, gk_ref, gng_ref, w_ref, sem = refs[count:]
    copies = start_pieces(scal[0], pieces, plan, w_ref, sem, rows)
    chunks = act_ref.shape[0] // CHUNK
    half = gng_ref.shape[1] // 2
    left = lax.broadcasted_iota(jnp.int32, (CHUNK, LANES), 1) < HDIM

    def chunk(c, carry):
        at = pl.ds(pl.multiple_of(c * CHUNK, CHUNK), CHUNK)
        in_keys = act_ref[at, INNER : INNER + STATE]
        out_keys = act_ref[at, INNER + STATE : CHANNELS]
        affinity = jnp.where(causal_tile(), dot(out_keys, in_keys, 1, 1), 0.0)
        cum = cum_ref[at, :]
        cum_rows = cum.T
        step_rows = step_ref[at, :].T
        gaff = jnp.zeros((CHUNK, CHUNK), F32)
        for tile in range(INNER // LANES):
            cols = slice(tile * LANES, (tile + 1) * LANES)
            values = act_ref[at, cols]
            grads = gcore_ref[at, cols]
            zero = jnp.zeros_like(grads)
            apart = jnp.concatenate(
                [jnp.where(left, grads, zero), jnp.where(left, zero, grads)], axis=0
            )
            gmix = dot(apart, values, 1, 1)
            mixing = []
            for n in range(2):
                weight = mixing_parts(cum, cum_rows, step_rows, 2 * tile + n)
                gaff = gaff + gmix[n * CHUNK : (n + 1) * CHUNK] * weight
                mixing.append((affinity * weight).astype(BF16))
            back = dot(jnp.concatenate(mixing, axis=1), grads, 0, 0)
            gvl_ref[at, cols] = jnp.where(left, back[0:CHUNK], back[CHUNK:])
        gaff = jnp.where(causal_tile(), gaff, 0.0).astype(BF16)
        gk_ref[at, 0:STATE] = dot(gaff, out_keys, 0, 0)
        gk_ref[at, STATE : 2 * STATE] = dot(gaff, in_keys)
        return carry

    lax.fori_loop(0, chunks, chunk, 0)
    wait_all(copies)
    for j in range(2):
        cols = slice(j * half, (j + 1) * half)
        gng_ref[:, cols] = dot(dgate_ref[...], w_ref[cols, :], 1, 1)


def scan_back_kernel(act_ref, step_ref, sig_ref, cum_ref, gcore_ref, gvl_ref, gk_ref, rowq_ref, states_ref,
                     gout_ref, gskip_ref, skip_ref, cext_ref, cw_ref, cb_ref, dl_ref, gpad_ref, graw_ref, small_ref,
                     gstate_ref, wide_ref, gact_ref, expand_ref):
    length = act_ref.shape[0]
    chunks = length // CHUNK
    tiles = INNER // LANES
    fill_expander(expand_ref)
    gstate_ref[...] = gout_ref[...].astype(F32)
    small_ref[...] = jnp.zeros_like(small_ref)
    small_ref[6:7, 0:INNER] = jnp.sum(gskip_ref[...], axis=0, keepdims=True)
    gpad_ref[0:HALO, :] = jnp.zeros((HALO, CHANNELS), F32)
    gpad_ref[HALO + length :, :] = jnp.zeros((HALO, CHANNELS), F32)
    graw_ref[0:HALO, :] = jnp.zeros((HALO, LANES), BF16)
    rate = -jnp.exp(dl_ref[0:1, :])
    end = lax.broadcasted_iota(jnp.int32, (CHUNK, LANES), 0) == CHUNK - 1

    def chunk(n, carry):
        gdecay, gbias = carry
        c = chunks - 1 - n
        at = pl.ds(pl.multiple_of(c * CHUNK, CHUNK), CHUNK)
        in_keys = act_ref[at, INNER : INNER + STATE]
        out_keys = act_ref[at, INNER + STATE : CHANNELS]
        cum = cum_ref[at, :]
        step = step_ref[at, :]
        sig = sig_ref[at, :]
        last = cum[CHUNK - 1 : CHUNK]
        small = jnp.concatenate(
            [jnp.exp(cum), jnp.exp(last - cum) * step, jnp.broadcast_to(jnp.exp(last), (8, LANES))], axis=0
        )
        wide_ref[...] = dot(jnp.concatenate(two_parts(small), axis=1), expand_ref[...])
        colq = jnp.zeros((CHUNK, LANES), F32)
        ends = jnp.zeros((8, LANES), F32)
        gin = gk_ref[at, 0:STATE]
        gout = gk_ref[at, STATE : 2 * STATE]
        for tile in range(tiles):
            cols = slice(tile * LANES, (tile + 1) * LANES)
            values = act_ref[at, cols].astype(F32)
            grads = gcore_ref[at, cols].astype(F32)
            gstate = gstate_ref[:, cols]
            gstate_b = gstate.astype(BF16)
            state = states_ref[c, :, cols]
            weight = wide_ref[CHUNK : 2 * CHUNK, cols]
            decay = wide_ref[2 * CHUNK : 2 * CHUNK + 1, cols]
            gvs = weight * dot(in_keys, gstate_b)
            gvalues = gvl_ref[at, cols] + gvs
            colq = colq + head_sums(values * gvalues, tile)
            passed = jnp.sum((values * gvs).reshape(CHUNK // 8, 8, LANES), axis=0) + decay * jnp.sum(
                (gstate * state.astype(F32)).reshape(STATE // 8, 8, LANES), axis=0
            )
            ends = ends + head_sums(passed, tile)
            gin = gin + dot((weight * values).astype(BF16), gstate_b, 1, 1)
            scaled = (wide_ref[0:CHUNK, cols] * grads).astype(BF16)
            gout = gout + dot(scaled, state, 1, 1)
            gstate_ref[:, cols] = decay * gstate + dot(out_keys, scaled, 0, 0)
            gact_ref[:, cols] = gvalues + skip_ref[0:1, cols] * grads
        gact_ref[:, INNER : INNER + STATE] = gin
        gact_ref[:, INNER + STATE : CHANNELS] = gout
        gcum = rowq_ref[at, :] - colq
        gcum = gcum + jnp.where(end, jnp.sum(ends, axis=0, keepdims=True), 0.0)
        glog = running_sum(gcum, reverse=True)
        gdecay = gdecay + jnp.sum((glog * (rate * step)).reshape(CHUNK // 8, 8, LANES), axis=0)
        ratio = jnp.where(step > 0.0, sig / jnp.where(step > 0.0, step, 1.0), 0.0)
        graw = colq * ratio + rate * glog * sig
        gbias = gbias + jnp.sum(graw.reshape(CHUNK // 8, 8, LANES), axis=0)
        first = pl.multiple_of(c * CHUNK, CHUNK)
        graw_ref[pl.ds(first + HALO, CHUNK), :] = graw.astype(BF16)
        for tile in range(CHANNELS // LANES):
            cols = slice(tile * LANES, (tile + 1) * LANES)
            part = cext_ref[pl.ds(first, CHUNK + HALO), cols].astype(F32)
            moved = [pltpu.roll(part, KCONV - 1 - k, 0)[HALO:] for k in range(KCONV - 1)] + [part[HALO:]]
            out = cb_ref[0:1, cols]
            for k in range(KCONV):
                out = out + cw_ref[k : k + 1, cols] * moved[k]
            sc = jax.nn.sigmoid(out)
            gconv = gact_ref[:, cols] * (sc * (1.0 + out * (1.0 - sc)))
            gpad_ref[pl.ds(first + HALO, CHUNK), cols] = gconv
            for k in range(KCONV):
                small_ref[k : k + 1, cols] = small_ref[k : k + 1, cols] + jnp.sum(
                    gconv * moved[k], axis=0, keepdims=True
                )
            small_ref[4:5, cols] = small_ref[4:5, cols] + jnp.sum(gconv, axis=0, keepdims=True)
        return gdecay, gbias

    zero = jnp.zeros((8, LANES), F32)
    gdecay, gbias = lax.fori_loop(0, chunks, chunk, (zero, zero))
    small_ref[5:6, 0:LANES] = jnp.sum(gdecay, axis=0, keepdims=True)
    small_ref[5:6, LANES : 2 * LANES] = jnp.sum(gbias, axis=0, keepdims=True)


def conv_back_kernel(rows, devices, scal, gpad_ref, graw_ref, nh_ref, cw_ref, gproj_ref, keep_ref, send_ref):
    total_rows = nh_ref.shape[0]
    gproj_ref[:, CHANNELS:] = graw_ref[...]

    def conv_back(i, carry):
        first = pl.multiple_of(i * HALO, HALO)
        for tile in range(CHANNELS // LANES):
            cols = slice(tile * LANES, (tile + 1) * LANES)
            part = gpad_ref[pl.ds(first, 2 * HALO), cols]
            total = cw_ref[KCONV - 1 : KCONV, cols] * part[:HALO]
            for k in range(KCONV - 1):
                ahead = pltpu.roll(part, 2 * HALO - (KCONV - 1 - k), 0)[:HALO]
                total = total + cw_ref[k : k + 1, cols] * ahead
            gproj_ref[pl.ds(first, HALO), cols] = total.astype(BF16)
        return carry

    lax.fori_loop(0, total_rows // HALO, conv_back, 0)
    for j in range(WIDTH // 384):
        cols = slice(j * 384, (j + 1) * 384)
        part = dot(nh_ref[...], gproj_ref[:, cols], 0, 0).astype(BF16)
        for block in range(devices):
            put_block(
                scal[0], block, keep_ref, send_ref, 0, cols, part[block * rows : (block + 1) * rows]
            )


def token_back_kernel(plan, rows, scal, gproj_ref, gng_ref, x_ref, c_ref, *refs):
    count = len(plan)
    pieces = refs[:count]
    gtok_ref, last_ref, ghalo_ref, w_ref, acc_ref, sem = refs[count:]
    copies = start_pieces(scal[0], pieces, plan, w_ref, sem, rows)
    length, model = c_ref.shape
    wait_all(copies)
    for j in range(2):
        cols = slice(j * model // 2, (j + 1) * model // 2)
        acc_ref[:, cols] = dot(gproj_ref[...], w_ref[cols, :], 1, 1)
    acc_ref[HALO:, :] = acc_ref[HALO:, :] + gng_ref[...]
    gain = gain_row(w_ref)

    def norm_back(i, carry):
        at = pl.ds(pl.multiple_of(i * HALO, HALO), HALO)
        u = x_ref[at, :].astype(F32)
        scale = lax.rsqrt(jnp.mean(u * u, axis=1, keepdims=True) + EPSILON)
        nh = u * scale
        g = acc_ref[at, :] * gain
        acc_ref[at, :] = scale * (g - nh * jnp.mean(g * nh, axis=1, keepdims=True))
        return carry

    lax.fori_loop(0, (length + HALO) // HALO, norm_back, 0)
    ghalo_ref[...] = acc_ref[0:HALO, :]
    last_ref[...] = acc_ref[length:, :] + c_ref[length - HALO :, :].astype(F32)

    def finish(i, carry):
        at = pl.ds(pl.multiple_of(i * HALO, HALO), HALO)
        grads = acc_ref[pl.ds(pl.multiple_of((i + 1) * HALO, HALO), HALO), :]
        gtok_ref[at, :] = (grads + c_ref[at, :].astype(F32)).astype(BF16)
        return carry

    lax.fori_loop(0, length // HALO, finish, 0)


def call(body, scal, whole, pieces, outs, scratch):
    first = [] if scal is None else [scal]
    smem = pl.BlockSpec(memory_space=pltpu.SMEM)
    vmem = pl.BlockSpec(memory_space=pltpu.VMEM)
    return list(pl.pallas_call(
        body,
        out_shape=[jax.ShapeDtypeStruct(shape, kind) for shape, kind in outs],
        in_specs=[smem] * len(first) + [vmem] * len(whole) + [pl.BlockSpec(memory_space=pl.ANY)] * len(pieces),
        out_specs=[vmem] * len(outs),
        scratch_shapes=scratch,
        compiler_params=pltpu.CompilerParams(vmem_limit_bytes=VMEM_LIMIT),
    )(*first, *whole, *pieces))


def lane_row(vector):
    return jnp.pad(vector, (0, LANES - vector.shape[0]))[None]


def per_device(tokens, lengths, dealing, cotangent, in_weight, out_weight, norm_gain, gate_gain, conv_weight,
               conv_bias, decay_log, step_bias, skip_gain):
    dp, seq = lax.axis_index("dp"), lax.axis_index("seq")
    devices, size = lax.axis_size("dp"), lax.axis_size("seq")
    group = size // 2
    lin = seq * 2 + dp % 2
    holder = lin // group
    place = {"dp": dp, "seq": seq, "micro": holder // 2, "column": holder % 2, "turn": lin % group}
    block_len, model = tokens.shape[2:]
    length = 2 * block_len
    shard_rows = in_weight.shape[0]
    rows = shard_rows * size
    bits = list(range(1, devices.bit_length() - 1))
    tok = tokens[:, 0]
    cot = cotangent[:, 0]

    gains = jnp.concatenate(
        [norm_gain[:, None], jnp.swapaxes(gate_gain.reshape(2, shard_rows), 0, 1)], axis=1
    )
    conv_shard = jnp.concatenate([in_weight[:, INNER:], gains], axis=1)
    conv_shard = jnp.pad(conv_shard, ((0, 0), (0, WIDTH - conv_shard.shape[1])))
    rest_shard = jnp.concatenate([in_weight[:, :model], in_weight[:, model:INNER], out_weight], axis=0)
    conv_bits, rest_bits = bits, bits[::-1]

    def conv_streams(gathered):
        gain_rows = jnp.swapaxes(gathered[:, :, CHANNELS + HEADS + 1 : CHANNELS + HEADS + 3], 1, 2)
        gain_rows = jnp.pad(gain_rows.reshape(2 * rows, 1), ((0, 0), (0, LANES - 1)))
        gate_gains.append(gain_rows)
        block = gathered.reshape(rows, WIDTH)
        return [(block[:, :SPLIT], conv_bits), (block[:, SPLIT:], rest_bits)]

    def rest_streams(gathered):
        gate_block = jnp.swapaxes(gathered[:, : 2 * shard_rows].reshape(size, 2, shard_rows, model), 0, 1)
        out_block = gathered[:, 2 * shard_rows :].reshape(2 * rows, model)
        out_block = jnp.concatenate([out_block, gate_gains[0]], axis=1)
        return [(gate_block.reshape(2 * rows, model), conv_bits), (out_block, rest_bits)]

    gate_gains = []

    dealt = devices == 8
    conv = Chain(gather_stages(conv_shard, place, conv_streams))
    if dealt:
        table = Chain(table_stages(jnp.concatenate([dealing[:, 0], lengths[:, 0]])))
        routes = Routes(place, table)
        cot_chain = Chain(cotangent_stages(cot, routes, place))
        moving = [conv, table, cot_chain]
    else:
        every = lax.all_gather(jnp.concatenate([dealing, lengths], axis=0)[:, 0], "dp", axis=0)
        goals = every[:, :2]
        source_of_out = jnp.argmax(goals == dp, axis=0)
        cot_given = deal_gathered(cot, dealing[:, 0])
        mate = lax.dynamic_index_in_dim(every, dp - dp % 2 + place["column"], 0, keepdims=False)
        own_length = jnp.where(place["micro"] == 0, mate[2], mate[3])
        moving = [conv]

    tok, rest_shard = advance((tok, rest_shard), *moving)
    blocks = to_stretch(tok, place)
    rest_shard = advance(rest_shard, *moving)
    late = place["micro"] == 1
    while conv.pending is not None:
        if blocks is not None:
            rest_shard, blocks = advance((rest_shard, blocks), *moving)
            first, second = swapped(late, blocks)
            halo = lax.ppermute(second[block_len - HALO :], BOTH, neighbour_pairs(1))
            blocks = None
        else:
            rest_shard, first, second, halo = advance((rest_shard, first, second, halo), *moving)
    x_ext = jnp.concatenate([halo, first, second])
    conv_pieces, conv_plan = [], []
    for pieces, col, width in zip(conv.value, (0, SPLIT), (SPLIT, WIDTH - SPLIT)):
        conv_pieces += [part for _, part in pieces]
        conv_plan += [(masks, [(0, 1, col, width)]) for masks, _ in pieces]
    rest = Chain(gather_stages(rest_shard, place, rest_streams))
    moving = [rest]
    if dealt:
        while table.pending is not None:
            advance((), table)
        own_length = routes.value[4, 0]
        moving = [rest, cot_chain]
    n_valid = jnp.clip(own_length - place["turn"] * length, 0, length)
    scal = jnp.stack([dp, n_valid])

    taps = jnp.pad(conv_weight, ((0, 8 - KCONV), (0, 0)))
    conv_bias_row = conv_bias[None]
    decay_row, bias_row = lane_row(decay_log), lane_row(step_bias)
    skip_row = jnp.repeat(skip_gain, HDIM)[None]

    def sems(plan):
        return pltpu.SemaphoreType.DMA((piece_count(plan),))

    wide = (length, INNER)
    made = call(
        functools.partial(project_kernel, conv_plan, rows),
        scal,
        [x_ext, taps, conv_bias_row, decay_row, bias_row],
        conv_pieces,
        [((length + HALO, model), BF16), ((length + HALO, CHANNELS), BF16), ((length, CHANNELS), BF16)]
        + [((length, LANES), F32)] * 3,
        [pltpu.VMEM((model, WIDTH), BF16), pltpu.VMEM((length + HALO, WIDTH), F32), sems(conv_plan)],
    )
    nh, cext, act, step, sig, cum = advance(made, *moving)
    local, update, total = advance(
        call(
            local_kernel,
            None,
            [act, step, cum],
            [],
            [(wide, F32), ((STATE, INNER), BF16), ((8, LANES), F32)],
            [pltpu.VMEM((STATE, INNER), F32), pltpu.VMEM((2 * LANES, INNER), BF16)],
        ),
        *moving,
    )
    passing = jnp.repeat(jnp.exp(total[0, :HEADS]), HDIM)[None] if group > 2 else None

    def relay(own, pairs):
        carried = None
        for _ in range(group - 1):
            given = own if carried is None else (passing * carried.astype(F32) + own.astype(F32)).astype(BF16)
            carried = lax.ppermute(given, BOTH, pairs)
        return jnp.zeros_like(own) if carried is None else carried

    state_in = relay(update, neighbour_pairs(1))
    while rest.pending is not None:
        state_in = advance(state_in, *moving)
    if dealt:
        while cot_chain.pending is not None:
            advance((), cot_chain)
        c_own = cot_chain.value
    else:
        c_own = jnp.concatenate(swapped(late, to_stretch(cot_given, place)))
    gate_pieces = [part for _, part in rest.value[0]]
    gate_plan = [(masks, [(0, 1, 0, model), (rows, 1, model, model)]) for masks, _ in rest.value[0]]
    out_pieces = [part for _, part in rest.value[1]]
    out_plan = [(masks, [(0, 2, 0, model + LANES)]) for masks, _ in rest.value[1]]

    out, gn, dgate, gcore, rowq, lsg, states, gskip = call(
        functools.partial(middle_kernel, gate_plan, out_plan, rows),
        scal,
        [local, act, step, cum, nh, state_in, x_ext, c_own, skip_row],
        gate_pieces + out_pieces,
        [((length, model), BF16), (wide, BF16), (wide, BF16), (wide, BF16), ((length, LANES), F32),
         ((STATE, INNER), BF16), ((length // CHUNK, STATE, INNER), BF16), ((8, INNER), F32)],
        [pltpu.VMEM((INNER, model + LANES), BF16), pltpu.VMEM((model, INNER), BF16), pltpu.VMEM(wide, F32),
         pltpu.VMEM((8, INNER), F32), pltpu.VMEM((length, model), BF16), pltpu.VMEM(wide, F32),
         pltpu.VMEM((STATE, INNER), F32), pltpu.VMEM((3 * CHUNK + 8, INNER), F32),
         pltpu.VMEM((CHUNK, INNER), F32), pltpu.VMEM((CHUNK, INNER), F32), pltpu.VMEM((STATE, INNER), F32),
         pltpu.VMEM((2 * LANES, INNER), BF16), sems(gate_plan), sems(out_plan)],
    )
    if dealt:
        moving = [Chain(output_stages(out, routes, place))]
        out_chain = moving[0]
    else:
        moving = []
        blocks = jnp.stack(swapped(place["seq"] % 2 == 1, from_stretch(out[:block_len], out[block_len:], place)))
        outputs = deal_gathered(blocks, source_of_out)
    grad_out_state = relay(lsg, neighbour_pairs(-1))

    half_dp = devices // 2
    keep1, send1, gcore, dgate = advance(
        call(
            functools.partial(early_kernel, rows, devices),
            scal,
            [gn, c_own, nh, dgate],
            [],
            [((half_dp, 4 * rows, model), BF16)] * 2,
            [pltpu.VMEM((length, model), BF16)],
        )
        + [gcore, dgate],
        *moving,
    )

    def early_streams(parts):
        return [(parts[:, : 2 * rows], bits[::-1]), (parts[:, 2 * rows :], bits)]

    def early_join(parts):
        gates = parts[0].reshape(2, size, shard_rows, model)
        return jnp.concatenate([gates[0], gates[1], parts[1].reshape(size, 2 * shard_rows, model)], axis=1)

    early = Chain(reduce_stages(keep1, send1, place, early_streams, early_join))
    moving.append(early)
    made = call(
        functools.partial(local_back_kernel, gate_plan, rows),
        scal,
        [act, step, cum, gcore, dgate],
        gate_pieces,
        [(wide, F32), ((length, 2 * STATE), F32), ((length, model), F32)],
        [pltpu.VMEM((model, INNER), BF16), sems(gate_plan)],
    )
    gvl, gk, gng, grad_out_state = advance(made + [grad_out_state], *moving)
    gpad, graw, small = advance(
        call(
            scan_back_kernel,
            None,
            [act, step, sig, cum, gcore, gvl, gk, rowq, states, grad_out_state, gskip, skip_row, cext, taps,
             conv_bias_row, decay_row],
            [],
            [((length + 2 * HALO, CHANNELS), F32), ((length + HALO, LANES), BF16), ((8, WIDTH), F32)],
            [pltpu.VMEM((STATE, INNER), F32), pltpu.VMEM((2 * CHUNK + 8, INNER), F32),
             pltpu.VMEM((CHUNK, CHANNELS), F32), pltpu.VMEM((2 * LANES, INNER), BF16)],
        ),
        *moving,
    )
    sums = Chain(sum_stages(small))
    moving.append(sums)
    gproj, keep2, send2 = advance(
        call(
            functools.partial(conv_back_kernel, rows, devices),
            scal,
            [gpad, graw, nh, taps],
            [],
            [((length + HALO, WIDTH), BF16)] + [((half_dp, rows, WIDTH), BF16)] * 2,
            [],
        ),
        *moving,
    )

    def late_streams(parts):
        return [(parts[:, :, :SPLIT], bits[::-1]), (parts[:, :, SPLIT:], bits)]

    def late_join(parts):
        return jnp.concatenate(parts, axis=1).reshape(size, shard_rows, WIDTH)

    final = Chain(reduce_stages(keep2, send2, place, late_streams, late_join))
    moving.append(final)
    gtok, last, ghalo = advance(
        call(
            functools.partial(token_back_kernel, conv_plan, rows),
            scal,
            [gproj, gng, x_ext, c_own],
            conv_pieces,
            [((length, model), BF16), ((HALO, model), F32), ((HALO, model), F32)],
            [pltpu.VMEM((model, WIDTH), BF16), pltpu.VMEM((length + HALO, model), F32), sems(conv_plan)],
        ),
        *moving,
    )

    from_next = lax.ppermute(ghalo, BOTH, neighbour_pairs(-1))
    from_next = advance(from_next, *moving)
    tail = (last + from_next).astype(BF16)
    gtok_second = jnp.concatenate([gtok[block_len : length - HALO], tail])
    back = from_stretch(gtok[:block_len], gtok_second, place)
    while any(chain.pending is not None for chain in moving):
        advance((), *moving)
    grad_tokens = jnp.stack(swapped(place["seq"] % 2 == 1, back))
    if dealt:
        outputs = out_chain.value

    early_sum, late_sum, sums = early.value, final.value, sums.value
    raw_in = jnp.concatenate(
        [early_sum[:shard_rows], early_sum[shard_rows : 2 * shard_rows],
         late_sum[:, : in_weight.shape[1] - INNER]], axis=1
    )
    raw_out = early_sum[2 * shard_rows :]
    grad_norm_gain = jnp.sum(raw_in * in_weight.astype(F32), axis=1) / norm_gain.astype(F32)
    grad_gate_gain = jnp.sum(raw_out * out_weight.astype(F32), axis=1) / gate_gain.astype(F32)
    grad_skip = jnp.sum(sums[6, :INNER].reshape(HEADS, HDIM), axis=1)
    return (
        outputs[:, None],
        grad_tokens[:, None],
        raw_in,
        raw_out,
        grad_norm_gain,
        grad_gate_gain,
        sums[0:KCONV, :CHANNELS],
        sums[4, :CHANNELS],
        sums[5, :HEADS],
        sums[5, LANES : LANES + HEADS],
        grad_skip,
    )


def solution(mesh):
    in_specs = (
        P(None, "dp", "seq", None),
        P(None, "dp"),
        P(None, "dp"),
        P(None, "dp", "seq", None),
        P(BOTH, None),
        P(BOTH, None),
        P(BOTH),
        P(BOTH),
        P(),
        P(),
        P(),
        P(),
        P(),
    )
    out_specs = (
        P(None, "dp", "seq", None),
        P(None, "dp", "seq", None),
        P(BOTH, None),
        P(BOTH, None),
        P(BOTH),
        P(BOTH),
        P(),
        P(),
        P(),
        P(),
        P(),
    )
    return jax.shard_map(per_device, mesh=mesh, in_specs=in_specs, out_specs=out_specs, check_vma=False)
```

```python
import functools

import jax
import jax.numpy as jnp
from jax import lax
from jax.experimental import pallas as pl
from jax.experimental.pallas import tpu as pltpu
from jax.sharding import PartitionSpec as P

INNER = 1536
HEADS = 24
HDIM = 64
STATE = 128
KCONV = 4
CHANNELS = INNER + 2 * STATE
LANES = 128
CHUNK = 128
HALO = 16
PIECES = 4
EPSILON = 1e-05
WIDTH = CHANNELS + LANES
F32 = jnp.float32
BF16 = jnp.bfloat16
BOTH = ("dp", "seq")
VMEM_LIMIT = 60 * 1024 * 1024


def flip_dp(value, mask):
    pairs = [(i, i ^ mask) for i in range(lax.axis_size("dp"))]
    return lax.ppermute(value, "dp", pairs)


def step_bits(size):
    return list(range(1, size.bit_length() - 1))


def flip_step(value, step):
    size = lax.axis_size("dp")
    bits = step_bits(size)
    pairs = [(i, i ^ (1 << (bits[-1 - step] if i % 2 else bits[step]))) for i in range(size)]
    return lax.ppermute(value, "dp", pairs)


def shift_seq(value, step):
    size = lax.axis_size("seq")
    return lax.ppermute(value, "seq", [(i, (i + step) % size) for i in range(size)])


def column_place(dp_even, lin):
    return (dp_even + lin % 2) * lax.axis_size("seq") + lin // 2


def unit_pairs(parity):
    size = lax.axis_size("seq")
    pairs = []
    for dp in range(lax.axis_size("dp")):
        core = dp % 2
        for block in range(size):
            micro = (block % 2) ^ parity
            lin = (2 * micro + core) * (size // 2) + block // 2
            pairs.append((dp * size + block, column_place(dp - core, lin)))
    return pairs


def neighbour_pairs(step):
    size = lax.axis_size("seq")
    group = size // 2
    pairs = []
    for dp_even in range(0, lax.axis_size("dp"), 2):
        for lin in range(2 * size):
            if 0 <= lin % group + step < group:
                pairs.append((column_place(dp_even, lin), column_place(dp_even, lin + step)))
    return pairs


def reversed_pairs(pairs):
    return [(target, source) for source, target in pairs]


def to_stretch(blocks, place):
    odd = place["seq"] % 2 == 1
    first = lax.ppermute(jnp.where(odd, blocks[1], blocks[0]), BOTH, unit_pairs(0))
    second = lax.ppermute(jnp.where(odd, blocks[0], blocks[1]), BOTH, unit_pairs(1))
    return first, second


def swapped(swap, pair):
    return jnp.where(swap, pair[1], pair[0]), jnp.where(swap, pair[0], pair[1])


def from_stretch(first, second, place):
    late = place["micro"] == 1
    one = lax.ppermute(jnp.where(late, second, first), BOTH, reversed_pairs(unit_pairs(0)))
    two = lax.ppermute(jnp.where(late, first, second), BOTH, reversed_pairs(unit_pairs(1)))
    return one, two


class Chain:
    def __init__(self, stages):
        self.stages = stages
        self.value = None
        self.pending = next(stages)

    def feed(self, arrived):
        try:
            self.pending = self.stages.send(arrived)
        except StopIteration as stop:
            self.pending = None
            self.value = stop.value


def advance(held, *chains):
    moving = [chain for chain in chains if chain.pending is not None]
    held, arrived = lax.optimization_barrier((held, [chain.pending for chain in moving]))
    for chain, got in zip(moving, arrived):
        chain.feed(got)
    return held


def seq_shifts(shard):
    return [shift_seq(shard, j) for j in range(1, lax.axis_size("seq"))]


def seq_order(shard, arrived, place):
    size = lax.axis_size("seq")
    got = [shard] + list(arrived)
    rows = []
    for i in range(size):
        row = got[0]
        for j in range(1, size):
            row = jnp.where((place["seq"] - i) % size == j, got[j], row)
        rows.append(row)
    return jnp.stack(rows)


def seq_stages(shard, place):
    arrived = yield seq_shifts(shard)
    return seq_order(shard, arrived, place)


def spread_stages(block):
    steps = len(step_bits(lax.axis_size("dp")))
    held, last, turned = block[None], None, None
    for step in range(steps):
        if last is not None:
            held = jnp.concatenate([held, last])
        if step < steps - 1:
            last = (yield [flip_step(held, step)])[0]
        else:
            last, turned = yield [flip_step(held, step), flip_dp(held, 1)]
    end = (yield [flip_dp(last, 1)])[0]
    return [held, last, turned, end]


def spread_masks(size):
    found = []
    for bits in (step_bits(size), step_bits(size)[::-1]):
        masks, last = (0,), None
        for bit in bits:
            if last is not None:
                masks = masks + last
            last = tuple(m ^ (1 << bit) for m in masks)
        found.append((masks, last))
    even, odd = found
    own = [(even[n], odd[n]) for n in range(2)]
    return own + [(tuple(m ^ 1 for m in b), tuple(m ^ 1 for m in a)) for a, b in own]


def reduce_stages(keep, send, place, take):
    steps = len(step_bits(lax.axis_size("dp")))
    got = yield [flip_dp(send, 1)]
    parts = [part.reshape((2,) * steps + part.shape[1:]) for part in (keep, got[0])]
    for step in range(steps):
        got = yield [flip_step(add_up([part[1] for part in parts]).astype(BF16), step)]
        parts = [part[0] for part in parts] + got
    size = lax.axis_size("seq")

    def rows_for(j):
        return add_up([take(part, (place["seq"] + j) % size) for part in parts])

    moved = yield [shift_seq(rows_for(j).astype(BF16), j) for j in range(1, size)]
    return add_up([rows_for(0)] + moved)


def add_up(parts):
    total = parts[0].astype(F32)
    for part in parts[1:]:
        total = total + part.astype(F32)
    return total


def sum_stages(value):
    value = value + flip_dp(value, 1)
    size = lax.axis_size("seq")
    apart = 1
    while apart < size:
        got = yield [lax.ppermute(value, "seq", [(i, i ^ apart) for i in range(size)])]
        value = value + got[0]
        apart *= 2
    for bit in range(1, lax.axis_size("dp").bit_length() - 1):
        got = yield [flip_dp(value, 1 << bit)]
        value = value + got[0]
    return value


def dp_table(row):
    table = row[None]
    for bit in range(lax.axis_size("dp").bit_length() - 1):
        table = jnp.concatenate([table, flip_dp(table, 1 << bit)])
    return table


def route_row(dp, goal, first_bit, second_bit):
    held = [0, 1, first_bit, first_bit | 1]

    def chosen(base):
        low = jnp.int32(0)
        high = jnp.int32(0)
        for n in range(3, -1, -1):
            away = jnp.bitwise_xor(goal[base ^ held[n]], jnp.bitwise_xor(dp, base))
            cross = (jnp.bitwise_and(away, second_bit) != 0) & (jnp.bitwise_and(away, first_bit) == 0)
            low = jnp.where(cross, n, low)
        for n in range(4):
            away = jnp.bitwise_xor(goal[base ^ held[n]], jnp.bitwise_xor(dp, base))
            cross = (jnp.bitwise_and(away, second_bit) != 0) & (jnp.bitwise_and(away, first_bit) == 0)
            high = jnp.where(cross, n, high)
        return low, high

    low, high = chosen(0)
    other_low, _ = chosen(second_bit)
    row = [low, high]
    for side in range(2):
        pick = jnp.int32(0)
        target = jnp.bitwise_xor(dp, side)
        for n in range(4):
            pick = jnp.where(goal[held[n]] == target, n, pick)
            far = jnp.where(other_low == n, 4, 5)
            pick = jnp.where(goal[held[n] ^ second_bit] == target, far, pick)
        row.append(pick)
    return row


def route_kernel(place_ref, table_ref, out_ref):
    dp = place_ref[0]
    size = table_ref.shape[0]
    for way in range(2):
        for micro in range(2):
            goal = []
            for r in range(size):
                if way == 1:
                    goal.append(table_ref[r, micro])
                else:
                    found = jnp.int32(0)
                    for other in range(size):
                        hit = table_ref[other, micro] == jnp.bitwise_xor(dp, r)
                        found = jnp.where(hit, jnp.bitwise_xor(dp, other), found)
                    goal.append(found)
            even = route_row(dp, goal, 2, 4)
            odd = route_row(dp, goal, 4, 2)
            for n in range(4):
                out_ref[way * 2 + micro, n] = jnp.where(jnp.bitwise_and(dp, 1) == 0, even[n], odd[n])
    core = jnp.bitwise_and(dp, 1)
    column = jnp.bitwise_xor(core, place_ref[2])
    micro = place_ref[1]
    own = jnp.where(micro == 0, table_ref[0, 2], table_ref[0, 3])
    other = jnp.where(micro == 0, table_ref[1, 2], table_ref[1, 3])
    out_ref[4, 0] = jnp.where(column == 0, own, other)
    out_ref[4, 1] = place_ref[3]
    for n in range(2, 4):
        out_ref[4, n] = jnp.int32(0)


def make_routes(place, table):
    return pl.pallas_call(
        route_kernel,
        out_shape=jax.ShapeDtypeStruct((5, 4), jnp.int32),
        in_specs=[pl.BlockSpec(memory_space=pltpu.SMEM)] * 2,
        out_specs=pl.BlockSpec(memory_space=pltpu.SMEM),
    )(jnp.stack([place["dp"], place["micro"], place["column"], place["seq"] % 2]), table)


def pick_entries(index, entries, out, also=True):
    for n, entry in enumerate(entries):

        @pl.when((index == n) & also)
        def _():
            out[...] = entry[...]


def entries_of(micro, refs):
    return [ref.at[micro, n] for ref in refs for n in range(2)]


def pick_sent_kernel(first, route_ref, pair_ref, came_ref, sent_ref):
    for micro in range(2):
        for k in range(2):
            entries = entries_of(micro, (pair_ref, came_ref))
            pick_entries(route_ref[first + micro, k], entries, sent_ref.at[micro, k])


def pick_last_kernel(first, route_ref, pair_ref, came_ref, far_ref, own_ref, partner_ref):
    for micro in range(2):
        entries = entries_of(micro, (pair_ref, came_ref, far_ref))
        for k, out_ref in enumerate((own_ref, partner_ref)):
            pick_entries(route_ref[first + micro, 2 + k], entries, out_ref.at[micro])


def pick(body, routes, shapes, *held):
    vmem = pl.BlockSpec(memory_space=pltpu.VMEM)
    return pl.pallas_call(
        body,
        out_shape=[jax.ShapeDtypeStruct(shape, BF16) for shape in shapes],
        in_specs=[pl.BlockSpec(memory_space=pltpu.SMEM)] + [vmem] * len(held),
        out_specs=[vmem] * len(shapes),
    )(routes, *held)


def core_pair(items, place):
    low_core = place["dp"] % 2 == 0
    half = items.shape[1] // 2
    mine, give = swapped(jnp.logical_not(low_core), (items[:, :half], items[:, half:]))
    return jnp.stack([mine, flip_dp(give, 1)], axis=1)


def cotangent_stages(pair, routes, place):
    low_core = place["dp"] % 2 == 0
    pair = (yield [pair])[0]
    came = (yield [flip_step(pair, 0)])[0]
    (sent,) = yield pick(functools.partial(pick_sent_kernel, 0), routes, [pair.shape], pair, came)
    far = flip_step(sent, 1)
    yield []
    far = (yield [far])[0]
    body = functools.partial(pick_last_kernel, 0)
    own, partner = pick(body, routes, [pair[:, 0].shape] * 2, pair, came, far)
    blocks = jnp.concatenate(swapped(jnp.logical_not(low_core), (own, flip_dp(partner, 1))), axis=1)
    one, two = to_stretch(blocks, place)
    one = (yield [one])[0]
    two = (yield [two])[0]
    return jnp.concatenate(swapped(place["micro"] == 1, (one, two)))


def output_stages(out, routes, place):
    block = out.shape[0] // 2
    one, two = from_stretch(out[:block], out[block:], place)
    one = (yield [one])[0]
    two = (yield [two])[0]
    blocks = jnp.stack(swapped(place["seq"] % 2 == 1, (one, two)))
    tops, bottoms = blocks[:, : block // 2], blocks[:, block // 2 :]
    mine, give = swapped(place["dp"] % 2 == 1, (tops, bottoms))
    got = (yield [flip_dp(give, 1)])[0]
    pair = jnp.stack([mine, got], axis=1)
    came = (yield [flip_step(pair, 0)])[0]
    (sent,) = pick(functools.partial(pick_sent_kernel, 2), routes, [pair.shape], pair, came)
    far = (yield [flip_step(sent, 1)])[0]
    body = functools.partial(pick_last_kernel, 2)
    own, partner = pick(body, routes, [mine.shape] * 2, pair, came, far)
    back = (yield [flip_dp(partner, 1)])[0]
    return jnp.concatenate(swapped(place["dp"] % 2 == 1, (own, back)), axis=1)


def deal_gathered(items, source):
    every = lax.all_gather(items, "dp", axis=0)
    picked = [
        lax.dynamic_index_in_dim(every[:, m], source[m], 0, keepdims=False) for m in range(2)
    ]
    return jnp.stack(picked)


def dot(a, b, ca=1, cb=0):
    return lax.dot_general(a, b, (((ca,), (cb,)), ((), ())), preferred_element_type=F32)


def two_parts(x):
    high = x.astype(BF16)
    return high, (x - high.astype(F32)).astype(BF16)


def running_sum(x, reverse=False):
    rows = lax.broadcasted_iota(jnp.int32, (CHUNK, CHUNK), 0)
    cols = lax.broadcasted_iota(jnp.int32, (CHUNK, CHUNK), 1)
    reach = (rows <= cols) if reverse else (rows >= cols)
    reach = jnp.where(reach, 1.0, 0.0).astype(BF16)
    high, rest = two_parts(x)
    middle, low = two_parts(x - high.astype(F32))
    del rest
    return dot(reach, high) + dot(reach, middle) + dot(reach, low)


def fill_expander(expand_ref):
    head = lax.broadcasted_iota(jnp.int32, (LANES, INNER), 0)
    col = lax.broadcasted_iota(jnp.int32, (LANES, INNER), 1)
    one = jnp.where(col // HDIM == head, 1.0, 0.0).astype(BF16)
    expand_ref[0:LANES, :] = one
    expand_ref[LANES : 2 * LANES, :] = one


def head_sums(prod, tile):
    lane = lax.broadcasted_iota(jnp.int32, (LANES, LANES), 0)
    head = lax.broadcasted_iota(jnp.int32, (LANES, LANES), 1)
    one = jnp.where(2 * tile + lane // HDIM == head, 1.0, 0.0).astype(BF16)
    high, low = two_parts(prod)
    return dot(jnp.concatenate([high, low], axis=1), jnp.concatenate([one, one], axis=0))


def start_pieces(dp, pieces, plan, target, sem, rows):
    copies = []
    masks, spots = plan
    for piece, (even, odd) in zip(pieces, masks):
        for n in range(len(even)):
            mask = jnp.where(jnp.bitwise_and(dp, 1) == 0, even[n], odd[n])
            for source, scale, source_col, col, width in spots:
                first = pl.multiple_of(jnp.bitwise_xor(dp, mask) * (rows * scale), 8)
                copy = pltpu.make_async_copy(
                    piece.at[n, pl.ds(source, rows * scale), pl.ds(source_col, width)],
                    target.at[pl.ds(first, rows * scale), pl.ds(col, width)],
                    sem.at[len(copies)],
                )
                copy.start()
                copies.append(copy)
    return copies


def wait_all(copies):
    for copy in copies:
        copy.wait()


def piece_count(plan):
    masks, spots = plan
    return sum(len(even) for even, _ in masks) * len(spots)


def gain_row(w_ref):
    return w_ref[:, CHANNELS:].astype(F32).T[HEADS : HEADS + 1]


def project_kernel(plan, rows, scal, x_ref, cw_ref, cb_ref, dl_ref, sb_ref, *refs):
    count = PIECES
    pieces = refs[:count]
    nh_ref, cext_ref, act_ref, step_ref, sig_ref, cum_ref = refs[count : count + 6]
    w_ref, proj_ref, sem = refs[count + 6 :]
    copies = start_pieces(scal[0], pieces, plan, w_ref, sem, rows)
    total = x_ref.shape[0]
    length = total - HALO
    chunks = length // CHUNK

    tall = 3 * HALO if total % (3 * HALO) == 0 else HALO

    def norm(i, carry):
        at = pl.ds(pl.multiple_of(i * tall, tall), tall)
        u = x_ref[at, :].astype(F32)
        scale = lax.rsqrt(jnp.mean(u * u, axis=1, keepdims=True) + EPSILON)
        nh_ref[at, :] = (u * scale * gain).astype(BF16)
        return carry

    wait_all(copies)
    gain = gain_row(w_ref)
    lax.fori_loop(0, total // tall, norm, 0)

    def project(j, carry):
        at = pl.ds(pl.multiple_of(j * 384, 384), 384)
        proj_ref[:, at] = dot(nh_ref[...], w_ref[:, at])
        return carry

    lax.fori_loop(0, WIDTH // 384, project, 0)

    def conv(idx, carry):
        i, j = idx // (CHANNELS // LANES), idx % (CHANNELS // LANES)
        cols = pl.ds(pl.multiple_of(j * LANES, LANES), LANES)
        first = pl.multiple_of(i * CHUNK, CHUNK)
        part = proj_ref[pl.ds(first, CHUNK + HALO), cols]
        weights = cw_ref[:, cols]
        out = cb_ref[0:1, cols] + weights[KCONV - 1 : KCONV] * part[HALO:]
        for k in range(KCONV - 1):
            out = out + weights[k : k + 1] * pltpu.roll(part, KCONV - 1 - k, 0)[HALO:]
        act_ref[pl.ds(first, CHUNK), cols] = (out * jax.nn.sigmoid(out)).astype(BF16)
        cext_ref[pl.ds(first + HALO, CHUNK), cols] = part[HALO:].astype(BF16)
        return carry

    lax.fori_loop(0, chunks * (CHANNELS // LANES), conv, 0)
    cext_ref[0:HALO, :] = proj_ref[0:HALO, 0:CHANNELS].astype(BF16)
    lane = lax.broadcasted_iota(jnp.int32, (CHUNK, LANES), 1)
    row = lax.broadcasted_iota(jnp.int32, (CHUNK, LANES), 0)
    rate = -jnp.exp(dl_ref[0:1, :])
    for i in range(chunks):
        at = pl.ds(i * CHUNK, CHUNK)
        pre = proj_ref[pl.ds(HALO + i * CHUNK, CHUNK), pl.ds(CHANNELS, LANES)] + sb_ref[0:1, :]
        live = (row + i * CHUNK < scal[1]) & (lane < HEADS)
        soft = jnp.maximum(pre, 0.0) + jnp.log1p(jnp.exp(-jnp.abs(pre)))
        step = jnp.where(live, soft, 0.0)
        step_ref[at, :] = step
        sig_ref[at, :] = jnp.where(live, jax.nn.sigmoid(pre), 0.0)
        cum_ref[at, :] = running_sum(rate * step)


def mixing_parts(cum, cum_rows, step_rows, head):
    gap = jnp.minimum(cum[:, head : head + 1] - cum_rows[head : head + 1, :], 0.0)
    return jnp.exp(gap) * step_rows[head : head + 1, :]


def causal_tile():
    rows = lax.broadcasted_iota(jnp.int32, (CHUNK, CHUNK), 0)
    cols = lax.broadcasted_iota(jnp.int32, (CHUNK, CHUNK), 1)
    return rows >= cols


def local_kernel(act_ref, step_ref, cum_ref, local_ref, upd_ref, tot_ref, sum_ref, expand_ref):
    chunks = act_ref.shape[0] // CHUNK
    left = lax.broadcasted_iota(jnp.int32, (CHUNK, LANES), 1) < HDIM
    fill_expander(expand_ref)
    after = jnp.zeros((1, LANES), F32)
    for i in range(chunks - 1, -1, -1):
        at = pl.ds(i * CHUNK, CHUNK)
        cum = cum_ref[at, :]
        last = cum[CHUNK - 1 : CHUNK]
        weight = jnp.exp(last + after - cum) * step_ref[at, :]
        wide = dot(jnp.concatenate(two_parts(weight), axis=1), expand_ref[...])
        values = act_ref[at, 0:INNER].astype(F32)
        keys = act_ref[at, INNER : INNER + STATE]
        update = dot(keys, (wide * values).astype(BF16), 0, 0)
        sum_ref[...] = update if i == chunks - 1 else sum_ref[...] + update
        after = after + last
    upd_ref[...] = sum_ref[...].astype(BF16)
    tot_ref[...] = jnp.broadcast_to(after, tot_ref.shape)

    def chunk(c, carry):
        at = pl.ds(pl.multiple_of(c * CHUNK, CHUNK), CHUNK)
        in_keys = act_ref[at, INNER : INNER + STATE]
        out_keys = act_ref[at, INNER + STATE : CHANNELS]
        affinity = jnp.where(causal_tile(), dot(out_keys, in_keys, 1, 1), 0.0)
        cum = cum_ref[at, :]
        cum_rows = cum.T
        step_rows = step_ref[at, :].T
        for tile in range(INNER // LANES):
            cols = slice(tile * LANES, (tile + 1) * LANES)
            mixing = [
                (affinity * mixing_parts(cum, cum_rows, step_rows, 2 * tile + n)).astype(BF16)
                for n in range(2)
            ]
            values = act_ref[at, cols]
            zero = jnp.zeros_like(values)
            apart = jnp.concatenate(
                [jnp.where(left, values, zero), jnp.where(left, zero, values)], axis=0
            )
            local_ref[at, cols] = dot(jnp.concatenate(mixing, axis=1), apart)
        return carry

    lax.fori_loop(0, chunks, chunk, 0)


def middle_kernel(gate_plan, plan, rows, scal, local_ref, act_ref, step_ref, cum_ref, nh_ref, state_ref, x_ref,
                  c_ref, skip_ref, *refs):
    count = PIECES
    out_ref, gn_ref, dgate_ref, gcore_ref, rowq_ref, lsg_ref, states_ref, gskip_ref = refs[
        count : count + 8
    ]
    (w_ref, wg_ref, gate_ref, gain_ref, mc_ref, gno_ref, state_s, wide_ref, core_ref, mixed_ref, acc_ref, expand_ref,
     gate_sem, sem) = refs[count + 8 :]
    gate_copies = start_pieces(scal[0], refs[:count], gate_plan, wg_ref, gate_sem, rows)
    copies = start_pieces(scal[0], refs[:count], plan, w_ref, sem, rows)
    length = act_ref.shape[0]
    chunks = length // CHUNK
    tiles = INNER // LANES
    model = c_ref.shape[1]
    fill_expander(expand_ref)

    def mask(i, carry):
        at = pl.ds(pl.multiple_of(i * CHUNK, CHUNK), CHUNK)
        row = lax.broadcasted_iota(jnp.int32, (CHUNK, model), 0) + i * CHUNK
        c = c_ref[at, :]
        mc_ref[at, :] = jnp.where(row < scal[1], c.astype(F32), 0.0).astype(BF16)
        return carry

    lax.fori_loop(0, chunks, mask, 0)
    wait_all(gate_copies)

    def project(j, carry):
        at = pl.ds(pl.multiple_of(j * 384, 384), 384)
        gate_ref[:, at] = dot(nh_ref[HALO:, :], wg_ref[:, at])
        return carry

    lax.fori_loop(0, INNER // 384, project, 0)
    wait_all(copies)

    def back_project(j, carry):
        at = pl.ds(pl.multiple_of(j * 384, 384), 384)
        gno_ref[:, at] = dot(mc_ref[...], w_ref[at, 0:model], 1, 1)
        return carry

    lax.fori_loop(0, INNER // 384, back_project, 0)
    gain_ref[...] = w_ref[:, model:].astype(F32).T[0:8]
    state_s[...] = state_ref[...].astype(F32)
    acc_ref[...] = jnp.zeros_like(acc_ref)
    gskip_ref[...] = jnp.zeros_like(gskip_ref)

    def chunk(c, before):
        at = pl.ds(pl.multiple_of(c * CHUNK, CHUNK), CHUNK)
        in_keys = act_ref[at, INNER : INNER + STATE]
        out_keys = act_ref[at, INNER + STATE : CHANNELS]
        cum = cum_ref[at, :]
        last = cum[CHUNK - 1 : CHUNK]
        growth = jnp.exp(cum)
        weight = jnp.exp(last - cum) * step_ref[at, :]
        small = jnp.concatenate(
            [growth, weight, jnp.exp(cum + before), jnp.broadcast_to(jnp.exp(last), (8, LANES))], axis=0
        )
        wide_ref[...] = dot(jnp.concatenate(two_parts(small), axis=1), expand_ref[...])
        state_b = state_s[...].astype(BF16)
        states_ref[c] = state_b
        squares = jnp.zeros((CHUNK, LANES), F32)
        for tile in range(tiles):
            cols = slice(tile * LANES, (tile + 1) * LANES)
            values = act_ref[at, cols].astype(F32)
            readout = dot(out_keys, state_b[:, cols])
            core = local_ref[at, cols] + wide_ref[0:CHUNK, cols] * readout
            mixed = core + skip_ref[0:1, cols] * values
            core_ref[:, cols] = core
            mixed_ref[:, cols] = mixed
            gate = gate_ref[at, cols]
            gated = mixed * (gate * jax.nn.sigmoid(gate))
            squares = squares + gated * gated
            weighted = (wide_ref[CHUNK : 2 * CHUNK, cols] * values).astype(BF16)
            state_s[:, cols] = wide_ref[3 * CHUNK : 3 * CHUNK + 1, cols] * state_s[:, cols] + dot(
                in_keys, weighted, 0, 0
            )
        scale = lax.rsqrt(jnp.sum(squares, axis=1, keepdims=True) / INNER + EPSILON)
        products = jnp.zeros((CHUNK, LANES), F32)
        for tile in range(tiles):
            cols = slice(tile * LANES, (tile + 1) * LANES)
            gate = gate_ref[at, cols]
            gn = mixed_ref[:, cols] * (gate * jax.nn.sigmoid(gate)) * scale
            gain = gain_ref[0:1, cols]
            gn_ref[at, cols] = (gn * gain).astype(BF16)
            products = products + gn * (gno_ref[at, cols] * gain)
        mean = jnp.sum(products, axis=1, keepdims=True) / INNER
        rowq = jnp.zeros((CHUNK, LANES), F32)
        for tile in range(tiles):
            cols = slice(tile * LANES, (tile + 1) * LANES)
            gate = gate_ref[at, cols]
            sig = jax.nn.sigmoid(gate)
            silu = gate * sig
            mixed = mixed_ref[:, cols]
            dgated = scale * (gno_ref[at, cols] * gain_ref[0:1, cols] - (mixed * silu * scale) * mean)
            g = dgated * silu
            dgate_ref[at, cols] = (dgated * mixed * (sig * (1.0 + gate * (1.0 - sig)))).astype(BF16)
            gcore = g.astype(BF16)
            gcore_ref[at, cols] = gcore
            values = act_ref[at, cols].astype(F32)
            gskip_ref[:, cols] = gskip_ref[:, cols] + jnp.sum(
                (g * values).reshape(CHUNK // 8, 8, LANES), axis=0
            )
            gcore_f = gcore.astype(F32)
            rowq = rowq + head_sums(gcore_f * core_ref[:, cols], tile)
            scaled = (wide_ref[2 * CHUNK : 3 * CHUNK, cols] * gcore_f).astype(BF16)
            acc_ref[:, cols] = acc_ref[:, cols] + dot(out_keys, scaled, 0, 0)
        rowq_ref[at, :] = rowq
        return before + last

    lax.fori_loop(0, chunks, chunk, jnp.zeros((1, LANES), F32))
    lsg_ref[...] = acc_ref[...].astype(BF16)

    def finish(i, carry):
        at = pl.ds(pl.multiple_of(i * CHUNK, CHUNK), CHUNK)
        row = lax.broadcasted_iota(jnp.int32, (CHUNK, model), 0) + i * CHUNK
        u = x_ref[pl.ds(pl.multiple_of(i * CHUNK + HALO, HALO), CHUNK), :].astype(F32)
        out_ref[at, :] = (u + jnp.where(row < scal[1], gno_ref[at, 0:model], 0.0)).astype(BF16)
        return carry

    for j in range(2):
        cols = slice(j * model // 2, (j + 1) * model // 2)
        gno_ref[:, cols] = dot(gn_ref[...], w_ref[:, cols])
    lax.fori_loop(0, chunks, finish, 0)


def put_block(dp, devices, block, keep_ref, send_ref, start, cols, part):
    steps = len(step_bits(devices))
    away = jnp.bitwise_xor(dp, block)
    backward = away // 2
    forward = jnp.int32(0)
    for k in range(steps):
        forward = forward * 2 + jnp.bitwise_and(jnp.right_shift(backward, k), 1)
    even = jnp.bitwise_and(dp, 1) == 0
    rows = part.shape[0]

    @pl.when(away % 2 == 0)
    def _():
        keep_ref[jnp.where(even, forward, backward), start : start + rows, cols] = part

    @pl.when(away % 2 == 1)
    def _():
        send_ref[jnp.where(even, backward, forward), start : start + rows, cols] = part


def early_kernel(rows, devices, scal, gn_ref, c_ref, nh_ref, dgate_ref, keep_ref, send_ref, mc_ref):
    length, model = c_ref.shape
    chunks = length // CHUNK

    def mask(i, carry):
        at = pl.ds(pl.multiple_of(i * CHUNK, CHUNK), CHUNK)
        row = lax.broadcasted_iota(jnp.int32, (CHUNK, model), 0) + i * CHUNK
        mc_ref[at, :] = jnp.where(row < scal[1], c_ref[at, :].astype(F32), 0.0).astype(BF16)
        return carry

    lax.fori_loop(0, chunks, mask, 0)
    half = model // 2
    for j in range(2 * INNER // model):
        part = dot(nh_ref[HALO:, :], dgate_ref[:, j * half : (j + 1) * half], 0, 0).astype(BF16)
        start = (j // 2) * rows
        cols = slice((j % 2) * half, (j % 2 + 1) * half)
        for block in range(devices):
            put_block(
                scal[0], devices, block, keep_ref, send_ref, start, cols, part[block * rows : (block + 1) * rows]
            )
    for j in range(INNER // half):
        part = dot(gn_ref[:, j * half : (j + 1) * half], mc_ref[...], 0, 0).astype(BF16)
        each = half // (2 * rows)
        for n in range(each):
            put_block(
                scal[0], devices, j * each + n, keep_ref, send_ref, 2 * rows, slice(0, model),
                part[n * 2 * rows : (n + 1) * 2 * rows],
            )


def local_back_kernel(plan, rows, scal, act_ref, step_ref, cum_ref, gcore_ref, dgate_ref, *refs):
    count = PIECES
    pieces = refs[:count]
    gvl_ref, gk_ref, gng_ref, w_ref, sem = refs[count:]
    copies = start_pieces(scal[0], pieces, plan, w_ref, sem, rows)
    chunks = act_ref.shape[0] // CHUNK
    half = gng_ref.shape[1] // 2
    left = lax.broadcasted_iota(jnp.int32, (CHUNK, LANES), 1) < HDIM

    def chunk(c, carry):
        at = pl.ds(pl.multiple_of(c * CHUNK, CHUNK), CHUNK)
        in_keys = act_ref[at, INNER : INNER + STATE]
        out_keys = act_ref[at, INNER + STATE : CHANNELS]
        affinity = jnp.where(causal_tile(), dot(out_keys, in_keys, 1, 1), 0.0)
        cum = cum_ref[at, :]
        cum_rows = cum.T
        step_rows = step_ref[at, :].T
        gaff = jnp.zeros((CHUNK, CHUNK), F32)
        for tile in range(INNER // LANES):
            cols = slice(tile * LANES, (tile + 1) * LANES)
            values = act_ref[at, cols]
            grads = gcore_ref[at, cols]
            zero = jnp.zeros_like(grads)
            apart = jnp.concatenate(
                [jnp.where(left, grads, zero), jnp.where(left, zero, grads)], axis=0
            )
            gmix = dot(apart, values, 1, 1)
            mixing = []
            for n in range(2):
                weight = mixing_parts(cum, cum_rows, step_rows, 2 * tile + n)
                gaff = gaff + gmix[n * CHUNK : (n + 1) * CHUNK] * weight
                mixing.append((affinity * weight).astype(BF16))
            back = dot(jnp.concatenate(mixing, axis=1), grads, 0, 0)
            gvl_ref[at, cols] = jnp.where(left, back[0:CHUNK], back[CHUNK:])
        gaff = jnp.where(causal_tile(), gaff, 0.0).astype(BF16)
        gk_ref[at, 0:STATE] = dot(gaff, out_keys, 0, 0)
        gk_ref[at, STATE : 2 * STATE] = dot(gaff, in_keys)
        return carry

    lax.fori_loop(0, chunks, chunk, 0)
    wait_all(copies)
    for j in range(2):
        cols = slice(j * half, (j + 1) * half)
        gng_ref[:, cols] = dot(dgate_ref[...], w_ref[cols, :], 1, 1)


def scan_back_kernel(act_ref, step_ref, sig_ref, cum_ref, gcore_ref, gvl_ref, gk_ref, rowq_ref, states_ref,
                     gout_ref, gskip_ref, skip_ref, cext_ref, cw_ref, cb_ref, dl_ref, gconv_ref, head_ref, graw_ref, small_ref,
                     gstate_ref, wide_ref, gact_ref, expand_ref):
    chunks = act_ref.shape[0] // CHUNK
    tiles = INNER // LANES
    fill_expander(expand_ref)
    gstate_ref[...] = gout_ref[...].astype(F32)
    small_ref[...] = jnp.zeros_like(small_ref)
    small_ref[6:7, 0:INNER] = jnp.sum(gskip_ref[...], axis=0, keepdims=True)
    rate = -jnp.exp(dl_ref[0:1, :])
    end = lax.broadcasted_iota(jnp.int32, (CHUNK, LANES), 0) == CHUNK - 1

    def chunk(n, carry):
        gdecay, gbias = carry
        c = chunks - 1 - n
        at = pl.ds(pl.multiple_of(c * CHUNK, CHUNK), CHUNK)
        in_keys = act_ref[at, INNER : INNER + STATE]
        out_keys = act_ref[at, INNER + STATE : CHANNELS]
        cum = cum_ref[at, :]
        step = step_ref[at, :]
        sig = sig_ref[at, :]
        last = cum[CHUNK - 1 : CHUNK]
        small = jnp.concatenate(
            [jnp.exp(cum), jnp.exp(last - cum) * step, jnp.broadcast_to(jnp.exp(last), (8, LANES))], axis=0
        )
        wide_ref[...] = dot(jnp.concatenate(two_parts(small), axis=1), expand_ref[...])
        colq = jnp.zeros((CHUNK, LANES), F32)
        ends = jnp.zeros((8, LANES), F32)
        gin = gk_ref[at, 0:STATE]
        gout = gk_ref[at, STATE : 2 * STATE]
        for tile in range(tiles):
            cols = slice(tile * LANES, (tile + 1) * LANES)
            values = act_ref[at, cols].astype(F32)
            grads = gcore_ref[at, cols].astype(F32)
            gstate = gstate_ref[:, cols]
            gstate_b = gstate.astype(BF16)
            state = states_ref[c, :, cols]
            weight = wide_ref[CHUNK : 2 * CHUNK, cols]
            decay = wide_ref[2 * CHUNK : 2 * CHUNK + 1, cols]
            gvs = weight * dot(in_keys, gstate_b)
            gvalues = gvl_ref[at, cols] + gvs
            colq = colq + head_sums(values * gvalues, tile)
            passed = jnp.sum((values * gvs).reshape(CHUNK // 8, 8, LANES), axis=0) + decay * jnp.sum(
                (gstate * state.astype(F32)).reshape(STATE // 8, 8, LANES), axis=0
            )
            ends = ends + head_sums(passed, tile)
            gin = gin + dot((weight * values).astype(BF16), gstate_b, 1, 1)
            scaled = (wide_ref[0:CHUNK, cols] * grads).astype(BF16)
            gout = gout + dot(scaled, state, 1, 1)
            gstate_ref[:, cols] = decay * gstate + dot(out_keys, scaled, 0, 0)
            gact_ref[:, cols] = gvalues + skip_ref[0:1, cols] * grads
        gact_ref[:, INNER : INNER + STATE] = gin
        gact_ref[:, INNER + STATE : CHANNELS] = gout
        gcum = rowq_ref[at, :] - colq
        gcum = gcum + jnp.where(end, jnp.sum(ends, axis=0, keepdims=True), 0.0)
        glog = running_sum(gcum, reverse=True)
        gdecay = gdecay + jnp.sum((glog * (rate * step)).reshape(CHUNK // 8, 8, LANES), axis=0)
        ratio = jnp.where(step > 0.0, sig / jnp.where(step > 0.0, step, 1.0), 0.0)
        graw = colq * ratio + rate * glog * sig
        gbias = gbias + jnp.sum(graw.reshape(CHUNK // 8, 8, LANES), axis=0)
        first = pl.multiple_of(c * CHUNK, CHUNK)
        graw_ref[at, :] = graw.astype(BF16)
        for tile in range(CHANNELS // LANES):
            cols = slice(tile * LANES, (tile + 1) * LANES)
            part = cext_ref[pl.ds(first, CHUNK + HALO), cols].astype(F32)
            moved = [pltpu.roll(part, KCONV - 1 - k, 0)[HALO:] for k in range(KCONV - 1)] + [part[HALO:]]
            out = cb_ref[0:1, cols]
            for k in range(KCONV):
                out = out + cw_ref[k : k + 1, cols] * moved[k]
            sc = jax.nn.sigmoid(out)
            gconv = gact_ref[:, cols] * (sc * (1.0 + out * (1.0 - sc)))
            gconv_ref[at, cols] = gconv
            for k in range(KCONV):
                small_ref[k : k + 1, cols] = small_ref[k : k + 1, cols] + jnp.sum(
                    gconv * moved[k], axis=0, keepdims=True
                )
            small_ref[4:5, cols] = small_ref[4:5, cols] + jnp.sum(gconv, axis=0, keepdims=True)
        return gdecay, gbias

    zero = jnp.zeros((8, LANES), F32)
    gdecay, gbias = lax.fori_loop(0, chunks, chunk, (zero, zero))
    small_ref[5:6, 0:LANES] = jnp.sum(gdecay, axis=0, keepdims=True)
    small_ref[5:6, LANES : 2 * LANES] = jnp.sum(gbias, axis=0, keepdims=True)
    head_ref[...] = gconv_ref[0:HALO, :]


def conv_back_kernel(rows, devices, scal, gconv_ref, ahead_ref, graw_ref, nh_ref, cw_ref, gproj_ref, keep_ref,
                     send_ref):
    length = gconv_ref.shape[0]
    tall = 4 * HALO
    gproj_ref[:, CHANNELS:] = graw_ref[...]

    def rows_back(first, part_of):
        for tile in range(CHANNELS // LANES):
            cols = slice(tile * LANES, (tile + 1) * LANES)
            part = part_of(cols)
            total = cw_ref[KCONV - 1 : KCONV, cols] * part[:tall]
            for k in range(KCONV - 1):
                ahead = pltpu.roll(part, part.shape[0] - (KCONV - 1 - k), 0)[:tall]
                total = total + cw_ref[k : k + 1, cols] * ahead
            gproj_ref[pl.ds(first, tall), cols] = total.astype(BF16)

    def conv_back(i, carry):
        first = pl.multiple_of(i * tall, tall)
        rows_back(first, lambda cols: gconv_ref[pl.ds(first, tall + 8), cols])
        return carry

    lax.fori_loop(0, length // tall - 1, conv_back, 0)
    rows_back(
        length - tall,
        lambda cols: jnp.concatenate([gconv_ref[length - tall :, cols], ahead_ref[0:8, cols]], axis=0),
    )
    for j in range(WIDTH // 384):
        cols = slice(j * 384, (j + 1) * 384)
        part = dot(nh_ref[HALO:, :], gproj_ref[:, cols], 0, 0).astype(BF16)
        for block in range(devices):
            put_block(
                scal[0], devices, block, keep_ref, send_ref, 0, cols, part[block * rows : (block + 1) * rows]
            )


def token_back_kernel(plan, rows, scal, gproj_ref, gng_ref, x_ref, c_ref, *refs):
    count = PIECES
    pieces = refs[:count]
    gtok_ref, w_ref, acc_ref, sem = refs[count:]
    copies = start_pieces(scal[0], pieces, plan, w_ref, sem, rows)
    length, model = c_ref.shape
    tall = 4 * HALO
    wait_all(copies)
    for j in range(2):
        cols = slice(j * model // 2, (j + 1) * model // 2)
        acc_ref[:, cols] = dot(gproj_ref[...], w_ref[cols, :], 1, 1) + gng_ref[:, cols]
    gain = gain_row(w_ref)

    def norm_back(i, carry):
        at = pl.ds(pl.multiple_of(i * tall, tall), tall)
        u = x_ref[pl.ds(pl.multiple_of(i * tall + HALO, HALO), tall), :].astype(F32)
        scale = lax.rsqrt(jnp.mean(u * u, axis=1, keepdims=True) + EPSILON)
        nh = u * scale
        g = acc_ref[at, :] * gain
        grads = scale * (g - nh * jnp.mean(g * nh, axis=1, keepdims=True))
        gtok_ref[at, :] = (grads + c_ref[at, :].astype(F32)).astype(BF16)
        return carry

    lax.fori_loop(0, length // tall, norm_back, 0)


def call(body, scal, whole, pieces, outs, scratch):
    first = [] if scal is None else [scal]
    smem = pl.BlockSpec(memory_space=pltpu.SMEM)
    vmem = pl.BlockSpec(memory_space=pltpu.VMEM)
    return list(pl.pallas_call(
        body,
        out_shape=[jax.ShapeDtypeStruct(shape, kind) for shape, kind in outs],
        in_specs=[smem] * len(first) + [vmem] * len(whole) + [pl.BlockSpec(memory_space=pl.ANY)] * len(pieces),
        out_specs=[vmem] * len(outs),
        scratch_shapes=scratch,
        compiler_params=pltpu.CompilerParams(vmem_limit_bytes=VMEM_LIMIT),
    )(*first, *whole, *pieces))


def lane_row(vector):
    return jnp.pad(vector, (0, LANES - vector.shape[0]))[None]


def per_device(tokens, lengths, dealing, cotangent, in_weight, out_weight, norm_gain, gate_gain, conv_weight,
               conv_bias, decay_log, step_bias, skip_gain):
    dp, seq = lax.axis_index("dp"), lax.axis_index("seq")
    devices, size = lax.axis_size("dp"), lax.axis_size("seq")
    group = size // 2
    lin = seq * 2 + dp % 2
    holder = lin // group
    place = {"dp": dp, "seq": seq, "micro": holder // 2, "column": holder % 2, "turn": lin % group}
    block_len, model = tokens.shape[2:]
    length = 2 * block_len
    shard_rows = in_weight.shape[0]
    rows = shard_rows * size
    tok = tokens[:, 0]
    cot = cotangent[:, 0]

    gains = jnp.concatenate(
        [norm_gain[:, None], jnp.swapaxes(gate_gain.reshape(2, shard_rows), 0, 1)], axis=1
    )
    conv_shard = jnp.concatenate([in_weight[:, INNER:], gains], axis=1)
    conv_shard = jnp.pad(conv_shard, ((0, 0), (0, WIDTH - conv_shard.shape[1])))
    rest_shard = jnp.concatenate(
        [in_weight[:, :INNER], out_weight[:shard_rows], out_weight[shard_rows:]], axis=1
    )
    masks = spread_masks(devices)
    conv_plan = (masks, [(0, 1, 0, 0, WIDTH)])
    gate_plan = (masks, [(0, 1, 0, 0, model), (rows, 1, 0, model, model)])
    out_plan = (masks, [(0, 2, model, 0, model + LANES)])

    dealt = devices == 8
    if dealt:
        routes = make_routes(place, dp_table(jnp.concatenate([dealing[:, 0], lengths[:, 0]])))
        cot_chain = Chain(cotangent_stages(core_pair(cot, place), routes, place))
        own_length = routes[4, 0]
        moving = [cot_chain]
    else:
        every = lax.all_gather(jnp.concatenate([dealing, lengths], axis=0)[:, 0], "dp", axis=0)
        goals = every[:, :2]
        source_of_out = jnp.argmax(goals == dp, axis=0)
        cot_given = deal_gathered(cot, dealing[:, 0])
        mate = lax.dynamic_index_in_dim(every, dp - dp % 2 + place["column"], 0, keepdims=False)
        own_length = jnp.where(place["micro"] == 0, mate[2], mate[3])
        moving = []

    taps = jnp.pad(conv_weight, ((0, 8 - KCONV), (0, 0)))
    skip_row = jnp.repeat(skip_gain, HDIM)[None]
    n_valid = jnp.clip(own_length - place["turn"] * length, 0, length)
    scal = jnp.stack([dp, n_valid])
    rows_of = (taps, conv_bias[None], lane_row(decay_log), lane_row(step_bias), skip_row, scal)

    shards = Chain(seq_stages(conv_shard, place))
    tok = advance(tok, shards, *moving)
    conv_z = shards.value
    conv = Chain(spread_stages(conv_z.reshape(rows, WIDTH)))
    one, two = to_stretch(tok, place)
    one, two, rows_of, rest_shard = advance((one, two, rows_of, rest_shard), conv, *moving)
    taps, conv_bias_row, decay_row, bias_row, skip_row, scal = rows_of
    first, second = swapped(place["micro"] == 1, (one, two))
    halo = lax.ppermute(second[block_len - HALO :], BOTH, neighbour_pairs(1))
    first, second, halo = advance((first, second, halo), conv, *moving)
    shards = Chain(seq_stages(rest_shard, place))
    while conv.pending is not None:
        halo = advance(halo, conv, *moving)
    x_ext = jnp.concatenate([halo, first, second])
    conv_pieces = conv.value
    gain_rows = jnp.swapaxes(conv_z[:, :, CHANNELS + HEADS + 1 : CHANNELS + HEADS + 3], 1, 2)
    gain_rows = jnp.pad(gain_rows.reshape(2 * rows, 1), ((0, 0), (0, LANES - 1)))
    moving = moving + [shards]
    def sems(plan):
        return pltpu.SemaphoreType.DMA((piece_count(plan),))

    wide = (length, INNER)
    made = call(
        functools.partial(project_kernel, conv_plan, rows),
        scal,
        [x_ext, taps, conv_bias_row, decay_row, bias_row],
        conv_pieces,
        [((length + HALO, model), BF16), ((length + HALO, CHANNELS), BF16), ((length, CHANNELS), BF16)]
        + [((length, LANES), F32)] * 3,
        [pltpu.VMEM((model, WIDTH), BF16), pltpu.VMEM((length + HALO, WIDTH), F32), sems(conv_plan)],
    )
    nh, cext, act, step, sig, cum = advance(made, *moving)
    rest_z = shards.value
    gate_z = [rest_z[:, :, n * model : (n + 1) * model].reshape(rows, model) for n in range(2)]
    out_z = jnp.concatenate([rest_z[:, :, INNER : INNER + model], rest_z[:, :, INNER + model :]], axis=1)
    out_z = out_z.reshape(2 * rows, model)
    rest = Chain(spread_stages(jnp.concatenate([jnp.concatenate(gate_z), out_z, gain_rows], axis=1)))
    moving[-1] = rest
    local, update, total = advance(
        call(
            local_kernel,
            None,
            [act, step, cum],
            [],
            [(wide, F32), ((STATE, INNER), BF16), ((8, LANES), F32)],
            [pltpu.VMEM((STATE, INNER), F32), pltpu.VMEM((2 * LANES, INNER), BF16)],
        ),
        *moving,
    )
    passing = jnp.repeat(jnp.exp(total[0, :HEADS]), HDIM)[None] if group > 2 else None

    def relay(own, pairs):
        carried = None
        for _ in range(group - 1):
            given = own if carried is None else (passing * carried.astype(F32) + own.astype(F32)).astype(BF16)
            carried = lax.ppermute(given, BOTH, pairs)
        return jnp.zeros_like(own) if carried is None else carried

    state_in = relay(update, neighbour_pairs(1))
    while rest.pending is not None:
        state_in = advance(state_in, *moving)
    if dealt:
        while cot_chain.pending is not None:
            advance((), cot_chain)
        c_own = cot_chain.value
    else:
        c_own = jnp.concatenate(swapped(place["micro"] == 1, to_stretch(cot_given, place)))
    rest_pieces = rest.value

    out, gn, dgate, gcore, rowq, lsg, states, gskip = call(
        functools.partial(middle_kernel, gate_plan, out_plan, rows),
        scal,
        [local, act, step, cum, nh, state_in, x_ext, c_own, skip_row],
        rest_pieces,
        [((length, model), BF16), (wide, BF16), (wide, BF16), (wide, BF16), ((length, LANES), F32),
         ((STATE, INNER), BF16), ((length // CHUNK, STATE, INNER), BF16), ((8, INNER), F32)],
        [pltpu.VMEM((INNER, model + LANES), BF16), pltpu.VMEM((model, INNER), BF16), pltpu.VMEM(wide, F32),
         pltpu.VMEM((8, INNER), F32), pltpu.VMEM((length, model), BF16), pltpu.VMEM(wide, F32),
         pltpu.VMEM((STATE, INNER), F32), pltpu.VMEM((3 * CHUNK + 8, INNER), F32),
         pltpu.VMEM((CHUNK, INNER), F32), pltpu.VMEM((CHUNK, INNER), F32), pltpu.VMEM((STATE, INNER), F32),
         pltpu.VMEM((2 * LANES, INNER), BF16), sems(gate_plan), sems(out_plan)],
    )
    if dealt:
        moving = [Chain(output_stages(out, routes, place))]
        out_chain = moving[0]
    else:
        moving = []
        blocks = jnp.stack(swapped(place["seq"] % 2 == 1, from_stretch(out[:block_len], out[block_len:], place)))
        outputs = deal_gathered(blocks, source_of_out)
    grad_out_state = relay(lsg, neighbour_pairs(-1))

    half_dp = devices // 2
    keep1, send1, gcore, dgate = advance(
        call(
            functools.partial(early_kernel, rows, devices),
            scal,
            [gn, c_own, nh, dgate],
            [],
            [((half_dp, 4 * rows, model), BF16)] * 2,
            [pltpu.VMEM((length, model), BF16)],
        )
        + [gcore, dgate],
        *moving,
    )

    def early_take(part, index):
        gates = part[: 2 * rows].reshape(2, size, shard_rows, model)
        gates = lax.dynamic_index_in_dim(gates, index, 1, keepdims=False).reshape(2 * shard_rows, model)
        outs = part[2 * rows :].reshape(size, 2 * shard_rows, model)
        return jnp.concatenate([gates, lax.dynamic_index_in_dim(outs, index, 0, keepdims=False)])

    early = Chain(reduce_stages(keep1, send1, place, early_take))
    moving.append(early)
    made = call(
        functools.partial(local_back_kernel, gate_plan, rows),
        scal,
        [act, step, cum, gcore, dgate],
        rest_pieces,
        [(wide, F32), ((length, 2 * STATE), F32), ((length, model), F32)],
        [pltpu.VMEM((model, INNER), BF16), sems(gate_plan)],
    )
    gvl, gk, gng, grad_out_state = advance(made + [grad_out_state], *moving)
    gconv, head, graw, small = advance(
        call(
            scan_back_kernel,
            None,
            [act, step, sig, cum, gcore, gvl, gk, rowq, states, grad_out_state, gskip, skip_row, cext, taps,
             conv_bias_row, decay_row],
            [],
            [((length, CHANNELS), F32), ((HALO, CHANNELS), F32), ((length, LANES), BF16), ((8, WIDTH), F32)],
            [pltpu.VMEM((STATE, INNER), F32), pltpu.VMEM((2 * CHUNK + 8, INNER), F32),
             pltpu.VMEM((CHUNK, CHANNELS), F32), pltpu.VMEM((2 * LANES, INNER), BF16)],
        ),
        *moving,
    )
    ahead = lax.ppermute(head, BOTH, neighbour_pairs(-1))
    sums = Chain(sum_stages(small))
    moving.append(sums)
    gproj, keep2, send2 = advance(
        call(
            functools.partial(conv_back_kernel, rows, devices),
            scal,
            [gconv, ahead, graw, nh, taps],
            [],
            [((length, WIDTH), BF16)] + [((half_dp, rows, WIDTH), BF16)] * 2,
            [],
        ),
        *moving,
    )

    def late_take(part, index):
        return lax.dynamic_index_in_dim(part.reshape(size, shard_rows, WIDTH), index, 0, keepdims=False)

    final = Chain(reduce_stages(keep2, send2, place, late_take))
    moving.append(final)
    (gtok,) = advance(
        call(
            functools.partial(token_back_kernel, conv_plan, rows),
            scal,
            [gproj, gng, x_ext, c_own],
            conv_pieces,
            [((length, model), BF16)],
            [pltpu.VMEM((model, WIDTH), BF16), pltpu.VMEM((length, model), F32), sems(conv_plan)],
        ),
        *moving,
    )

    one, two = from_stretch(gtok[:block_len], gtok[block_len:], place)
    one = advance(one, *moving)
    back = one, advance(two, *moving)
    while any(chain.pending is not None for chain in moving):
        advance((), *moving)
    grad_tokens = jnp.stack(swapped(place["seq"] % 2 == 1, back))
    if dealt:
        outputs = out_chain.value

    early_sum, late_sum, sums = early.value, final.value, sums.value
    raw_in = jnp.concatenate(
        [early_sum[:shard_rows], early_sum[shard_rows : 2 * shard_rows],
         late_sum[:, : in_weight.shape[1] - INNER]], axis=1
    )
    raw_out = early_sum[2 * shard_rows :]
    grad_norm_gain = jnp.sum(raw_in * in_weight.astype(F32), axis=1) / norm_gain.astype(F32)
    grad_gate_gain = jnp.sum(raw_out * out_weight.astype(F32), axis=1) / gate_gain.astype(F32)
    grad_skip = jnp.sum(sums[6, :INNER].reshape(HEADS, HDIM), axis=1)
    return (
        outputs[:, None],
        grad_tokens[:, None],
        raw_in,
        raw_out,
        grad_norm_gain,
        grad_gate_gain,
        sums[0:KCONV, :CHANNELS],
        sums[4, :CHANNELS],
        sums[5, :HEADS],
        sums[5, LANES : LANES + HEADS],
        grad_skip,
    )


def solution(mesh):
    in_specs = (
        P(None, "dp", "seq", None),
        P(None, "dp"),
        P(None, "dp"),
        P(None, "dp", "seq", None),
        P(BOTH, None),
        P(BOTH, None),
        P(BOTH),
        P(BOTH),
        P(),
        P(),
        P(),
        P(),
        P(),
    )
    out_specs = (
        P(None, "dp", "seq", None),
        P(None, "dp", "seq", None),
        P(BOTH, None),
        P(BOTH, None),
        P(BOTH),
        P(BOTH),
        P(),
        P(),
        P(),
        P(),
        P(),
    )
    return jax.shard_map(per_device, mesh=mesh, in_specs=in_specs, out_specs=out_specs, check_vma=False)
```

```python
import functools

import jax
import jax.numpy as jnp
from jax import lax
from jax.experimental import pallas as pl
from jax.experimental.pallas import tpu as pltpu
from jax.sharding import PartitionSpec as P

INNER = 1536
HEADS = 24
HDIM = 64
STATE = 128
KCONV = 4
CHANNELS = INNER + 2 * STATE
LANES = 128
CHUNK = 128
HALO = 16
PIECES = 4
EPSILON = 1e-05
WIDTH = CHANNELS + LANES
F32 = jnp.float32
BF16 = jnp.bfloat16
BOTH = ("dp", "seq")
VMEM_LIMIT = 60 * 1024 * 1024


def flip_dp(value, mask):
    pairs = [(i, i ^ mask) for i in range(lax.axis_size("dp"))]
    return lax.ppermute(value, "dp", pairs)


def step_bits(size):
    return list(range(1, size.bit_length() - 1))


def flip_step(value, step):
    size = lax.axis_size("dp")
    bits = step_bits(size)
    pairs = [(i, i ^ (1 << (bits[-1 - step] if i % 2 else bits[step]))) for i in range(size)]
    return lax.ppermute(value, "dp", pairs)


def shift_seq(value, step):
    size = lax.axis_size("seq")
    return lax.ppermute(value, "seq", [(i, (i + step) % size) for i in range(size)])


def column_place(dp_even, lin):
    return (dp_even + lin % 2) * lax.axis_size("seq") + lin // 2


def unit_pairs(parity):
    size = lax.axis_size("seq")
    pairs = []
    for dp in range(lax.axis_size("dp")):
        core = dp % 2
        for block in range(size):
            micro = (block % 2) ^ parity
            lin = (2 * micro + core) * (size // 2) + block // 2
            pairs.append((dp * size + block, column_place(dp - core, lin)))
    return pairs


def neighbour_pairs(step):
    size = lax.axis_size("seq")
    group = size // 2
    pairs = []
    for dp_even in range(0, lax.axis_size("dp"), 2):
        for lin in range(2 * size):
            if 0 <= lin % group + step < group:
                pairs.append((column_place(dp_even, lin), column_place(dp_even, lin + step)))
    return pairs


def reversed_pairs(pairs):
    return [(target, source) for source, target in pairs]


def to_stretch(blocks, place):
    return send_stretch(swapped(place["seq"] % 2 == 1, blocks))


def send_stretch(pair):
    return tuple(lax.ppermute(pair[n], BOTH, unit_pairs(n)) for n in range(2))


def swapped(swap, pair):
    return jnp.where(swap, pair[1], pair[0]), jnp.where(swap, pair[0], pair[1])


def from_stretch(first, second, place):
    late = place["micro"] == 1
    one = lax.ppermute(jnp.where(late, second, first), BOTH, reversed_pairs(unit_pairs(0)))
    two = lax.ppermute(jnp.where(late, first, second), BOTH, reversed_pairs(unit_pairs(1)))
    return one, two


class Chain:
    def __init__(self, stages):
        self.stages = stages
        self.value = None
        self.pending = next(stages)

    def feed(self, arrived):
        try:
            self.pending = self.stages.send(arrived)
        except StopIteration as stop:
            self.pending = None
            self.value = stop.value


def advance(held, *chains):
    moving = [chain for chain in chains if chain.pending is not None]
    held, arrived = lax.optimization_barrier((held, [chain.pending for chain in moving]))
    for chain, got in zip(moving, arrived):
        chain.feed(got)
    return held


def seq_shifts(shard):
    return [shift_seq(shard, j) for j in range(1, lax.axis_size("seq"))]


def seq_order(shard, arrived, place):
    size = lax.axis_size("seq")
    got = [shard] + list(arrived)
    rows = []
    for i in range(size):
        row = got[0]
        for j in range(1, size):
            row = jnp.where((place["seq"] - i) % size == j, got[j], row)
        rows.append(row)
    return jnp.stack(rows)


def seq_stages(shard, place):
    arrived = yield seq_shifts(shard)
    return seq_order(shard, arrived, place)


def spread_stages(block):
    steps = len(step_bits(lax.axis_size("dp")))
    held, last, turned = block[None], None, None
    for step in range(steps):
        if last is not None:
            held = jnp.concatenate([held, last])
        if step < steps - 1:
            last = (yield [flip_step(held, step)])[0]
        else:
            last, turned = yield [flip_step(held, step), flip_dp(held, 1)]
    end = (yield [flip_dp(last, 1)])[0]
    return [held, last, turned, end]


def spread_masks(size):
    found = []
    for bits in (step_bits(size), step_bits(size)[::-1]):
        masks, last = (0,), None
        for bit in bits:
            if last is not None:
                masks = masks + last
            last = tuple(m ^ (1 << bit) for m in masks)
        found.append((masks, last))
    even, odd = found
    own = [(even[n], odd[n]) for n in range(2)]
    return own + [(tuple(m ^ 1 for m in b), tuple(m ^ 1 for m in a)) for a, b in own]


def reduce_stages(keep, send, place, segments):
    steps = len(step_bits(lax.axis_size("dp")))
    parts = [keep] + (yield [flip_dp(send, 1)])
    for step in range(steps):
        first = 1 << (steps - 1 - step)
        parts = parts + (yield [flip_step(give_up(parts, first), step)])
    gives = take_rows(parts, segments, place)
    moved = yield [shift_seq(gives[j], j) for j in range(1, lax.axis_size("seq"))]
    return add_up([gives[0]] + moved)


def row_loop(rows, body):
    tall = 32 if rows % 32 == 0 else rows

    def step(i, carry):
        body(pl.ds(pl.multiple_of(i * tall, tall), tall))
        return carry

    lax.fori_loop(0, rows // tall, step, 0)


def give_kernel(*refs):
    *parts, out_ref = refs

    def some(at):
        out_ref[0, at, :] = add_up([part[0, at, :] for part in parts]).astype(BF16)

    row_loop(out_ref.shape[1], some)


def give_up(parts, first):
    rows, cols = parts[0].shape[1:]
    return pl.pallas_call(
        give_kernel,
        grid=(first,),
        out_shape=jax.ShapeDtypeStruct((first, rows, cols), BF16),
        in_specs=[pl.BlockSpec((1, rows, cols), lambda n: (first + n, 0, 0))] * len(parts),
        out_specs=pl.BlockSpec((1, rows, cols), lambda n: (n, 0, 0)),
    )(*parts)


def take_kernel(size, segments, seq_ref, *refs):
    parts = refs[: len(refs) - size - 1]
    own_ref, *out_refs = refs[len(parts) : -1]
    total_ref = refs[-1]

    def some(at):
        total_ref[at, :] = add_up([part[0, at, :] for part in parts])

    row_loop(total_ref.shape[0], some)
    for j in range(size):
        index = (seq_ref[0] + j) % size
        start = 0
        for first, rows in segments:
            found = total_ref[pl.ds(pl.multiple_of(first + index * rows, 8), rows), :]
            if j == 0:
                own_ref[start : start + rows, :] = found
            else:
                out_refs[j - 1][start : start + rows, :] = found.astype(BF16)
            start += rows


def take_rows(parts, segments, place):
    size = lax.axis_size("seq")
    rows, cols = parts[0].shape[1:]
    taken = sum(count for _, count in segments)
    if any(first % 8 or count % 8 for first, count in segments):
        total = add_up([part[0] for part in parts])
        gives = []
        for j in range(size):
            index = (place["seq"] + j) % size
            found = [lax.dynamic_slice_in_dim(total, f + index * count, count) for f, count in segments]
            gives.append(jnp.concatenate(found).astype(BF16 if j else F32))
        return gives
    return pl.pallas_call(
        functools.partial(take_kernel, size, segments),
        grid=(1,),
        out_shape=[jax.ShapeDtypeStruct((taken, cols), BF16 if j else F32) for j in range(size)],
        in_specs=[pl.BlockSpec(memory_space=pltpu.SMEM)]
        + [pl.BlockSpec((1, rows, cols), lambda n: (0, 0, 0))] * len(parts),
        out_specs=[pl.BlockSpec((taken, cols), lambda n: (0, 0))] * size,
        scratch_shapes=[pltpu.VMEM((rows, cols), F32)],
    )(place["seq"][None], *parts)


def add_up(parts):
    total = parts[0].astype(F32)
    for part in parts[1:]:
        total = total + part.astype(F32)
    return total


def sum_stages(value):
    value = value + flip_dp(value, 1)
    size = lax.axis_size("seq")
    apart = 1
    while apart < size:
        got = yield [lax.ppermute(value, "seq", [(i, i ^ apart) for i in range(size)])]
        value = value + got[0]
        apart *= 2
    for bit in range(1, lax.axis_size("dp").bit_length() - 1):
        got = yield [flip_dp(value, 1 << bit)]
        value = value + got[0]
    return value


def dp_table(row):
    table = row[None]
    for bit in range(lax.axis_size("dp").bit_length() - 1):
        table = jnp.concatenate([table, flip_dp(table, 1 << bit)])
    return table


def route_row(dp, goal, first_bit, second_bit):
    held = [0, 1, first_bit, first_bit | 1]

    def chosen(base):
        low = jnp.int32(0)
        high = jnp.int32(0)
        for n in range(3, -1, -1):
            away = jnp.bitwise_xor(goal[base ^ held[n]], jnp.bitwise_xor(dp, base))
            cross = (jnp.bitwise_and(away, second_bit) != 0) & (jnp.bitwise_and(away, first_bit) == 0)
            low = jnp.where(cross, n, low)
        for n in range(4):
            away = jnp.bitwise_xor(goal[base ^ held[n]], jnp.bitwise_xor(dp, base))
            cross = (jnp.bitwise_and(away, second_bit) != 0) & (jnp.bitwise_and(away, first_bit) == 0)
            high = jnp.where(cross, n, high)
        return low, high

    low, high = chosen(0)
    other_low, _ = chosen(second_bit)
    row = [low, high]
    for side in range(2):
        pick = jnp.int32(0)
        target = jnp.bitwise_xor(dp, side)
        for n in range(4):
            pick = jnp.where(goal[held[n]] == target, n, pick)
            far = jnp.where(other_low == n, 4, 5)
            pick = jnp.where(goal[held[n] ^ second_bit] == target, far, pick)
        row.append(pick)
    return row


def route_kernel(place_ref, table_ref, out_ref):
    dp = place_ref[0]
    size = table_ref.shape[0]
    for way in range(2):
        for micro in range(2):
            goal = []
            for r in range(size):
                if way == 1:
                    goal.append(table_ref[r, micro])
                else:
                    found = jnp.int32(0)
                    for other in range(size):
                        hit = table_ref[other, micro] == jnp.bitwise_xor(dp, r)
                        found = jnp.where(hit, jnp.bitwise_xor(dp, other), found)
                    goal.append(found)
            even = route_row(dp, goal, 2, 4)
            odd = route_row(dp, goal, 4, 2)
            for n in range(4):
                out_ref[way * 2 + micro, n] = jnp.where(jnp.bitwise_and(dp, 1) == 0, even[n], odd[n])
    core = jnp.bitwise_and(dp, 1)
    column = jnp.bitwise_xor(core, place_ref[2])
    micro = place_ref[1]
    own = jnp.where(micro == 0, table_ref[0, 2], table_ref[0, 3])
    other = jnp.where(micro == 0, table_ref[1, 2], table_ref[1, 3])
    out_ref[4, 0] = jnp.where(column == 0, own, other)
    out_ref[4, 1] = place_ref[3]
    for n in range(2, 4):
        out_ref[4, n] = jnp.int32(0)


def make_routes(place, table):
    return pl.pallas_call(
        route_kernel,
        out_shape=jax.ShapeDtypeStruct((5, 4), jnp.int32),
        in_specs=[pl.BlockSpec(memory_space=pltpu.SMEM)] * 2,
        out_specs=pl.BlockSpec(memory_space=pltpu.SMEM),
    )(jnp.stack([place["dp"], place["micro"], place["column"], place["seq"] % 2]), table)


def pick_entries(index, entries, out, also=True):
    for n, entry in enumerate(entries):

        @pl.when((index == n) & also)
        def _():
            out[...] = entry[...]


def entries_of(micro, refs):
    return [ref.at[micro, n] for ref in refs for n in range(2)]


def pick_sent_kernel(first, route_ref, pair_ref, came_ref, sent_ref):
    for micro in range(2):
        for k in range(2):
            entries = entries_of(micro, (pair_ref, came_ref))
            pick_entries(route_ref[first + micro, k], entries, sent_ref.at[micro, k])


def pick_last_kernel(first, route_ref, pair_ref, came_ref, far_ref, own_ref, partner_ref):
    for micro in range(2):
        entries = entries_of(micro, (pair_ref, came_ref, far_ref))
        for k, out_ref in enumerate((own_ref, partner_ref)):
            pick_entries(route_ref[first + micro, 2 + k], entries, out_ref.at[micro])


def pick(body, routes, shapes, *held):
    vmem = pl.BlockSpec(memory_space=pltpu.VMEM)
    return pl.pallas_call(
        body,
        out_shape=[jax.ShapeDtypeStruct(shape, BF16) for shape in shapes],
        in_specs=[pl.BlockSpec(memory_space=pltpu.SMEM)] + [vmem] * len(held),
        out_specs=[vmem] * len(shapes),
    )(routes, *held)


def core_pair(items, place):
    low_core = place["dp"] % 2 == 0
    half = items.shape[1] // 2
    mine, give = swapped(jnp.logical_not(low_core), (items[:, :half], items[:, half:]))
    return jnp.stack([mine, flip_dp(give, 1)], axis=1)


def cotangent_stages(pair, routes, place):
    low_core = place["dp"] % 2 == 0
    pair = (yield [pair])[0]
    came = (yield [flip_step(pair, 0)])[0]
    (sent,) = yield pick(functools.partial(pick_sent_kernel, 0), routes, [pair.shape], pair, came)
    far = flip_step(sent, 1)
    yield []
    far = (yield [far])[0]
    body = functools.partial(pick_last_kernel, 0)
    own, partner = pick(body, routes, [pair[:, 0].shape] * 2, pair, came, far)
    blocks = jnp.concatenate(swapped(jnp.logical_not(low_core), (own, flip_dp(partner, 1))), axis=1)
    one, two = to_stretch(blocks, place)
    one = (yield [one])[0]
    two = (yield [two])[0]
    return one, two


def output_stages(out, routes, place):
    block = out.shape[0] // 2
    one, two = from_stretch(out[:block], out[block:], place)
    one = (yield [one])[0]
    two = (yield [two])[0]
    blocks = jnp.stack(swapped(place["seq"] % 2 == 1, (one, two)))
    tops, bottoms = blocks[:, : block // 2], blocks[:, block // 2 :]
    mine, give = swapped(place["dp"] % 2 == 1, (tops, bottoms))
    got = (yield [flip_dp(give, 1)])[0]
    pair = jnp.stack([mine, got], axis=1)
    came = (yield [flip_step(pair, 0)])[0]
    (sent,) = pick(functools.partial(pick_sent_kernel, 2), routes, [pair.shape], pair, came)
    far = (yield [flip_step(sent, 1)])[0]
    body = functools.partial(pick_last_kernel, 2)
    own, partner = pick(body, routes, [mine.shape] * 2, pair, came, far)
    back = (yield [flip_dp(partner, 1)])[0]
    return jnp.concatenate(swapped(place["dp"] % 2 == 1, (own, back)), axis=1)


def deal_gathered(items, source):
    every = lax.all_gather(items, "dp", axis=0)
    picked = [
        lax.dynamic_index_in_dim(every[:, m], source[m], 0, keepdims=False) for m in range(2)
    ]
    return jnp.stack(picked)


def dot(a, b, ca=1, cb=0):
    return lax.dot_general(a, b, (((ca,), (cb,)), ((), ())), preferred_element_type=F32)


def two_parts(x):
    high = x.astype(BF16)
    return high, (x - high.astype(F32)).astype(BF16)


def running_sum(x, reverse=False):
    rows = lax.broadcasted_iota(jnp.int32, (CHUNK, CHUNK), 0)
    cols = lax.broadcasted_iota(jnp.int32, (CHUNK, CHUNK), 1)
    reach = (rows <= cols) if reverse else (rows >= cols)
    reach = jnp.where(reach, 1.0, 0.0).astype(BF16)
    high, rest = two_parts(x)
    middle, low = two_parts(x - high.astype(F32))
    del rest
    return dot(reach, high) + dot(reach, middle) + dot(reach, low)


def fill_expander(expand_ref):
    head = lax.broadcasted_iota(jnp.int32, (LANES, INNER), 0)
    col = lax.broadcasted_iota(jnp.int32, (LANES, INNER), 1)
    one = jnp.where(col // HDIM == head, 1.0, 0.0).astype(BF16)
    expand_ref[0:LANES, :] = one
    expand_ref[LANES : 2 * LANES, :] = one


def head_sums(prod, tile):
    lane = lax.broadcasted_iota(jnp.int32, (LANES, LANES), 0)
    head = lax.broadcasted_iota(jnp.int32, (LANES, LANES), 1)
    one = jnp.where(2 * tile + lane // HDIM == head, 1.0, 0.0).astype(BF16)
    high, low = two_parts(prod)
    return dot(jnp.concatenate([high, low], axis=1), jnp.concatenate([one, one], axis=0))


def start_pieces(dp, pieces, plan, target, sem, rows):
    copies = []
    masks, spots = plan
    for piece, (even, odd) in zip(pieces, masks):
        for n in range(len(even)):
            mask = jnp.where(jnp.bitwise_and(dp, 1) == 0, even[n], odd[n])
            for source, scale, source_col, col, width in spots:
                first = pl.multiple_of(jnp.bitwise_xor(dp, mask) * (rows * scale), 8)
                copy = pltpu.make_async_copy(
                    piece.at[n, pl.ds(source, rows * scale), pl.ds(source_col, width)],
                    target.at[pl.ds(first, rows * scale), pl.ds(col, width)],
                    sem.at[len(copies)],
                )
                copy.start()
                copies.append(copy)
    return copies


def wait_all(copies):
    for copy in copies:
        copy.wait()


def piece_count(plan):
    masks, spots = plan
    return sum(len(even) for even, _ in masks) * len(spots)


def gain_row(w_ref):
    return w_ref[:, CHANNELS:].astype(F32).T[HEADS : HEADS + 1]


def join_blocks(late, one_ref, two_ref, out_ref, start):
    rows = one_ref.shape[0]
    for turn, pair in enumerate(((one_ref, two_ref), (two_ref, one_ref))):

        @pl.when(late == turn)
        def _():
            for n, block_ref in enumerate(pair):
                out_ref[start + n * rows : start + (n + 1) * rows, :] = block_ref[...]


def project_kernel(plan, rows, scal, one_ref, two_ref, halo_ref, cw_ref, cb_ref, dl_ref, sb_ref, *refs):
    count = PIECES
    pieces = refs[:count]
    x_ref, nh_ref, cext_ref, act_ref, step_ref, sig_ref, cum_ref = refs[count : count + 7]
    w_ref, proj_ref, sem = refs[count + 7 :]
    copies = start_pieces(scal[0], pieces, plan, w_ref, sem, rows)
    total = x_ref.shape[0]
    length = total - HALO
    x_ref[0:HALO, :] = halo_ref[...]
    join_blocks(scal[2], one_ref, two_ref, x_ref, HALO)
    chunks = length // CHUNK

    tall = 3 * HALO if total % (3 * HALO) == 0 else HALO

    def norm(i, carry):
        at = pl.ds(pl.multiple_of(i * tall, tall), tall)
        u = x_ref[at, :].astype(F32)
        scale = lax.rsqrt(jnp.mean(u * u, axis=1, keepdims=True) + EPSILON)
        nh_ref[at, :] = (u * scale * gain).astype(BF16)
        return carry

    wait_all(copies)
    gain = gain_row(w_ref)
    lax.fori_loop(0, total // tall, norm, 0)

    def project(j, carry):
        at = pl.ds(pl.multiple_of(j * 384, 384), 384)
        proj_ref[:, at] = dot(nh_ref[...], w_ref[:, at])
        return carry

    lax.fori_loop(0, WIDTH // 384, project, 0)

    def conv(idx, carry):
        i, j = idx // (CHANNELS // LANES), idx % (CHANNELS // LANES)
        cols = pl.ds(pl.multiple_of(j * LANES, LANES), LANES)
        first = pl.multiple_of(i * CHUNK, CHUNK)
        part = proj_ref[pl.ds(first, CHUNK + HALO), cols]
        weights = cw_ref[:, cols]
        out = cb_ref[0:1, cols] + weights[KCONV - 1 : KCONV] * part[HALO:]
        for k in range(KCONV - 1):
            out = out + weights[k : k + 1] * pltpu.roll(part, KCONV - 1 - k, 0)[HALO:]
        act_ref[pl.ds(first, CHUNK), cols] = (out * jax.nn.sigmoid(out)).astype(BF16)
        cext_ref[pl.ds(first + HALO, CHUNK), cols] = part[HALO:].astype(BF16)
        return carry

    lax.fori_loop(0, chunks * (CHANNELS // LANES), conv, 0)
    cext_ref[0:HALO, :] = proj_ref[0:HALO, 0:CHANNELS].astype(BF16)
    lane = lax.broadcasted_iota(jnp.int32, (CHUNK, LANES), 1)
    row = lax.broadcasted_iota(jnp.int32, (CHUNK, LANES), 0)
    rate = -jnp.exp(dl_ref[0:1, :])
    for i in range(chunks):
        at = pl.ds(i * CHUNK, CHUNK)
        pre = proj_ref[pl.ds(HALO + i * CHUNK, CHUNK), pl.ds(CHANNELS, LANES)] + sb_ref[0:1, :]
        live = (row + i * CHUNK < scal[1]) & (lane < HEADS)
        soft = jnp.maximum(pre, 0.0) + jnp.log1p(jnp.exp(-jnp.abs(pre)))
        step = jnp.where(live, soft, 0.0)
        step_ref[at, :] = step
        sig_ref[at, :] = jnp.where(live, jax.nn.sigmoid(pre), 0.0)
        cum_ref[at, :] = running_sum(rate * step)


def mixing_parts(cum, cum_rows, step_rows, head):
    gap = jnp.minimum(cum[:, head : head + 1] - cum_rows[head : head + 1, :], 0.0)
    return jnp.exp(gap) * step_rows[head : head + 1, :]


def causal_tile():
    rows = lax.broadcasted_iota(jnp.int32, (CHUNK, CHUNK), 0)
    cols = lax.broadcasted_iota(jnp.int32, (CHUNK, CHUNK), 1)
    return rows >= cols


def local_kernel(act_ref, step_ref, cum_ref, local_ref, upd_ref, tot_ref, sum_ref, expand_ref):
    chunks = act_ref.shape[0] // CHUNK
    left = lax.broadcasted_iota(jnp.int32, (CHUNK, LANES), 1) < HDIM
    fill_expander(expand_ref)
    after = jnp.zeros((1, LANES), F32)
    for i in range(chunks - 1, -1, -1):
        at = pl.ds(i * CHUNK, CHUNK)
        cum = cum_ref[at, :]
        last = cum[CHUNK - 1 : CHUNK]
        weight = jnp.exp(last + after - cum) * step_ref[at, :]
        wide = dot(jnp.concatenate(two_parts(weight), axis=1), expand_ref[...])
        values = act_ref[at, 0:INNER].astype(F32)
        keys = act_ref[at, INNER : INNER + STATE]
        update = dot(keys, (wide * values).astype(BF16), 0, 0)
        sum_ref[...] = update if i == chunks - 1 else sum_ref[...] + update
        after = after + last
    upd_ref[...] = sum_ref[...].astype(BF16)
    tot_ref[...] = jnp.broadcast_to(after, tot_ref.shape)

    def chunk(c, carry):
        at = pl.ds(pl.multiple_of(c * CHUNK, CHUNK), CHUNK)
        in_keys = act_ref[at, INNER : INNER + STATE]
        out_keys = act_ref[at, INNER + STATE : CHANNELS]
        affinity = jnp.where(causal_tile(), dot(out_keys, in_keys, 1, 1), 0.0)
        cum = cum_ref[at, :]
        cum_rows = cum.T
        step_rows = step_ref[at, :].T
        for tile in range(INNER // LANES):
            cols = slice(tile * LANES, (tile + 1) * LANES)
            mixing = [
                (affinity * mixing_parts(cum, cum_rows, step_rows, 2 * tile + n)).astype(BF16)
                for n in range(2)
            ]
            values = act_ref[at, cols]
            zero = jnp.zeros_like(values)
            apart = jnp.concatenate(
                [jnp.where(left, values, zero), jnp.where(left, zero, values)], axis=0
            )
            local_ref[at, cols] = dot(jnp.concatenate(mixing, axis=1), apart)
        return carry

    lax.fori_loop(0, chunks, chunk, 0)


def core_kernel(local_ref, act_ref, step_ref, cum_ref, state_ref, core_ref, states_ref, state_s, wide_ref, expand_ref):
    chunks = act_ref.shape[0] // CHUNK
    fill_expander(expand_ref)
    state_s[...] = state_ref[...].astype(F32)

    def chunk(c, carry):
        at = pl.ds(pl.multiple_of(c * CHUNK, CHUNK), CHUNK)
        in_keys = act_ref[at, INNER : INNER + STATE]
        out_keys = act_ref[at, INNER + STATE : CHANNELS]
        cum = cum_ref[at, :]
        last = cum[CHUNK - 1 : CHUNK]
        weight = jnp.exp(last - cum) * step_ref[at, :]
        small = jnp.concatenate([jnp.exp(cum), weight, jnp.broadcast_to(jnp.exp(last), (8, LANES))], axis=0)
        wide_ref[...] = dot(jnp.concatenate(two_parts(small), axis=1), expand_ref[...])
        state_b = state_s[...].astype(BF16)
        states_ref[c] = state_b
        for tile in range(INNER // LANES):
            cols = slice(tile * LANES, (tile + 1) * LANES)
            values = act_ref[at, cols].astype(F32)
            core_ref[at, cols] = local_ref[at, cols] + wide_ref[0:CHUNK, cols] * dot(out_keys, state_b[:, cols])
            weighted = (wide_ref[CHUNK : 2 * CHUNK, cols] * values).astype(BF16)
            state_s[:, cols] = wide_ref[2 * CHUNK : 2 * CHUNK + 1, cols] * state_s[:, cols] + dot(
                in_keys, weighted, 0, 0
            )
        return carry

    lax.fori_loop(0, chunks, chunk, 0)


def middle_kernel(gate_plan, plan, rows, scal, core_ref, act_ref, cum_ref, nh_ref, x_ref, one_ref, two_ref, skip_ref,
                  *refs):
    count = PIECES
    c_ref, out_ref, gn_ref, dgate_ref, gcore_ref, rowq_ref, lsg_ref, gskip_ref = refs[count : count + 8]
    (w_ref, wg_ref, gate_ref, gain_ref, mc_ref, gno_ref, wide_ref, mixed_ref, sig_ref, gated_ref, acc_ref, expand_ref, gate_sem,
     sem) = refs[count + 8 :]
    gate_copies = start_pieces(scal[0], refs[:count], gate_plan, wg_ref, gate_sem, rows)
    copies = start_pieces(scal[0], refs[:count], plan, w_ref, sem, rows)
    length = act_ref.shape[0]
    chunks = length // CHUNK
    tiles = INNER // LANES
    model = c_ref.shape[1]
    join_blocks(scal[2], one_ref, two_ref, c_ref, 0)
    fill_expander(expand_ref)

    def mask(i, carry):
        at = pl.ds(pl.multiple_of(i * CHUNK, CHUNK), CHUNK)
        row = lax.broadcasted_iota(jnp.int32, (CHUNK, model), 0) + i * CHUNK
        c = c_ref[at, :]
        mc_ref[at, :] = jnp.where(row < scal[1], c.astype(F32), 0.0).astype(BF16)
        return carry

    lax.fori_loop(0, chunks, mask, 0)
    wait_all(gate_copies)

    def project(j, carry):
        at = pl.ds(pl.multiple_of(j * 384, 384), 384)
        gate_ref[:, at] = dot(nh_ref[HALO:, :], wg_ref[:, at])
        return carry

    lax.fori_loop(0, INNER // 384, project, 0)
    wait_all(copies)

    def back_project(j, carry):
        at = pl.ds(pl.multiple_of(j * 384, 384), 384)
        gno_ref[:, at] = dot(mc_ref[...], w_ref[at, 0:model], 1, 1)
        return carry

    lax.fori_loop(0, INNER // 384, back_project, 0)
    gain_ref[...] = w_ref[:, model:].astype(F32).T[0:8]
    acc_ref[...] = jnp.zeros_like(acc_ref)
    gskip_ref[...] = jnp.zeros_like(gskip_ref)

    def chunk(c, before):
        at = pl.ds(pl.multiple_of(c * CHUNK, CHUNK), CHUNK)
        out_keys = act_ref[at, INNER + STATE : CHANNELS]
        cum = cum_ref[at, :]
        wide_ref[...] = dot(jnp.concatenate(two_parts(jnp.exp(cum + before)), axis=1), expand_ref[...])
        squares = jnp.zeros((CHUNK, LANES), F32)
        for tile in range(tiles):
            cols = slice(tile * LANES, (tile + 1) * LANES)
            mixed = core_ref[at, cols] + skip_ref[0:1, cols] * act_ref[at, cols].astype(F32)
            mixed_ref[:, cols] = mixed
            gate = gate_ref[at, cols]
            sig = jax.nn.sigmoid(gate)
            gated = mixed * (gate * sig)
            sig_ref[:, cols] = sig
            gated_ref[:, cols] = gated
            squares = squares + gated * gated
        scale = lax.rsqrt(jnp.sum(squares, axis=1, keepdims=True) / INNER + EPSILON)
        products = jnp.zeros((CHUNK, LANES), F32)
        for tile in range(tiles):
            cols = slice(tile * LANES, (tile + 1) * LANES)
            gn = gated_ref[:, cols] * scale
            gain = gain_ref[0:1, cols]
            gn_ref[at, cols] = (gn * gain).astype(BF16)
            products = products + gn * (gno_ref[at, cols] * gain)
        mean = jnp.sum(products, axis=1, keepdims=True) / INNER
        rowq = jnp.zeros((CHUNK, LANES), F32)
        for tile in range(tiles):
            cols = slice(tile * LANES, (tile + 1) * LANES)
            gate = gate_ref[at, cols]
            sig = sig_ref[:, cols]
            silu = gate * sig
            mixed = mixed_ref[:, cols]
            dgated = scale * (gno_ref[at, cols] * gain_ref[0:1, cols] - (gated_ref[:, cols] * scale) * mean)
            g = dgated * silu
            dgate_ref[at, cols] = (dgated * mixed * (sig * (1.0 + gate * (1.0 - sig)))).astype(BF16)
            gcore = g.astype(BF16)
            gcore_ref[at, cols] = gcore
            values = act_ref[at, cols].astype(F32)
            gskip_ref[:, cols] = gskip_ref[:, cols] + jnp.sum(
                (g * values).reshape(CHUNK // 8, 8, LANES), axis=0
            )
            gcore_f = gcore.astype(F32)
            rowq = rowq + head_sums(gcore_f * core_ref[at, cols], tile)
            scaled = (wide_ref[:, cols] * gcore_f).astype(BF16)
            acc_ref[:, cols] = acc_ref[:, cols] + dot(out_keys, scaled, 0, 0)
        rowq_ref[at, :] = rowq
        return before + cum[CHUNK - 1 : CHUNK]

    lax.fori_loop(0, chunks, chunk, jnp.zeros((1, LANES), F32))
    lsg_ref[...] = acc_ref[...].astype(BF16)

    def finish(i, carry):
        at = pl.ds(pl.multiple_of(i * CHUNK, CHUNK), CHUNK)
        row = lax.broadcasted_iota(jnp.int32, (CHUNK, model), 0) + i * CHUNK
        u = x_ref[pl.ds(pl.multiple_of(i * CHUNK + HALO, HALO), CHUNK), :].astype(F32)
        out_ref[at, :] = (u + jnp.where(row < scal[1], gno_ref[at, 0:model], 0.0)).astype(BF16)
        return carry

    for j in range(2):
        cols = slice(j * model // 2, (j + 1) * model // 2)
        gno_ref[:, cols] = dot(gn_ref[...], w_ref[:, cols])
    lax.fori_loop(0, chunks, finish, 0)


def put_block(dp, devices, block, keep_ref, send_ref, start, cols, part):
    steps = len(step_bits(devices))
    away = jnp.bitwise_xor(dp, block)
    backward = away // 2
    forward = jnp.int32(0)
    for k in range(steps):
        forward = forward * 2 + jnp.bitwise_and(jnp.right_shift(backward, k), 1)
    even = jnp.bitwise_and(dp, 1) == 0
    rows = part.shape[0]

    @pl.when(away % 2 == 0)
    def _():
        keep_ref[jnp.where(even, forward, backward), start : start + rows, cols] = part

    @pl.when(away % 2 == 1)
    def _():
        send_ref[jnp.where(even, backward, forward), start : start + rows, cols] = part


def early_kernel(rows, devices, scal, gn_ref, c_ref, nh_ref, dgate_ref, keep_ref, send_ref, mc_ref):
    length, model = c_ref.shape
    chunks = length // CHUNK

    def mask(i, carry):
        at = pl.ds(pl.multiple_of(i * CHUNK, CHUNK), CHUNK)
        row = lax.broadcasted_iota(jnp.int32, (CHUNK, model), 0) + i * CHUNK
        mc_ref[at, :] = jnp.where(row < scal[1], c_ref[at, :].astype(F32), 0.0).astype(BF16)
        return carry

    lax.fori_loop(0, chunks, mask, 0)
    half = model // 2
    for j in range(2 * INNER // model):
        part = dot(nh_ref[HALO:, :], dgate_ref[:, j * half : (j + 1) * half], 0, 0).astype(BF16)
        start = (j // 2) * rows
        cols = slice((j % 2) * half, (j % 2 + 1) * half)
        for block in range(devices):
            put_block(
                scal[0], devices, block, keep_ref, send_ref, start, cols, part[block * rows : (block + 1) * rows]
            )
    for j in range(INNER // half):
        part = dot(gn_ref[:, j * half : (j + 1) * half], mc_ref[...], 0, 0).astype(BF16)
        each = half // (2 * rows)
        for n in range(each):
            put_block(
                scal[0], devices, j * each + n, keep_ref, send_ref, 2 * rows, slice(0, model),
                part[n * 2 * rows : (n + 1) * 2 * rows],
            )


def local_back_kernel(plan, rows, scal, act_ref, step_ref, cum_ref, gcore_ref, dgate_ref, *refs):
    count = PIECES
    pieces = refs[:count]
    gvl_ref, gk_ref, gng_ref, w_ref, sem = refs[count:]
    copies = start_pieces(scal[0], pieces, plan, w_ref, sem, rows)
    chunks = act_ref.shape[0] // CHUNK
    half = gng_ref.shape[1] // 2
    left = lax.broadcasted_iota(jnp.int32, (CHUNK, LANES), 1) < HDIM

    def chunk(c, carry):
        at = pl.ds(pl.multiple_of(c * CHUNK, CHUNK), CHUNK)
        in_keys = act_ref[at, INNER : INNER + STATE]
        out_keys = act_ref[at, INNER + STATE : CHANNELS]
        affinity = jnp.where(causal_tile(), dot(out_keys, in_keys, 1, 1), 0.0)
        cum = cum_ref[at, :]
        cum_rows = cum.T
        step_rows = step_ref[at, :].T
        gaff = jnp.zeros((CHUNK, CHUNK), F32)
        for tile in range(INNER // LANES):
            cols = slice(tile * LANES, (tile + 1) * LANES)
            values = act_ref[at, cols]
            grads = gcore_ref[at, cols]
            zero = jnp.zeros_like(grads)
            apart = jnp.concatenate(
                [jnp.where(left, grads, zero), jnp.where(left, zero, grads)], axis=0
            )
            gmix = dot(apart, values, 1, 1)
            mixing = []
            for n in range(2):
                weight = mixing_parts(cum, cum_rows, step_rows, 2 * tile + n)
                gaff = gaff + gmix[n * CHUNK : (n + 1) * CHUNK] * weight
                mixing.append((affinity * weight).astype(BF16))
            back = dot(jnp.concatenate(mixing, axis=1), grads, 0, 0)
            gvl_ref[at, cols] = jnp.where(left, back[0:CHUNK], back[CHUNK:])
        gaff = jnp.where(causal_tile(), gaff, 0.0).astype(BF16)
        gk_ref[at, 0:STATE] = dot(gaff, out_keys, 0, 0)
        gk_ref[at, STATE : 2 * STATE] = dot(gaff, in_keys)
        return carry

    lax.fori_loop(0, chunks, chunk, 0)
    wait_all(copies)
    for j in range(2):
        cols = slice(j * half, (j + 1) * half)
        gng_ref[:, cols] = dot(dgate_ref[...], w_ref[cols, :], 1, 1)


def scan_back_kernel(act_ref, step_ref, sig_ref, cum_ref, gcore_ref, gvl_ref, gk_ref, rowq_ref, states_ref,
                     gout_ref, gskip_ref, skip_ref, cext_ref, cw_ref, cb_ref, dl_ref, gconv_ref, head_ref, graw_ref, small_ref,
                     gstate_ref, wide_ref, gact_ref, expand_ref):
    chunks = act_ref.shape[0] // CHUNK
    tiles = INNER // LANES
    fill_expander(expand_ref)
    gstate_ref[...] = gout_ref[...].astype(F32)
    small_ref[...] = jnp.zeros_like(small_ref)
    small_ref[6:7, 0:INNER] = jnp.sum(gskip_ref[...], axis=0, keepdims=True)
    rate = -jnp.exp(dl_ref[0:1, :])
    end = lax.broadcasted_iota(jnp.int32, (CHUNK, LANES), 0) == CHUNK - 1

    def chunk(n, carry):
        gdecay, gbias = carry
        c = chunks - 1 - n
        at = pl.ds(pl.multiple_of(c * CHUNK, CHUNK), CHUNK)
        in_keys = act_ref[at, INNER : INNER + STATE]
        out_keys = act_ref[at, INNER + STATE : CHANNELS]
        cum = cum_ref[at, :]
        step = step_ref[at, :]
        sig = sig_ref[at, :]
        last = cum[CHUNK - 1 : CHUNK]
        small = jnp.concatenate(
            [jnp.exp(cum), jnp.exp(last - cum) * step, jnp.broadcast_to(jnp.exp(last), (8, LANES))], axis=0
        )
        wide_ref[...] = dot(jnp.concatenate(two_parts(small), axis=1), expand_ref[...])
        colq = jnp.zeros((CHUNK, LANES), F32)
        ends = jnp.zeros((8, LANES), F32)
        gin = gk_ref[at, 0:STATE]
        gout = gk_ref[at, STATE : 2 * STATE]
        for tile in range(tiles):
            cols = slice(tile * LANES, (tile + 1) * LANES)
            values = act_ref[at, cols].astype(F32)
            grads = gcore_ref[at, cols].astype(F32)
            gstate = gstate_ref[:, cols]
            gstate_b = gstate.astype(BF16)
            state = states_ref[c, :, cols]
            weight = wide_ref[CHUNK : 2 * CHUNK, cols]
            decay = wide_ref[2 * CHUNK : 2 * CHUNK + 1, cols]
            gvs = weight * dot(in_keys, gstate_b)
            gvalues = gvl_ref[at, cols] + gvs
            colq = colq + head_sums(values * gvalues, tile)
            passed = jnp.sum((values * gvs).reshape(CHUNK // 8, 8, LANES), axis=0) + decay * jnp.sum(
                (gstate * state.astype(F32)).reshape(STATE // 8, 8, LANES), axis=0
            )
            ends = ends + head_sums(passed, tile)
            gin = gin + dot((weight * values).astype(BF16), gstate_b, 1, 1)
            scaled = (wide_ref[0:CHUNK, cols] * grads).astype(BF16)
            gout = gout + dot(scaled, state, 1, 1)
            gstate_ref[:, cols] = decay * gstate + dot(out_keys, scaled, 0, 0)
            gact_ref[:, cols] = gvalues + skip_ref[0:1, cols] * grads
        gact_ref[:, INNER : INNER + STATE] = gin
        gact_ref[:, INNER + STATE : CHANNELS] = gout
        gcum = rowq_ref[at, :] - colq
        gcum = gcum + jnp.where(end, jnp.sum(ends, axis=0, keepdims=True), 0.0)
        glog = running_sum(gcum, reverse=True)
        gdecay = gdecay + jnp.sum((glog * (rate * step)).reshape(CHUNK // 8, 8, LANES), axis=0)
        ratio = jnp.where(step > 0.0, sig / jnp.where(step > 0.0, step, 1.0), 0.0)
        graw = colq * ratio + rate * glog * sig
        gbias = gbias + jnp.sum(graw.reshape(CHUNK // 8, 8, LANES), axis=0)
        first = pl.multiple_of(c * CHUNK, CHUNK)
        graw_ref[at, :] = graw.astype(BF16)
        for tile in range(CHANNELS // LANES):
            cols = slice(tile * LANES, (tile + 1) * LANES)
            part = cext_ref[pl.ds(first, CHUNK + HALO), cols].astype(F32)
            moved = [pltpu.roll(part, KCONV - 1 - k, 0)[HALO:] for k in range(KCONV - 1)] + [part[HALO:]]
            out = cb_ref[0:1, cols]
            for k in range(KCONV):
                out = out + cw_ref[k : k + 1, cols] * moved[k]
            sc = jax.nn.sigmoid(out)
            gconv = gact_ref[:, cols] * (sc * (1.0 + out * (1.0 - sc)))
            gconv_ref[at, cols] = gconv
            for k in range(KCONV):
                small_ref[k : k + 1, cols] = small_ref[k : k + 1, cols] + jnp.sum(
                    gconv * moved[k], axis=0, keepdims=True
                )
            small_ref[4:5, cols] = small_ref[4:5, cols] + jnp.sum(gconv, axis=0, keepdims=True)
        return gdecay, gbias

    zero = jnp.zeros((8, LANES), F32)
    gdecay, gbias = lax.fori_loop(0, chunks, chunk, (zero, zero))
    small_ref[5:6, 0:LANES] = jnp.sum(gdecay, axis=0, keepdims=True)
    small_ref[5:6, LANES : 2 * LANES] = jnp.sum(gbias, axis=0, keepdims=True)
    head_ref[...] = gconv_ref[0:HALO, :]


def conv_back_kernel(rows, devices, scal, gconv_ref, ahead_ref, graw_ref, nh_ref, cw_ref, gproj_ref, keep_ref,
                     send_ref):
    length = gconv_ref.shape[0]
    tall = 4 * HALO
    gproj_ref[:, CHANNELS:] = graw_ref[...]

    def rows_back(first, part_of):
        for tile in range(CHANNELS // LANES):
            cols = slice(tile * LANES, (tile + 1) * LANES)
            part = part_of(cols)
            total = cw_ref[KCONV - 1 : KCONV, cols] * part[:tall]
            for k in range(KCONV - 1):
                ahead = pltpu.roll(part, part.shape[0] - (KCONV - 1 - k), 0)[:tall]
                total = total + cw_ref[k : k + 1, cols] * ahead
            gproj_ref[pl.ds(first, tall), cols] = total.astype(BF16)

    def conv_back(i, carry):
        first = pl.multiple_of(i * tall, tall)
        rows_back(first, lambda cols: gconv_ref[pl.ds(first, tall + 8), cols])
        return carry

    lax.fori_loop(0, length // tall - 1, conv_back, 0)
    rows_back(
        length - tall,
        lambda cols: jnp.concatenate([gconv_ref[length - tall :, cols], ahead_ref[0:8, cols]], axis=0),
    )
    for j in range(WIDTH // 384):
        cols = slice(j * 384, (j + 1) * 384)
        part = dot(nh_ref[HALO:, :], gproj_ref[:, cols], 0, 0).astype(BF16)
        for block in range(devices):
            put_block(
                scal[0], devices, block, keep_ref, send_ref, 0, cols, part[block * rows : (block + 1) * rows]
            )


def token_back_kernel(plan, rows, scal, gproj_ref, gng_ref, x_ref, c_ref, *refs):
    count = PIECES
    pieces = refs[:count]
    gtok_ref, w_ref, acc_ref, sem = refs[count:]
    copies = start_pieces(scal[0], pieces, plan, w_ref, sem, rows)
    length, model = c_ref.shape
    tall = 4 * HALO
    wait_all(copies)
    for j in range(2):
        cols = slice(j * model // 2, (j + 1) * model // 2)
        acc_ref[:, cols] = dot(gproj_ref[...], w_ref[cols, :], 1, 1) + gng_ref[:, cols]
    gain = gain_row(w_ref)

    def norm_back(i, carry):
        at = pl.ds(pl.multiple_of(i * tall, tall), tall)
        u = x_ref[pl.ds(pl.multiple_of(i * tall + HALO, HALO), tall), :].astype(F32)
        scale = lax.rsqrt(jnp.mean(u * u, axis=1, keepdims=True) + EPSILON)
        nh = u * scale
        g = acc_ref[at, :] * gain
        grads = scale * (g - nh * jnp.mean(g * nh, axis=1, keepdims=True))
        gtok_ref[at, :] = (grads + c_ref[at, :].astype(F32)).astype(BF16)
        return carry

    lax.fori_loop(0, length // tall, norm_back, 0)


def call(body, scal, whole, pieces, outs, scratch):
    first = [] if scal is None else [scal]
    smem = pl.BlockSpec(memory_space=pltpu.SMEM)
    vmem = pl.BlockSpec(memory_space=pltpu.VMEM)
    return list(pl.pallas_call(
        body,
        out_shape=[jax.ShapeDtypeStruct(shape, kind) for shape, kind in outs],
        in_specs=[smem] * len(first) + [vmem] * len(whole) + [pl.BlockSpec(memory_space=pl.ANY)] * len(pieces),
        out_specs=[vmem] * len(outs),
        scratch_shapes=scratch,
        compiler_params=pltpu.CompilerParams(vmem_limit_bytes=VMEM_LIMIT),
    )(*first, *whole, *pieces))


def lane_row(vector):
    return jnp.pad(vector, (0, LANES - vector.shape[0]))[None]


def per_device(tokens, lengths, dealing, cotangent, in_weight, out_weight, norm_gain, gate_gain, conv_weight,
               conv_bias, decay_log, step_bias, skip_gain):
    dp, seq = lax.axis_index("dp"), lax.axis_index("seq")
    devices, size = lax.axis_size("dp"), lax.axis_size("seq")
    group = size // 2
    lin = seq * 2 + dp % 2
    holder = lin // group
    place = {"dp": dp, "seq": seq, "micro": holder // 2, "column": holder % 2, "turn": lin % group}
    block_len, model = tokens.shape[2:]
    length = 2 * block_len
    shard_rows = in_weight.shape[0]
    rows = shard_rows * size
    tok = tokens[:, 0]
    cot = cotangent[:, 0]

    gains = jnp.concatenate(
        [norm_gain[:, None], jnp.swapaxes(gate_gain.reshape(2, shard_rows), 0, 1)], axis=1
    )
    conv_shard = jnp.concatenate([in_weight[:, INNER:], gains], axis=1)
    conv_shard = jnp.pad(conv_shard, ((0, 0), (0, WIDTH - conv_shard.shape[1])))
    rest_shard = jnp.concatenate(
        [in_weight[:, :INNER], out_weight[:shard_rows], out_weight[shard_rows:]], axis=1
    )
    masks = spread_masks(devices)
    conv_plan = (masks, [(0, 1, 0, 0, WIDTH)])
    gate_plan = (masks, [(0, 1, 0, 0, model), (rows, 1, 0, model, model)])
    out_plan = (masks, [(0, 2, model, 0, model + LANES)])

    dealt = devices == 8
    if dealt:
        routes = make_routes(place, dp_table(jnp.concatenate([dealing[:, 0], lengths[:, 0]])))
        cot_chain = Chain(cotangent_stages(core_pair(cot, place), routes, place))
        own_length = routes[4, 0]
        moving = [cot_chain]
    else:
        every = lax.all_gather(jnp.concatenate([dealing, lengths], axis=0)[:, 0], "dp", axis=0)
        goals = every[:, :2]
        source_of_out = jnp.argmax(goals == dp, axis=0)
        cot_given = deal_gathered(cot, dealing[:, 0])
        mate = lax.dynamic_index_in_dim(every, dp - dp % 2 + place["column"], 0, keepdims=False)
        own_length = jnp.where(place["micro"] == 0, mate[2], mate[3])
        moving = []

    taps = jnp.pad(conv_weight, ((0, 8 - KCONV), (0, 0)))
    skip_row = jnp.repeat(skip_gain, HDIM)[None]
    n_valid = jnp.clip(own_length - place["turn"] * length, 0, length)
    scal = jnp.stack([dp, n_valid, place["micro"]])
    rows_of = (taps, conv_bias[None], lane_row(decay_log), lane_row(step_bias), skip_row, scal)

    shards = Chain(seq_stages(conv_shard, place))
    tok = advance(swapped(place["seq"] % 2 == 1, tok), shards, *moving)
    conv_z = shards.value
    conv = Chain(spread_stages(conv_z.reshape(rows, WIDTH)))
    one, two = send_stretch(tok)
    one, two, rows_of, rest_shard = advance((one, two, rows_of, rest_shard), conv, *moving)
    taps, conv_bias_row, decay_row, bias_row, skip_row, scal = rows_of
    late = place["micro"] == 1
    tail = jnp.where(late, one[block_len - HALO :], two[block_len - HALO :])
    halo = lax.ppermute(tail, BOTH, neighbour_pairs(1))
    one, two, halo = advance((one, two, halo), conv, *moving)
    shards = Chain(seq_stages(rest_shard, place))
    while conv.pending is not None:
        halo = advance(halo, conv, *moving)
    conv_pieces = conv.value
    gain_rows = jnp.swapaxes(conv_z[:, :, CHANNELS + HEADS + 1 : CHANNELS + HEADS + 3], 1, 2)
    gain_rows = jnp.pad(gain_rows.reshape(2 * rows, 1), ((0, 0), (0, LANES - 1)))
    moving = moving + [shards]
    def sems(plan):
        return pltpu.SemaphoreType.DMA((piece_count(plan),))

    wide = (length, INNER)
    made = call(
        functools.partial(project_kernel, conv_plan, rows),
        scal,
        [one, two, halo, taps, conv_bias_row, decay_row, bias_row],
        conv_pieces,
        [((length + HALO, model), BF16)] * 2 + [((length + HALO, CHANNELS), BF16), ((length, CHANNELS), BF16)]
        + [((length, LANES), F32)] * 3,
        [pltpu.VMEM((model, WIDTH), BF16), pltpu.VMEM((length + HALO, WIDTH), F32), sems(conv_plan)],
    )
    x_ext, nh, cext, act, step, sig, cum = advance(made, *moving)
    rest_z = shards.value
    gate_z = [rest_z[:, :, n * model : (n + 1) * model].reshape(rows, model) for n in range(2)]
    out_z = jnp.concatenate([rest_z[:, :, INNER : INNER + model], rest_z[:, :, INNER + model :]], axis=1)
    out_z = out_z.reshape(2 * rows, model)
    rest = Chain(spread_stages(jnp.concatenate([jnp.concatenate(gate_z), out_z, gain_rows], axis=1)))
    moving[-1] = rest
    local, update, total = advance(
        call(
            local_kernel,
            None,
            [act, step, cum],
            [],
            [(wide, F32), ((STATE, INNER), BF16), ((8, LANES), F32)],
            [pltpu.VMEM((STATE, INNER), F32), pltpu.VMEM((2 * LANES, INNER), BF16)],
        ),
        *moving,
    )
    passing = jnp.repeat(jnp.exp(total[0, :HEADS]), HDIM)[None] if group > 2 else None

    def relay(own, pairs):
        carried = None
        for _ in range(group - 1):
            given = own if carried is None else (passing * carried.astype(F32) + own.astype(F32)).astype(BF16)
            carried = lax.ppermute(given, BOTH, pairs)
        return jnp.zeros_like(own) if carried is None else carried

    state_in = relay(update, neighbour_pairs(1))
    core, states = advance(
        call(
            core_kernel,
            None,
            [local, act, step, cum, state_in],
            [],
            [(wide, F32), ((length // CHUNK, STATE, INNER), BF16)],
            [pltpu.VMEM((STATE, INNER), F32), pltpu.VMEM((2 * CHUNK + 8, INNER), F32),
             pltpu.VMEM((2 * LANES, INNER), BF16)],
        ),
        *moving,
    )
    while rest.pending is not None:
        advance((), *moving)
    if dealt:
        while cot_chain.pending is not None:
            advance((), cot_chain)
        c_pair = cot_chain.value
    else:
        c_pair = to_stretch(cot_given, place)
    rest_pieces = rest.value

    c_own, out, gn, dgate, gcore, rowq, lsg, gskip = call(
        functools.partial(middle_kernel, gate_plan, out_plan, rows),
        scal,
        [core, act, cum, nh, x_ext, *c_pair, skip_row],
        rest_pieces,
        [((length, model), BF16)] * 2 + [(wide, BF16), (wide, BF16), (wide, BF16), ((length, LANES), F32),
         ((STATE, INNER), BF16), ((8, INNER), F32)],
        [pltpu.VMEM((INNER, model + LANES), BF16), pltpu.VMEM((model, INNER), BF16), pltpu.VMEM(wide, F32),
         pltpu.VMEM((8, INNER), F32), pltpu.VMEM((length, model), BF16), pltpu.VMEM(wide, F32),
         pltpu.VMEM((CHUNK, INNER), F32), pltpu.VMEM((CHUNK, INNER), F32), pltpu.VMEM((CHUNK, INNER), F32),
         pltpu.VMEM((CHUNK, INNER), F32), pltpu.VMEM((STATE, INNER), F32),
         pltpu.VMEM((2 * LANES, INNER), BF16), sems(gate_plan), sems(out_plan)],
    )
    if dealt:
        moving = [Chain(output_stages(out, routes, place))]
        out_chain = moving[0]
    else:
        moving = []
        blocks = jnp.stack(swapped(place["seq"] % 2 == 1, from_stretch(out[:block_len], out[block_len:], place)))
        outputs = deal_gathered(blocks, source_of_out)
    grad_out_state = relay(lsg, neighbour_pairs(-1))

    half_dp = devices // 2
    keep1, send1, gcore, dgate = advance(
        call(
            functools.partial(early_kernel, rows, devices),
            scal,
            [gn, c_own, nh, dgate],
            [],
            [((half_dp, 4 * rows, model), BF16)] * 2,
            [pltpu.VMEM((length, model), BF16)],
        )
        + [gcore, dgate],
        *moving,
    )

    early_segments = [(0, shard_rows), (rows, shard_rows), (2 * rows, 2 * shard_rows)]
    early = Chain(reduce_stages(keep1, send1, place, early_segments))
    moving.append(early)
    made = call(
        functools.partial(local_back_kernel, gate_plan, rows),
        scal,
        [act, step, cum, gcore, dgate],
        rest_pieces,
        [(wide, F32), ((length, 2 * STATE), F32), ((length, model), F32)],
        [pltpu.VMEM((model, INNER), BF16), sems(gate_plan)],
    )
    gvl, gk, gng, grad_out_state = advance(made + [grad_out_state], *moving)
    gconv, head, graw, small = advance(
        call(
            scan_back_kernel,
            None,
            [act, step, sig, cum, gcore, gvl, gk, rowq, states, grad_out_state, gskip, skip_row, cext, taps,
             conv_bias_row, decay_row],
            [],
            [((length, CHANNELS), F32), ((HALO, CHANNELS), F32), ((length, LANES), BF16), ((8, WIDTH), F32)],
            [pltpu.VMEM((STATE, INNER), F32), pltpu.VMEM((2 * CHUNK + 8, INNER), F32),
             pltpu.VMEM((CHUNK, CHANNELS), F32), pltpu.VMEM((2 * LANES, INNER), BF16)],
        ),
        *moving,
    )
    ahead = lax.ppermute(head, BOTH, neighbour_pairs(-1))
    sums = Chain(sum_stages(small))
    moving.append(sums)
    gproj, keep2, send2 = advance(
        call(
            functools.partial(conv_back_kernel, rows, devices),
            scal,
            [gconv, ahead, graw, nh, taps],
            [],
            [((length, WIDTH), BF16)] + [((half_dp, rows, WIDTH), BF16)] * 2,
            [],
        ),
        *moving,
    )

    final = Chain(reduce_stages(keep2, send2, place, [(0, shard_rows)]))
    moving.append(final)
    (gtok,) = advance(
        call(
            functools.partial(token_back_kernel, conv_plan, rows),
            scal,
            [gproj, gng, x_ext, c_own],
            conv_pieces,
            [((length, model), BF16)],
            [pltpu.VMEM((model, WIDTH), BF16), pltpu.VMEM((length, model), F32), sems(conv_plan)],
        ),
        *moving,
    )

    one, two = from_stretch(gtok[:block_len], gtok[block_len:], place)
    one = advance(one, sums, final)
    back = one, advance(two, sums, final)
    while any(chain.pending is not None for chain in moving):
        advance((), *moving)
    grad_tokens = jnp.stack(swapped(place["seq"] % 2 == 1, back))
    if dealt:
        outputs = out_chain.value

    early_sum, late_sum, sums = early.value, final.value, sums.value
    raw_in = jnp.concatenate(
        [early_sum[:shard_rows], early_sum[shard_rows : 2 * shard_rows],
         late_sum[:, : in_weight.shape[1] - INNER]], axis=1
    )
    raw_out = early_sum[2 * shard_rows :]
    grad_norm_gain = jnp.sum(raw_in * in_weight.astype(F32), axis=1) / norm_gain.astype(F32)
    grad_gate_gain = jnp.sum(raw_out * out_weight.astype(F32), axis=1) / gate_gain.astype(F32)
    grad_skip = jnp.sum(sums[6, :INNER].reshape(HEADS, HDIM), axis=1)
    return (
        outputs[:, None],
        grad_tokens[:, None],
        raw_in,
        raw_out,
        grad_norm_gain,
        grad_gate_gain,
        sums[0:KCONV, :CHANNELS],
        sums[4, :CHANNELS],
        sums[5, :HEADS],
        sums[5, LANES : LANES + HEADS],
        grad_skip,
    )


def solution(mesh):
    in_specs = (
        P(None, "dp", "seq", None),
        P(None, "dp"),
        P(None, "dp"),
        P(None, "dp", "seq", None),
        P(BOTH, None),
        P(BOTH, None),
        P(BOTH),
        P(BOTH),
        P(),
        P(),
        P(),
        P(),
        P(),
    )
    out_specs = (
        P(None, "dp", "seq", None),
        P(None, "dp", "seq", None),
        P(BOTH, None),
        P(BOTH, None),
        P(BOTH),
        P(BOTH),
        P(),
        P(),
        P(),
        P(),
        P(),
    )
    return jax.shard_map(per_device, mesh=mesh, in_specs=in_specs, out_specs=out_specs, check_vma=False)
```

```python
import functools

import jax
import jax.numpy as jnp
from jax import lax
from jax.experimental import pallas as pl
from jax.experimental.pallas import tpu as pltpu
from jax.sharding import PartitionSpec as P

INNER = 1536
HEADS = 24
HDIM = 64
STATE = 128
KCONV = 4
CHANNELS = INNER + 2 * STATE
LANES = 128
CHUNK = 128
HALO = 16
PIECES = 4
EPSILON = 1e-05
WIDTH = CHANNELS + LANES
F32 = jnp.float32
BF16 = jnp.bfloat16
BOTH = ("dp", "seq")
VMEM_LIMIT = 60 * 1024 * 1024


def flip_dp(value, mask):
    pairs = [(i, i ^ mask) for i in range(lax.axis_size("dp"))]
    return lax.ppermute(value, "dp", pairs)


def step_bits(size):
    return list(range(1, size.bit_length() - 1))


def flip_step(value, step):
    size = lax.axis_size("dp")
    bits = step_bits(size)
    pairs = [(i, i ^ (1 << (bits[-1 - step] if i % 2 else bits[step]))) for i in range(size)]
    return lax.ppermute(value, "dp", pairs)


def shift_seq(value, step):
    size = lax.axis_size("seq")
    return lax.ppermute(value, "seq", [(i, (i + step) % size) for i in range(size)])


def column_place(dp_even, lin):
    return (dp_even + lin % 2) * lax.axis_size("seq") + lin // 2


def unit_pairs(parity):
    size = lax.axis_size("seq")
    pairs = []
    for dp in range(lax.axis_size("dp")):
        core = dp % 2
        for block in range(size):
            micro = (block % 2) ^ parity
            lin = (2 * micro + core) * (size // 2) + block // 2
            pairs.append((dp * size + block, column_place(dp - core, lin)))
    return pairs


def neighbour_pairs(step):
    size = lax.axis_size("seq")
    group = size // 2
    pairs = []
    for dp_even in range(0, lax.axis_size("dp"), 2):
        for lin in range(2 * size):
            if 0 <= lin % group + step < group:
                pairs.append((column_place(dp_even, lin), column_place(dp_even, lin + step)))
    return pairs


def reversed_pairs(pairs):
    return [(target, source) for source, target in pairs]


def to_stretch(blocks, place):
    return send_stretch(swapped(place["seq"] % 2 == 1, blocks))


def send_stretch(pair):
    return tuple(lax.ppermute(pair[n], BOTH, unit_pairs(n)) for n in range(2))


def swapped(swap, pair):
    return jnp.where(swap, pair[1], pair[0]), jnp.where(swap, pair[0], pair[1])


def from_stretch(first, second, place):
    late = place["micro"] == 1
    one = lax.ppermute(jnp.where(late, second, first), BOTH, reversed_pairs(unit_pairs(0)))
    two = lax.ppermute(jnp.where(late, first, second), BOTH, reversed_pairs(unit_pairs(1)))
    return one, two


class Chain:
    def __init__(self, stages):
        self.stages = stages
        self.value = None
        self.pending = next(stages)

    def feed(self, arrived):
        try:
            self.pending = self.stages.send(arrived)
        except StopIteration as stop:
            self.pending = None
            self.value = stop.value


def advance(held, *chains):
    moving = [chain for chain in chains if chain.pending is not None]
    held, arrived = lax.optimization_barrier((held, [chain.pending for chain in moving]))
    for chain, got in zip(moving, arrived):
        chain.feed(got)
    return held


def seq_shifts(shard):
    return [shift_seq(shard, j) for j in range(1, lax.axis_size("seq"))]


def seq_order(shard, arrived, place):
    size = lax.axis_size("seq")
    got = [shard] + list(arrived)
    rows = []
    for i in range(size):
        row = got[0]
        for j in range(1, size):
            row = jnp.where((place["seq"] - i) % size == j, got[j], row)
        rows.append(row)
    return jnp.stack(rows)


def seq_stages(shard, place):
    arrived = yield seq_shifts(shard)
    return seq_order(shard, arrived, place)


def spread_stages(block):
    steps = len(step_bits(lax.axis_size("dp")))
    held, last, turned = block[None], None, None
    for step in range(steps):
        if last is not None:
            held = jnp.concatenate([held, last])
        if step < steps - 1:
            last = (yield [flip_step(held, step)])[0]
        else:
            last, turned = yield [flip_step(held, step), flip_dp(held, 1)]
    end = (yield [flip_dp(last, 1)])[0]
    return [held, last, turned, end]


def spread_masks(size):
    found = []
    for bits in (step_bits(size), step_bits(size)[::-1]):
        masks, last = (0,), None
        for bit in bits:
            if last is not None:
                masks = masks + last
            last = tuple(m ^ (1 << bit) for m in masks)
        found.append((masks, last))
    even, odd = found
    own = [(even[n], odd[n]) for n in range(2)]
    return own + [(tuple(m ^ 1 for m in b), tuple(m ^ 1 for m in a)) for a, b in own]


def reduce_stages(keep, send, place, segments):
    steps = len(step_bits(lax.axis_size("dp")))
    parts = [keep] + (yield [flip_dp(send, 1)])
    for step in range(steps):
        first = 1 << (steps - 1 - step)
        parts = parts + (yield [flip_step(give_up(parts, first), step)])
    gives = take_rows(parts, segments, place)
    moved = yield [shift_seq(gives[j], j) for j in range(1, lax.axis_size("seq"))]
    return add_up([gives[0]] + moved)


def row_loop(rows, body):
    tall = 32 if rows % 32 == 0 else rows

    def step(i, carry):
        body(pl.ds(pl.multiple_of(i * tall, tall), tall))
        return carry

    lax.fori_loop(0, rows // tall, step, 0)


def give_kernel(*refs):
    *parts, out_ref = refs

    def some(at):
        out_ref[0, at, :] = add_up([part[0, at, :] for part in parts]).astype(BF16)

    row_loop(out_ref.shape[1], some)


def give_up(parts, first):
    rows, cols = parts[0].shape[1:]
    return pl.pallas_call(
        give_kernel,
        grid=(first,),
        out_shape=jax.ShapeDtypeStruct((first, rows, cols), BF16),
        in_specs=[pl.BlockSpec((1, rows, cols), lambda n: (first + n, 0, 0))] * len(parts),
        out_specs=pl.BlockSpec((1, rows, cols), lambda n: (n, 0, 0)),
    )(*parts)


def take_kernel(size, segments, seq_ref, *refs):
    parts = refs[: len(refs) - size - 1]
    own_ref, *out_refs = refs[len(parts) : -1]
    total_ref = refs[-1]

    def some(at):
        total_ref[at, :] = add_up([part[0, at, :] for part in parts])

    row_loop(total_ref.shape[0], some)
    for j in range(size):
        index = (seq_ref[0] + j) % size
        start = 0
        for first, rows in segments:
            found = total_ref[pl.ds(pl.multiple_of(first + index * rows, 8), rows), :]
            if j == 0:
                own_ref[start : start + rows, :] = found
            else:
                out_refs[j - 1][start : start + rows, :] = found.astype(BF16)
            start += rows


def take_rows(parts, segments, place):
    size = lax.axis_size("seq")
    rows, cols = parts[0].shape[1:]
    taken = sum(count for _, count in segments)
    if any(first % 8 or count % 8 for first, count in segments):
        total = add_up([part[0] for part in parts])
        gives = []
        for j in range(size):
            index = (place["seq"] + j) % size
            found = [lax.dynamic_slice_in_dim(total, f + index * count, count) for f, count in segments]
            gives.append(jnp.concatenate(found).astype(BF16 if j else F32))
        return gives
    return pl.pallas_call(
        functools.partial(take_kernel, size, segments),
        grid=(1,),
        out_shape=[jax.ShapeDtypeStruct((taken, cols), BF16 if j else F32) for j in range(size)],
        in_specs=[pl.BlockSpec(memory_space=pltpu.SMEM)]
        + [pl.BlockSpec((1, rows, cols), lambda n: (0, 0, 0))] * len(parts),
        out_specs=[pl.BlockSpec((taken, cols), lambda n: (0, 0))] * size,
        scratch_shapes=[pltpu.VMEM((rows, cols), F32)],
    )(place["seq"][None], *parts)


def add_up(parts):
    total = parts[0].astype(F32)
    for part in parts[1:]:
        total = total + part.astype(F32)
    return total


def sum_stages(value):
    value = value + flip_dp(value, 1)
    size = lax.axis_size("seq")
    apart = 1
    while apart < size:
        got = yield [lax.ppermute(value, "seq", [(i, i ^ apart) for i in range(size)])]
        value = value + got[0]
        apart *= 2
    for bit in range(1, lax.axis_size("dp").bit_length() - 1):
        got = yield [flip_dp(value, 1 << bit)]
        value = value + got[0]
    return value


def dp_table(row):
    table = row[None]
    for bit in range(lax.axis_size("dp").bit_length() - 1):
        table = jnp.concatenate([table, flip_dp(table, 1 << bit)])
    return table


def route_row(dp, goal, first_bit, second_bit):
    held = [0, 1, first_bit, first_bit | 1]

    def chosen(base):
        low = jnp.int32(0)
        high = jnp.int32(0)
        for n in range(3, -1, -1):
            away = jnp.bitwise_xor(goal[base ^ held[n]], jnp.bitwise_xor(dp, base))
            cross = (jnp.bitwise_and(away, second_bit) != 0) & (jnp.bitwise_and(away, first_bit) == 0)
            low = jnp.where(cross, n, low)
        for n in range(4):
            away = jnp.bitwise_xor(goal[base ^ held[n]], jnp.bitwise_xor(dp, base))
            cross = (jnp.bitwise_and(away, second_bit) != 0) & (jnp.bitwise_and(away, first_bit) == 0)
            high = jnp.where(cross, n, high)
        return low, high

    low, high = chosen(0)
    other_low, _ = chosen(second_bit)
    row = [low, high]
    for side in range(2):
        pick = jnp.int32(0)
        target = jnp.bitwise_xor(dp, side)
        for n in range(4):
            pick = jnp.where(goal[held[n]] == target, n, pick)
            far = jnp.where(other_low == n, 4, 5)
            pick = jnp.where(goal[held[n] ^ second_bit] == target, far, pick)
        row.append(pick)
    return row


def route_kernel(place_ref, table_ref, out_ref):
    dp = place_ref[0]
    size = table_ref.shape[0]
    for way in range(2):
        for micro in range(2):
            goal = []
            for r in range(size):
                if way == 1:
                    goal.append(table_ref[r, micro])
                else:
                    found = jnp.int32(0)
                    for other in range(size):
                        hit = table_ref[other, micro] == jnp.bitwise_xor(dp, r)
                        found = jnp.where(hit, jnp.bitwise_xor(dp, other), found)
                    goal.append(found)
            even = route_row(dp, goal, 2, 4)
            odd = route_row(dp, goal, 4, 2)
            for n in range(4):
                out_ref[way * 2 + micro, n] = jnp.where(jnp.bitwise_and(dp, 1) == 0, even[n], odd[n])
    core = jnp.bitwise_and(dp, 1)
    column = jnp.bitwise_xor(core, place_ref[2])
    micro = place_ref[1]
    own = jnp.where(micro == 0, table_ref[0, 2], table_ref[0, 3])
    other = jnp.where(micro == 0, table_ref[1, 2], table_ref[1, 3])
    out_ref[4, 0] = jnp.where(column == 0, own, other)
    out_ref[4, 1] = place_ref[3]
    for n in range(2, 4):
        out_ref[4, n] = jnp.int32(0)


def make_routes(place, table):
    return pl.pallas_call(
        route_kernel,
        out_shape=jax.ShapeDtypeStruct((5, 4), jnp.int32),
        in_specs=[pl.BlockSpec(memory_space=pltpu.SMEM)] * 2,
        out_specs=pl.BlockSpec(memory_space=pltpu.SMEM),
    )(jnp.stack([place["dp"], place["micro"], place["column"], place["seq"] % 2]), table)


def pick_entries(index, entries, out, also=True):
    for n, entry in enumerate(entries):

        @pl.when((index == n) & also)
        def _():
            out[...] = entry[...]


def entries_of(micro, refs):
    return [ref.at[micro, n] for ref in refs for n in range(2)]


def pick_sent_kernel(first, route_ref, pair_ref, came_ref, sent_ref):
    for micro in range(2):
        for k in range(2):
            entries = entries_of(micro, (pair_ref, came_ref))
            pick_entries(route_ref[first + micro, k], entries, sent_ref.at[micro, k])


def pick_last_kernel(first, route_ref, pair_ref, came_ref, far_ref, own_ref, partner_ref):
    for micro in range(2):
        entries = entries_of(micro, (pair_ref, came_ref, far_ref))
        for k, out_ref in enumerate((own_ref, partner_ref)):
            pick_entries(route_ref[first + micro, 2 + k], entries, out_ref.at[micro])


def pick(body, routes, shapes, *held):
    vmem = pl.BlockSpec(memory_space=pltpu.VMEM)
    return pl.pallas_call(
        body,
        out_shape=[jax.ShapeDtypeStruct(shape, BF16) for shape in shapes],
        in_specs=[pl.BlockSpec(memory_space=pltpu.SMEM)] + [vmem] * len(held),
        out_specs=[vmem] * len(shapes),
    )(routes, *held)


def core_pair(items, place):
    low_core = place["dp"] % 2 == 0
    half = items.shape[1] // 2
    mine, give = swapped(jnp.logical_not(low_core), (items[:, :half], items[:, half:]))
    return jnp.stack([mine, flip_dp(give, 1)], axis=1)


def cotangent_stages(pair, routes, place):
    low_core = place["dp"] % 2 == 0
    pair = (yield [pair])[0]
    came = (yield [flip_step(pair, 0)])[0]
    (sent,) = yield pick(functools.partial(pick_sent_kernel, 0), routes, [pair.shape], pair, came)
    far = flip_step(sent, 1)
    yield []
    far = (yield [far])[0]
    body = functools.partial(pick_last_kernel, 0)
    own, partner = pick(body, routes, [pair[:, 0].shape] * 2, pair, came, far)
    blocks = jnp.concatenate(swapped(jnp.logical_not(low_core), (own, flip_dp(partner, 1))), axis=1)
    one, two = to_stretch(blocks, place)
    one = (yield [one])[0]
    two = (yield [two])[0]
    return one, two


def output_stages(out, routes, place):
    block = out.shape[0] // 2
    one, two = from_stretch(out[:block], out[block:], place)
    one = (yield [one])[0]
    two = (yield [two])[0]
    blocks = jnp.stack(swapped(place["seq"] % 2 == 1, (one, two)))
    tops, bottoms = blocks[:, : block // 2], blocks[:, block // 2 :]
    mine, give = swapped(place["dp"] % 2 == 1, (tops, bottoms))
    got = (yield [flip_dp(give, 1)])[0]
    pair = jnp.stack([mine, got], axis=1)
    came = (yield [flip_step(pair, 0)])[0]
    (sent,) = pick(functools.partial(pick_sent_kernel, 2), routes, [pair.shape], pair, came)
    far = (yield [flip_step(sent, 1)])[0]
    body = functools.partial(pick_last_kernel, 2)
    own, partner = pick(body, routes, [mine.shape] * 2, pair, came, far)
    back = (yield [flip_dp(partner, 1)])[0]
    return jnp.concatenate(swapped(place["dp"] % 2 == 1, (own, back)), axis=1)


def deal_gathered(items, source):
    every = lax.all_gather(items, "dp", axis=0)
    picked = [
        lax.dynamic_index_in_dim(every[:, m], source[m], 0, keepdims=False) for m in range(2)
    ]
    return jnp.stack(picked)


def dot(a, b, ca=1, cb=0):
    return lax.dot_general(a, b, (((ca,), (cb,)), ((), ())), preferred_element_type=F32)


def two_parts(x):
    high = x.astype(BF16)
    return high, (x - high.astype(F32)).astype(BF16)


def running_sum(x, reverse=False):
    rows = lax.broadcasted_iota(jnp.int32, (CHUNK, CHUNK), 0)
    cols = lax.broadcasted_iota(jnp.int32, (CHUNK, CHUNK), 1)
    reach = (rows <= cols) if reverse else (rows >= cols)
    reach = jnp.where(reach, 1.0, 0.0).astype(BF16)
    high, rest = two_parts(x)
    middle, low = two_parts(x - high.astype(F32))
    del rest
    return dot(reach, high) + dot(reach, middle) + dot(reach, low)


def fill_expander(expand_ref):
    head = lax.broadcasted_iota(jnp.int32, (LANES, INNER), 0)
    col = lax.broadcasted_iota(jnp.int32, (LANES, INNER), 1)
    one = jnp.where(col // HDIM == head, 1.0, 0.0).astype(BF16)
    expand_ref[0:LANES, :] = one
    expand_ref[LANES : 2 * LANES, :] = one


def head_sums(prod, tile):
    lane = lax.broadcasted_iota(jnp.int32, (LANES, LANES), 0)
    head = lax.broadcasted_iota(jnp.int32, (LANES, LANES), 1)
    one = jnp.where(2 * tile + lane // HDIM == head, 1.0, 0.0).astype(BF16)
    high, low = two_parts(prod)
    return dot(jnp.concatenate([high, low], axis=1), jnp.concatenate([one, one], axis=0))


def start_pieces(dp, pieces, plan, target, sem, rows):
    copies = []
    masks, spots = plan
    for piece, (even, odd) in zip(pieces, masks):
        for n in range(len(even)):
            mask = jnp.where(jnp.bitwise_and(dp, 1) == 0, even[n], odd[n])
            for source, scale, source_col, col, width in spots:
                first = pl.multiple_of(jnp.bitwise_xor(dp, mask) * (rows * scale), 8)
                copy = pltpu.make_async_copy(
                    piece.at[n, pl.ds(source, rows * scale), pl.ds(source_col, width)],
                    target.at[pl.ds(first, rows * scale), pl.ds(col, width)],
                    sem.at[len(copies)],
                )
                copy.start()
                copies.append(copy)
    return copies


def wait_all(copies):
    for copy in copies:
        copy.wait()


def piece_count(plan):
    masks, spots = plan
    return sum(len(even) for even, _ in masks) * len(spots)


def gain_row(w_ref):
    return w_ref[:, CHANNELS:].astype(F32).T[HEADS : HEADS + 1]


def join_blocks(late, one_ref, two_ref, out_ref, start):
    rows = one_ref.shape[0]
    for turn, pair in enumerate(((one_ref, two_ref), (two_ref, one_ref))):

        @pl.when(late == turn)
        def _():
            for n, block_ref in enumerate(pair):
                out_ref[start + n * rows : start + (n + 1) * rows, :] = block_ref[...]


def project_kernel(plan, rows, scal, one_ref, two_ref, halo_ref, cw_ref, cb_ref, dl_ref, sb_ref, *refs):
    count = PIECES
    pieces = refs[:count]
    x_ref, nh_ref, cext_ref, act_ref, step_ref, sig_ref, cum_ref = refs[count : count + 7]
    w_ref, proj_ref, sem = refs[count + 7 :]
    copies = start_pieces(scal[0], pieces, plan, w_ref, sem, rows)
    total = x_ref.shape[0]
    length = total - HALO
    x_ref[0:HALO, :] = halo_ref[...]
    join_blocks(scal[2], one_ref, two_ref, x_ref, HALO)
    chunks = length // CHUNK

    tall = 3 * HALO if total % (3 * HALO) == 0 else HALO

    model = x_ref.shape[1]

    def scaled(i, carry):
        at = pl.ds(pl.multiple_of(i * tall, tall), tall)
        u = x_ref[at, :].astype(F32)
        proj_ref[at, 0:model] = u * lax.rsqrt(jnp.mean(u * u, axis=1, keepdims=True) + EPSILON)
        return carry

    def norm(i, carry):
        at = pl.ds(pl.multiple_of(i * tall, tall), tall)
        nh_ref[at, :] = (proj_ref[at, 0:model] * gain).astype(BF16)
        return carry

    lax.fori_loop(0, total // tall, scaled, 0)
    wait_all(copies)
    gain = gain_row(w_ref)
    lax.fori_loop(0, total // tall, norm, 0)

    def project(j, carry):
        at = pl.ds(pl.multiple_of(j * 384, 384), 384)
        proj_ref[:, at] = dot(nh_ref[...], w_ref[:, at])
        return carry

    lax.fori_loop(0, WIDTH // 384, project, 0)

    def conv(idx, carry):
        i, j = idx // (CHANNELS // LANES), idx % (CHANNELS // LANES)
        cols = pl.ds(pl.multiple_of(j * LANES, LANES), LANES)
        first = pl.multiple_of(i * CHUNK, CHUNK)
        part = proj_ref[pl.ds(first, CHUNK + HALO), cols]
        weights = cw_ref[:, cols]
        out = cb_ref[0:1, cols] + weights[KCONV - 1 : KCONV] * part[HALO:]
        for k in range(KCONV - 1):
            out = out + weights[k : k + 1] * pltpu.roll(part, KCONV - 1 - k, 0)[HALO:]
        act_ref[pl.ds(first, CHUNK), cols] = (out * jax.nn.sigmoid(out)).astype(BF16)
        cext_ref[pl.ds(first + HALO, CHUNK), cols] = part[HALO:].astype(BF16)
        return carry

    lax.fori_loop(0, chunks * (CHANNELS // LANES), conv, 0)
    cext_ref[0:HALO, :] = proj_ref[0:HALO, 0:CHANNELS].astype(BF16)
    lane = lax.broadcasted_iota(jnp.int32, (CHUNK, LANES), 1)
    row = lax.broadcasted_iota(jnp.int32, (CHUNK, LANES), 0)
    rate = -jnp.exp(dl_ref[0:1, :])
    for i in range(chunks):
        at = pl.ds(i * CHUNK, CHUNK)
        pre = proj_ref[pl.ds(HALO + i * CHUNK, CHUNK), pl.ds(CHANNELS, LANES)] + sb_ref[0:1, :]
        live = (row + i * CHUNK < scal[1]) & (lane < HEADS)
        soft = jnp.maximum(pre, 0.0) + jnp.log1p(jnp.exp(-jnp.abs(pre)))
        step = jnp.where(live, soft, 0.0)
        step_ref[at, :] = step
        sig_ref[at, :] = jnp.where(live, jax.nn.sigmoid(pre), 0.0)
        cum_ref[at, :] = running_sum(rate * step)


def mixing_parts(cum, cum_rows, step_rows, head):
    gap = jnp.minimum(cum[:, head : head + 1] - cum_rows[head : head + 1, :], 0.0)
    return jnp.exp(gap) * step_rows[head : head + 1, :]


def causal_tile():
    rows = lax.broadcasted_iota(jnp.int32, (CHUNK, CHUNK), 0)
    cols = lax.broadcasted_iota(jnp.int32, (CHUNK, CHUNK), 1)
    return rows >= cols


def local_kernel(act_ref, step_ref, cum_ref, local_ref, upd_ref, tot_ref, sum_ref, expand_ref):
    chunks = act_ref.shape[0] // CHUNK
    left = lax.broadcasted_iota(jnp.int32, (CHUNK, LANES), 1) < HDIM
    fill_expander(expand_ref)
    after = jnp.zeros((1, LANES), F32)
    for i in range(chunks - 1, -1, -1):
        at = pl.ds(i * CHUNK, CHUNK)
        cum = cum_ref[at, :]
        last = cum[CHUNK - 1 : CHUNK]
        weight = jnp.exp(last + after - cum) * step_ref[at, :]
        wide = dot(jnp.concatenate(two_parts(weight), axis=1), expand_ref[...])
        values = act_ref[at, 0:INNER].astype(F32)
        keys = act_ref[at, INNER : INNER + STATE]
        update = dot(keys, (wide * values).astype(BF16), 0, 0)
        sum_ref[...] = update if i == chunks - 1 else sum_ref[...] + update
        after = after + last
    upd_ref[...] = sum_ref[...].astype(BF16)
    tot_ref[...] = jnp.broadcast_to(after, tot_ref.shape)

    def chunk(c, carry):
        at = pl.ds(pl.multiple_of(c * CHUNK, CHUNK), CHUNK)
        in_keys = act_ref[at, INNER : INNER + STATE]
        out_keys = act_ref[at, INNER + STATE : CHANNELS]
        affinity = jnp.where(causal_tile(), dot(out_keys, in_keys, 1, 1), 0.0)
        cum = cum_ref[at, :]
        cum_rows = cum.T
        step_rows = step_ref[at, :].T
        for tile in range(INNER // LANES):
            cols = slice(tile * LANES, (tile + 1) * LANES)
            mixing = [
                (affinity * mixing_parts(cum, cum_rows, step_rows, 2 * tile + n)).astype(BF16)
                for n in range(2)
            ]
            values = act_ref[at, cols]
            zero = jnp.zeros_like(values)
            apart = jnp.concatenate(
                [jnp.where(left, values, zero), jnp.where(left, zero, values)], axis=0
            )
            local_ref[at, cols] = dot(jnp.concatenate(mixing, axis=1), apart)
        return carry

    lax.fori_loop(0, chunks, chunk, 0)


def core_kernel(local_ref, act_ref, step_ref, cum_ref, state_ref, core_ref, states_ref, state_s, wide_ref, expand_ref):
    chunks = act_ref.shape[0] // CHUNK
    fill_expander(expand_ref)
    state_s[...] = state_ref[...].astype(F32)

    def chunk(c, carry):
        at = pl.ds(pl.multiple_of(c * CHUNK, CHUNK), CHUNK)
        in_keys = act_ref[at, INNER : INNER + STATE]
        out_keys = act_ref[at, INNER + STATE : CHANNELS]
        cum = cum_ref[at, :]
        last = cum[CHUNK - 1 : CHUNK]
        weight = jnp.exp(last - cum) * step_ref[at, :]
        small = jnp.concatenate([jnp.exp(cum), weight, jnp.broadcast_to(jnp.exp(last), (8, LANES))], axis=0)
        wide_ref[...] = dot(jnp.concatenate(two_parts(small), axis=1), expand_ref[...])
        state_b = state_s[...].astype(BF16)
        states_ref[c] = state_b
        for tile in range(INNER // LANES):
            cols = slice(tile * LANES, (tile + 1) * LANES)
            values = act_ref[at, cols].astype(F32)
            core_ref[at, cols] = local_ref[at, cols] + wide_ref[0:CHUNK, cols] * dot(out_keys, state_b[:, cols])
            weighted = (wide_ref[CHUNK : 2 * CHUNK, cols] * values).astype(BF16)
            state_s[:, cols] = wide_ref[2 * CHUNK : 2 * CHUNK + 1, cols] * state_s[:, cols] + dot(
                in_keys, weighted, 0, 0
            )
        return carry

    lax.fori_loop(0, chunks, chunk, 0)


def middle_kernel(gate_plan, plan, rows, scal, core_ref, act_ref, cum_ref, nh_ref, x_ref, one_ref, two_ref, skip_ref,
                  *refs):
    count = PIECES
    c_ref, out_ref, gn_ref, dgate_ref, gcore_ref, rowq_ref, lsg_ref, gskip_ref = refs[count : count + 8]
    (w_ref, wg_ref, gate_ref, gain_ref, mc_ref, gno_ref, wide_ref, mixed_ref, sig_ref, gated_ref, acc_ref, expand_ref, gate_sem,
     sem) = refs[count + 8 :]
    gate_copies = start_pieces(scal[0], refs[:count], gate_plan, wg_ref, gate_sem, rows)
    copies = start_pieces(scal[0], refs[:count], plan, w_ref, sem, rows)
    length = act_ref.shape[0]
    chunks = length // CHUNK
    tiles = INNER // LANES
    model = c_ref.shape[1]
    join_blocks(scal[2], one_ref, two_ref, c_ref, 0)
    fill_expander(expand_ref)

    def mask(i, carry):
        at = pl.ds(pl.multiple_of(i * CHUNK, CHUNK), CHUNK)
        row = lax.broadcasted_iota(jnp.int32, (CHUNK, model), 0) + i * CHUNK
        c = c_ref[at, :]
        mc_ref[at, :] = jnp.where(row < scal[1], c.astype(F32), 0.0).astype(BF16)
        return carry

    lax.fori_loop(0, chunks, mask, 0)
    wait_all(gate_copies)

    def project(j, carry):
        at = pl.ds(pl.multiple_of(j * 384, 384), 384)
        gate_ref[:, at] = dot(nh_ref[HALO:, :], wg_ref[:, at])
        return carry

    lax.fori_loop(0, INNER // 384, project, 0)
    wait_all(copies)

    def back_project(j, carry):
        at = pl.ds(pl.multiple_of(j * 384, 384), 384)
        gno_ref[:, at] = dot(mc_ref[...], w_ref[at, 0:model], 1, 1)
        return carry

    lax.fori_loop(0, INNER // 384, back_project, 0)
    gain_ref[...] = w_ref[:, model:].astype(F32).T[0:8]
    acc_ref[...] = jnp.zeros_like(acc_ref)
    gskip_ref[...] = jnp.zeros_like(gskip_ref)

    def chunk(c, before):
        at = pl.ds(pl.multiple_of(c * CHUNK, CHUNK), CHUNK)
        out_keys = act_ref[at, INNER + STATE : CHANNELS]
        cum = cum_ref[at, :]
        wide_ref[...] = dot(jnp.concatenate(two_parts(jnp.exp(cum + before)), axis=1), expand_ref[...])
        squares = jnp.zeros((CHUNK, LANES), F32)
        for tile in range(tiles):
            cols = slice(tile * LANES, (tile + 1) * LANES)
            mixed = core_ref[at, cols] + skip_ref[0:1, cols] * act_ref[at, cols].astype(F32)
            mixed_ref[:, cols] = mixed
            gate = gate_ref[at, cols]
            sig = jax.nn.sigmoid(gate)
            gated = mixed * (gate * sig)
            sig_ref[:, cols] = sig
            gated_ref[:, cols] = gated
            squares = squares + gated * gated
        scale = lax.rsqrt(jnp.sum(squares, axis=1, keepdims=True) / INNER + EPSILON)
        products = jnp.zeros((CHUNK, LANES), F32)
        for tile in range(tiles):
            cols = slice(tile * LANES, (tile + 1) * LANES)
            gn = gated_ref[:, cols] * scale
            gain = gain_ref[0:1, cols]
            gn_ref[at, cols] = (gn * gain).astype(BF16)
            products = products + gn * (gno_ref[at, cols] * gain)
        mean = jnp.sum(products, axis=1, keepdims=True) / INNER
        rowq = jnp.zeros((CHUNK, LANES), F32)
        for tile in range(tiles):
            cols = slice(tile * LANES, (tile + 1) * LANES)
            gate = gate_ref[at, cols]
            sig = sig_ref[:, cols]
            silu = gate * sig
            mixed = mixed_ref[:, cols]
            dgated = scale * (gno_ref[at, cols] * gain_ref[0:1, cols] - (gated_ref[:, cols] * scale) * mean)
            g = dgated * silu
            dgate_ref[at, cols] = (dgated * mixed * (sig * (1.0 + gate * (1.0 - sig)))).astype(BF16)
            gcore = g.astype(BF16)
            gcore_ref[at, cols] = gcore
            values = act_ref[at, cols].astype(F32)
            gskip_ref[:, cols] = gskip_ref[:, cols] + jnp.sum(
                (g * values).reshape(CHUNK // 8, 8, LANES), axis=0
            )
            gcore_f = gcore.astype(F32)
            rowq = rowq + head_sums(gcore_f * core_ref[at, cols], tile)
            scaled = (wide_ref[:, cols] * gcore_f).astype(BF16)
            acc_ref[:, cols] = acc_ref[:, cols] + dot(out_keys, scaled, 0, 0)
        rowq_ref[at, :] = rowq
        return before + cum[CHUNK - 1 : CHUNK]

    lax.fori_loop(0, chunks, chunk, jnp.zeros((1, LANES), F32))
    lsg_ref[...] = acc_ref[...].astype(BF16)

    def finish(i, carry):
        at = pl.ds(pl.multiple_of(i * CHUNK, CHUNK), CHUNK)
        row = lax.broadcasted_iota(jnp.int32, (CHUNK, model), 0) + i * CHUNK
        u = x_ref[pl.ds(pl.multiple_of(i * CHUNK + HALO, HALO), CHUNK), :].astype(F32)
        out_ref[at, :] = (u + jnp.where(row < scal[1], gno_ref[at, 0:model], 0.0)).astype(BF16)
        return carry

    for j in range(2):
        cols = slice(j * model // 2, (j + 1) * model // 2)
        gno_ref[:, cols] = dot(gn_ref[...], w_ref[:, cols])
    lax.fori_loop(0, chunks, finish, 0)


def put_block(dp, devices, block, keep_ref, send_ref, start, cols, part):
    steps = len(step_bits(devices))
    away = jnp.bitwise_xor(dp, block)
    backward = away // 2
    forward = jnp.int32(0)
    for k in range(steps):
        forward = forward * 2 + jnp.bitwise_and(jnp.right_shift(backward, k), 1)
    even = jnp.bitwise_and(dp, 1) == 0
    rows = part.shape[0]

    @pl.when(away % 2 == 0)
    def _():
        keep_ref[jnp.where(even, forward, backward), start : start + rows, cols] = part

    @pl.when(away % 2 == 1)
    def _():
        send_ref[jnp.where(even, backward, forward), start : start + rows, cols] = part


def early_kernel(rows, devices, scal, gn_ref, c_ref, nh_ref, dgate_ref, keep_ref, send_ref, mc_ref):
    length, model = c_ref.shape
    chunks = length // CHUNK

    def mask(i, carry):
        at = pl.ds(pl.multiple_of(i * CHUNK, CHUNK), CHUNK)
        row = lax.broadcasted_iota(jnp.int32, (CHUNK, model), 0) + i * CHUNK
        mc_ref[at, :] = jnp.where(row < scal[1], c_ref[at, :].astype(F32), 0.0).astype(BF16)
        return carry

    lax.fori_loop(0, chunks, mask, 0)
    half = model // 2
    for j in range(2 * INNER // model):
        part = dot(nh_ref[HALO:, :], dgate_ref[:, j * half : (j + 1) * half], 0, 0).astype(BF16)
        start = (j // 2) * rows
        cols = slice((j % 2) * half, (j % 2 + 1) * half)
        for block in range(devices):
            put_block(
                scal[0], devices, block, keep_ref, send_ref, start, cols, part[block * rows : (block + 1) * rows]
            )
    for j in range(INNER // half):
        part = dot(gn_ref[:, j * half : (j + 1) * half], mc_ref[...], 0, 0).astype(BF16)
        each = half // (2 * rows)
        for n in range(each):
            put_block(
                scal[0], devices, j * each + n, keep_ref, send_ref, 2 * rows, slice(0, model),
                part[n * 2 * rows : (n + 1) * 2 * rows],
            )


def local_back_kernel(plan, rows, scal, act_ref, step_ref, cum_ref, gcore_ref, dgate_ref, *refs):
    count = PIECES
    pieces = refs[:count]
    gvl_ref, gk_ref, gng_ref, w_ref, sem = refs[count:]
    copies = start_pieces(scal[0], pieces, plan, w_ref, sem, rows)
    chunks = act_ref.shape[0] // CHUNK
    half = gng_ref.shape[1] // 2
    left = lax.broadcasted_iota(jnp.int32, (CHUNK, LANES), 1) < HDIM

    def chunk(c, carry):
        at = pl.ds(pl.multiple_of(c * CHUNK, CHUNK), CHUNK)
        in_keys = act_ref[at, INNER : INNER + STATE]
        out_keys = act_ref[at, INNER + STATE : CHANNELS]
        affinity = jnp.where(causal_tile(), dot(out_keys, in_keys, 1, 1), 0.0)
        cum = cum_ref[at, :]
        cum_rows = cum.T
        step_rows = step_ref[at, :].T
        gaff = jnp.zeros((CHUNK, CHUNK), F32)
        for tile in range(INNER // LANES):
            cols = slice(tile * LANES, (tile + 1) * LANES)
            values = act_ref[at, cols]
            grads = gcore_ref[at, cols]
            zero = jnp.zeros_like(grads)
            apart = jnp.concatenate(
                [jnp.where(left, grads, zero), jnp.where(left, zero, grads)], axis=0
            )
            gmix = dot(apart, values, 1, 1)
            mixing = []
            for n in range(2):
                weight = mixing_parts(cum, cum_rows, step_rows, 2 * tile + n)
                gaff = gaff + gmix[n * CHUNK : (n + 1) * CHUNK] * weight
                mixing.append((affinity * weight).astype(BF16))
            back = dot(jnp.concatenate(mixing, axis=1), grads, 0, 0)
            gvl_ref[at, cols] = jnp.where(left, back[0:CHUNK], back[CHUNK:])
        gaff = jnp.where(causal_tile(), gaff, 0.0).astype(BF16)
        gk_ref[at, 0:STATE] = dot(gaff, out_keys, 0, 0)
        gk_ref[at, STATE : 2 * STATE] = dot(gaff, in_keys)
        return carry

    lax.fori_loop(0, chunks, chunk, 0)
    wait_all(copies)
    for j in range(2):
        cols = slice(j * half, (j + 1) * half)
        gng_ref[:, cols] = dot(dgate_ref[...], w_ref[cols, :], 1, 1)


def scan_back_kernel(act_ref, step_ref, sig_ref, cum_ref, gcore_ref, gvl_ref, gk_ref, rowq_ref, states_ref,
                     gout_ref, gskip_ref, skip_ref, cext_ref, cw_ref, cb_ref, dl_ref, gconv_ref, head_ref, graw_ref, small_ref,
                     gstate_ref, wide_ref, gact_ref, expand_ref):
    chunks = act_ref.shape[0] // CHUNK
    tiles = INNER // LANES
    fill_expander(expand_ref)
    gstate_ref[...] = gout_ref[...].astype(F32)
    small_ref[...] = jnp.zeros_like(small_ref)
    small_ref[6:7, 0:INNER] = jnp.sum(gskip_ref[...], axis=0, keepdims=True)
    rate = -jnp.exp(dl_ref[0:1, :])
    end = lax.broadcasted_iota(jnp.int32, (CHUNK, LANES), 0) == CHUNK - 1

    def chunk(n, carry):
        gdecay, gbias = carry
        c = chunks - 1 - n
        at = pl.ds(pl.multiple_of(c * CHUNK, CHUNK), CHUNK)
        in_keys = act_ref[at, INNER : INNER + STATE]
        out_keys = act_ref[at, INNER + STATE : CHANNELS]
        cum = cum_ref[at, :]
        step = step_ref[at, :]
        sig = sig_ref[at, :]
        last = cum[CHUNK - 1 : CHUNK]
        small = jnp.concatenate(
            [jnp.exp(cum), jnp.exp(last - cum) * step, jnp.broadcast_to(jnp.exp(last), (8, LANES))], axis=0
        )
        wide_ref[...] = dot(jnp.concatenate(two_parts(small), axis=1), expand_ref[...])
        colq = jnp.zeros((CHUNK, LANES), F32)
        ends = jnp.zeros((8, LANES), F32)
        gin = gk_ref[at, 0:STATE]
        gout = gk_ref[at, STATE : 2 * STATE]
        for tile in range(tiles):
            cols = slice(tile * LANES, (tile + 1) * LANES)
            values = act_ref[at, cols].astype(F32)
            grads = gcore_ref[at, cols].astype(F32)
            gstate = gstate_ref[:, cols]
            gstate_b = gstate.astype(BF16)
            state = states_ref[c, :, cols]
            weight = wide_ref[CHUNK : 2 * CHUNK, cols]
            decay = wide_ref[2 * CHUNK : 2 * CHUNK + 1, cols]
            gvs = weight * dot(in_keys, gstate_b)
            gvalues = gvl_ref[at, cols] + gvs
            colq = colq + head_sums(values * gvalues, tile)
            passed = jnp.sum((values * gvs).reshape(CHUNK // 8, 8, LANES), axis=0) + decay * jnp.sum(
                (gstate * state.astype(F32)).reshape(STATE // 8, 8, LANES), axis=0
            )
            ends = ends + head_sums(passed, tile)
            gin = gin + dot((weight * values).astype(BF16), gstate_b, 1, 1)
            scaled = (wide_ref[0:CHUNK, cols] * grads).astype(BF16)
            gout = gout + dot(scaled, state, 1, 1)
            gstate_ref[:, cols] = decay * gstate + dot(out_keys, scaled, 0, 0)
            gact_ref[:, cols] = gvalues + skip_ref[0:1, cols] * grads
        gact_ref[:, INNER : INNER + STATE] = gin
        gact_ref[:, INNER + STATE : CHANNELS] = gout
        gcum = rowq_ref[at, :] - colq
        gcum = gcum + jnp.where(end, jnp.sum(ends, axis=0, keepdims=True), 0.0)
        glog = running_sum(gcum, reverse=True)
        gdecay = gdecay + jnp.sum((glog * (rate * step)).reshape(CHUNK // 8, 8, LANES), axis=0)
        ratio = jnp.where(step > 0.0, sig / jnp.where(step > 0.0, step, 1.0), 0.0)
        graw = colq * ratio + rate * glog * sig
        gbias = gbias + jnp.sum(graw.reshape(CHUNK // 8, 8, LANES), axis=0)
        first = pl.multiple_of(c * CHUNK, CHUNK)
        graw_ref[at, :] = graw.astype(BF16)
        for tile in range(CHANNELS // LANES):
            cols = slice(tile * LANES, (tile + 1) * LANES)
            part = cext_ref[pl.ds(first, CHUNK + HALO), cols].astype(F32)
            moved = [pltpu.roll(part, KCONV - 1 - k, 0)[HALO:] for k in range(KCONV - 1)] + [part[HALO:]]
            out = cb_ref[0:1, cols]
            for k in range(KCONV):
                out = out + cw_ref[k : k + 1, cols] * moved[k]
            sc = jax.nn.sigmoid(out)
            gconv = gact_ref[:, cols] * (sc * (1.0 + out * (1.0 - sc)))
            gconv_ref[at, cols] = gconv
            for k in range(KCONV):
                small_ref[k : k + 1, cols] = small_ref[k : k + 1, cols] + jnp.sum(
                    gconv * moved[k], axis=0, keepdims=True
                )
            small_ref[4:5, cols] = small_ref[4:5, cols] + jnp.sum(gconv, axis=0, keepdims=True)
        return gdecay, gbias

    zero = jnp.zeros((8, LANES), F32)
    gdecay, gbias = lax.fori_loop(0, chunks, chunk, (zero, zero))
    small_ref[5:6, 0:LANES] = jnp.sum(gdecay, axis=0, keepdims=True)
    small_ref[5:6, LANES : 2 * LANES] = jnp.sum(gbias, axis=0, keepdims=True)
    head_ref[...] = gconv_ref[0:HALO, :]


def conv_back_kernel(rows, devices, scal, gconv_ref, ahead_ref, graw_ref, nh_ref, cw_ref, gproj_ref, keep_ref,
                     send_ref):
    length = gconv_ref.shape[0]
    tall = 4 * HALO
    gproj_ref[:, CHANNELS:] = graw_ref[...]

    def rows_back(first, part_of):
        for tile in range(CHANNELS // LANES):
            cols = slice(tile * LANES, (tile + 1) * LANES)
            part = part_of(cols)
            total = cw_ref[KCONV - 1 : KCONV, cols] * part[:tall]
            for k in range(KCONV - 1):
                ahead = pltpu.roll(part, part.shape[0] - (KCONV - 1 - k), 0)[:tall]
                total = total + cw_ref[k : k + 1, cols] * ahead
            gproj_ref[pl.ds(first, tall), cols] = total.astype(BF16)

    def conv_back(i, carry):
        first = pl.multiple_of(i * tall, tall)
        rows_back(first, lambda cols: gconv_ref[pl.ds(first, tall + 8), cols])
        return carry

    lax.fori_loop(0, length // tall - 1, conv_back, 0)
    rows_back(
        length - tall,
        lambda cols: jnp.concatenate([gconv_ref[length - tall :, cols], ahead_ref[0:8, cols]], axis=0),
    )
    for j in range(WIDTH // 384):
        cols = slice(j * 384, (j + 1) * 384)
        part = dot(nh_ref[HALO:, :], gproj_ref[:, cols], 0, 0).astype(BF16)
        for block in range(devices):
            put_block(
                scal[0], devices, block, keep_ref, send_ref, 0, cols, part[block * rows : (block + 1) * rows]
            )


def token_back_kernel(plan, rows, scal, gproj_ref, gng_ref, x_ref, c_ref, *refs):
    count = PIECES
    pieces = refs[:count]
    gtok_ref, w_ref, acc_ref, hat_ref, scale_ref, sem = refs[count:]
    copies = start_pieces(scal[0], pieces, plan, w_ref, sem, rows)
    length, model = c_ref.shape
    tall = 4 * HALO

    def scaled(i, carry):
        at = pl.ds(pl.multiple_of(i * tall, tall), tall)
        u = x_ref[pl.ds(pl.multiple_of(i * tall + HALO, HALO), tall), :].astype(F32)
        scale = lax.rsqrt(jnp.mean(u * u, axis=1, keepdims=True) + EPSILON)
        hat_ref[at, :] = u * scale
        scale_ref[at, :] = jnp.broadcast_to(scale, (tall, LANES))
        return carry

    lax.fori_loop(0, length // tall, scaled, 0)
    wait_all(copies)
    for j in range(2):
        cols = slice(j * model // 2, (j + 1) * model // 2)
        acc_ref[:, cols] = dot(gproj_ref[...], w_ref[cols, :], 1, 1) + gng_ref[:, cols]
    gain = gain_row(w_ref)

    def norm_back(i, carry):
        at = pl.ds(pl.multiple_of(i * tall, tall), tall)
        nh = hat_ref[at, :]
        g = acc_ref[at, :] * gain
        grads = scale_ref[at, 0:1] * (g - nh * jnp.mean(g * nh, axis=1, keepdims=True))
        gtok_ref[at, :] = (grads + c_ref[at, :].astype(F32)).astype(BF16)
        return carry

    lax.fori_loop(0, length // tall, norm_back, 0)


def call(body, scal, whole, pieces, outs, scratch):
    first = [] if scal is None else [scal]
    smem = pl.BlockSpec(memory_space=pltpu.SMEM)
    vmem = pl.BlockSpec(memory_space=pltpu.VMEM)
    return list(pl.pallas_call(
        body,
        out_shape=[jax.ShapeDtypeStruct(shape, kind) for shape, kind in outs],
        in_specs=[smem] * len(first) + [vmem] * len(whole) + [pl.BlockSpec(memory_space=pl.ANY)] * len(pieces),
        out_specs=[vmem] * len(outs),
        scratch_shapes=scratch,
        compiler_params=pltpu.CompilerParams(vmem_limit_bytes=VMEM_LIMIT),
    )(*first, *whole, *pieces))


def lane_row(vector):
    return jnp.pad(vector, (0, LANES - vector.shape[0]))[None]


def per_device(tokens, lengths, dealing, cotangent, in_weight, out_weight, norm_gain, gate_gain, conv_weight,
               conv_bias, decay_log, step_bias, skip_gain):
    dp, seq = lax.axis_index("dp"), lax.axis_index("seq")
    devices, size = lax.axis_size("dp"), lax.axis_size("seq")
    group = size // 2
    lin = seq * 2 + dp % 2
    holder = lin // group
    place = {"dp": dp, "seq": seq, "micro": holder // 2, "column": holder % 2, "turn": lin % group}
    block_len, model = tokens.shape[2:]
    length = 2 * block_len
    shard_rows = in_weight.shape[0]
    rows = shard_rows * size
    tok = tokens[:, 0]
    cot = cotangent[:, 0]

    gains = jnp.concatenate(
        [norm_gain[:, None], jnp.swapaxes(gate_gain.reshape(2, shard_rows), 0, 1)], axis=1
    )
    conv_shard = jnp.concatenate([in_weight[:, INNER:], gains], axis=1)
    conv_shard = jnp.pad(conv_shard, ((0, 0), (0, WIDTH - conv_shard.shape[1])))
    rest_shard = jnp.concatenate(
        [in_weight[:, :INNER], out_weight[:shard_rows], out_weight[shard_rows:]], axis=1
    )
    masks = spread_masks(devices)
    conv_plan = (masks, [(0, 1, 0, 0, WIDTH)])
    gate_plan = (masks, [(0, 1, 0, 0, model), (rows, 1, 0, model, model)])
    out_plan = (masks, [(0, 2, model, 0, model + LANES)])

    dealt = devices == 8
    if dealt:
        routes = make_routes(place, dp_table(jnp.concatenate([dealing[:, 0], lengths[:, 0]])))
        cot_chain = Chain(cotangent_stages(core_pair(cot, place), routes, place))
        own_length = routes[4, 0]
        moving = [cot_chain]
    else:
        every = lax.all_gather(jnp.concatenate([dealing, lengths], axis=0)[:, 0], "dp", axis=0)
        goals = every[:, :2]
        source_of_out = jnp.argmax(goals == dp, axis=0)
        cot_given = deal_gathered(cot, dealing[:, 0])
        mate = lax.dynamic_index_in_dim(every, dp - dp % 2 + place["column"], 0, keepdims=False)
        own_length = jnp.where(place["micro"] == 0, mate[2], mate[3])
        moving = []

    taps = jnp.pad(conv_weight, ((0, 8 - KCONV), (0, 0)))
    skip_row = jnp.repeat(skip_gain, HDIM)[None]
    n_valid = jnp.clip(own_length - place["turn"] * length, 0, length)
    scal = jnp.stack([dp, n_valid, place["micro"]])
    rows_of = (taps, conv_bias[None], lane_row(decay_log), lane_row(step_bias), skip_row, scal)

    shards = Chain(seq_stages(conv_shard, place))
    tok = advance(swapped(place["seq"] % 2 == 1, tok), shards, *moving)
    conv_z = shards.value
    conv = Chain(spread_stages(conv_z.reshape(rows, WIDTH)))
    one, two = send_stretch(tok)
    one, two, rows_of, rest_shard = advance((one, two, rows_of, rest_shard), conv, *moving)
    taps, conv_bias_row, decay_row, bias_row, skip_row, scal = rows_of
    late = place["micro"] == 1
    tail = jnp.where(late, one[block_len - HALO :], two[block_len - HALO :])
    halo = lax.ppermute(tail, BOTH, neighbour_pairs(1))
    one, two, halo = advance((one, two, halo), conv, *moving)
    shards = Chain(seq_stages(rest_shard, place))
    while conv.pending is not None:
        halo = advance(halo, conv, *moving)
    conv_pieces = conv.value
    gain_rows = jnp.swapaxes(conv_z[:, :, CHANNELS + HEADS + 1 : CHANNELS + HEADS + 3], 1, 2)
    gain_rows = jnp.pad(gain_rows.reshape(2 * rows, 1), ((0, 0), (0, LANES - 1)))
    moving = moving + [shards]
    def sems(plan):
        return pltpu.SemaphoreType.DMA((piece_count(plan),))

    wide = (length, INNER)
    made = call(
        functools.partial(project_kernel, conv_plan, rows),
        scal,
        [one, two, halo, taps, conv_bias_row, decay_row, bias_row],
        conv_pieces,
        [((length + HALO, model), BF16)] * 2 + [((length + HALO, CHANNELS), BF16), ((length, CHANNELS), BF16)]
        + [((length, LANES), F32)] * 3,
        [pltpu.VMEM((model, WIDTH), BF16), pltpu.VMEM((length + HALO, WIDTH), F32), sems(conv_plan)],
    )
    x_ext, nh, cext, act, step, sig, cum = advance(made, *moving)
    rest_z = shards.value
    gate_z = [rest_z[:, :, n * model : (n + 1) * model].reshape(rows, model) for n in range(2)]
    out_z = jnp.concatenate([rest_z[:, :, INNER : INNER + model], rest_z[:, :, INNER + model :]], axis=1)
    out_z = out_z.reshape(2 * rows, model)
    rest = Chain(spread_stages(jnp.concatenate([jnp.concatenate(gate_z), out_z, gain_rows], axis=1)))
    moving[-1] = rest
    local, update, total = advance(
        call(
            local_kernel,
            None,
            [act, step, cum],
            [],
            [(wide, F32), ((STATE, INNER), BF16), ((8, LANES), F32)],
            [pltpu.VMEM((STATE, INNER), F32), pltpu.VMEM((2 * LANES, INNER), BF16)],
        ),
        *moving,
    )
    passing = jnp.repeat(jnp.exp(total[0, :HEADS]), HDIM)[None] if group > 2 else None

    def relay(own, pairs):
        carried = None
        for _ in range(group - 1):
            given = own if carried is None else (passing * carried.astype(F32) + own.astype(F32)).astype(BF16)
            carried = lax.ppermute(given, BOTH, pairs)
        return jnp.zeros_like(own) if carried is None else carried

    state_in = relay(update, neighbour_pairs(1))
    core, states = advance(
        call(
            core_kernel,
            None,
            [local, act, step, cum, state_in],
            [],
            [(wide, F32), ((length // CHUNK, STATE, INNER), BF16)],
            [pltpu.VMEM((STATE, INNER), F32), pltpu.VMEM((2 * CHUNK + 8, INNER), F32),
             pltpu.VMEM((2 * LANES, INNER), BF16)],
        ),
        *moving,
    )
    while rest.pending is not None:
        advance((), *moving)
    if dealt:
        while cot_chain.pending is not None:
            advance((), cot_chain)
        c_pair = cot_chain.value
    else:
        c_pair = to_stretch(cot_given, place)
    rest_pieces = rest.value

    c_own, out, gn, dgate, gcore, rowq, lsg, gskip = call(
        functools.partial(middle_kernel, gate_plan, out_plan, rows),
        scal,
        [core, act, cum, nh, x_ext, *c_pair, skip_row],
        rest_pieces,
        [((length, model), BF16)] * 2 + [(wide, BF16), (wide, BF16), (wide, BF16), ((length, LANES), F32),
         ((STATE, INNER), BF16), ((8, INNER), F32)],
        [pltpu.VMEM((INNER, model + LANES), BF16), pltpu.VMEM((model, INNER), BF16), pltpu.VMEM(wide, F32),
         pltpu.VMEM((8, INNER), F32), pltpu.VMEM((length, model), BF16), pltpu.VMEM(wide, F32),
         pltpu.VMEM((CHUNK, INNER), F32), pltpu.VMEM((CHUNK, INNER), F32), pltpu.VMEM((CHUNK, INNER), F32),
         pltpu.VMEM((CHUNK, INNER), F32), pltpu.VMEM((STATE, INNER), F32),
         pltpu.VMEM((2 * LANES, INNER), BF16), sems(gate_plan), sems(out_plan)],
    )
    if dealt:
        moving = [Chain(output_stages(out, routes, place))]
        out_chain = moving[0]
    else:
        moving = []
        blocks = jnp.stack(swapped(place["seq"] % 2 == 1, from_stretch(out[:block_len], out[block_len:], place)))
        outputs = deal_gathered(blocks, source_of_out)
    grad_out_state = relay(lsg, neighbour_pairs(-1))

    half_dp = devices // 2
    keep1, send1, gcore, dgate = advance(
        call(
            functools.partial(early_kernel, rows, devices),
            scal,
            [gn, c_own, nh, dgate],
            [],
            [((half_dp, 4 * rows, model), BF16)] * 2,
            [pltpu.VMEM((length, model), BF16)],
        )
        + [gcore, dgate],
        *moving,
    )

    early_segments = [(0, shard_rows), (rows, shard_rows), (2 * rows, 2 * shard_rows)]
    early = Chain(reduce_stages(keep1, send1, place, early_segments))
    moving.append(early)
    made = call(
        functools.partial(local_back_kernel, gate_plan, rows),
        scal,
        [act, step, cum, gcore, dgate],
        rest_pieces,
        [(wide, F32), ((length, 2 * STATE), F32), ((length, model), F32)],
        [pltpu.VMEM((model, INNER), BF16), sems(gate_plan)],
    )
    gvl, gk, gng, grad_out_state = advance(made + [grad_out_state], *moving)
    gconv, head, graw, small = advance(
        call(
            scan_back_kernel,
            None,
            [act, step, sig, cum, gcore, gvl, gk, rowq, states, grad_out_state, gskip, skip_row, cext, taps,
             conv_bias_row, decay_row],
            [],
            [((length, CHANNELS), F32), ((HALO, CHANNELS), F32), ((length, LANES), BF16), ((8, WIDTH), F32)],
            [pltpu.VMEM((STATE, INNER), F32), pltpu.VMEM((2 * CHUNK + 8, INNER), F32),
             pltpu.VMEM((CHUNK, CHANNELS), F32), pltpu.VMEM((2 * LANES, INNER), BF16)],
        ),
        *moving,
    )
    ahead = lax.ppermute(head, BOTH, neighbour_pairs(-1))
    sums = Chain(sum_stages(small))
    moving.append(sums)
    gproj, keep2, send2 = advance(
        call(
            functools.partial(conv_back_kernel, rows, devices),
            scal,
            [gconv, ahead, graw, nh, taps],
            [],
            [((length, WIDTH), BF16)] + [((half_dp, rows, WIDTH), BF16)] * 2,
            [],
        ),
        *moving,
    )

    final = Chain(reduce_stages(keep2, send2, place, [(0, shard_rows)]))
    moving.append(final)
    (gtok,) = advance(
        call(
            functools.partial(token_back_kernel, conv_plan, rows),
            scal,
            [gproj, gng, x_ext, c_own],
            conv_pieces,
            [((length, model), BF16)],
            [pltpu.VMEM((model, WIDTH), BF16), pltpu.VMEM((length, model), F32), pltpu.VMEM((length, model), F32),
             pltpu.VMEM((length, LANES), F32), sems(conv_plan)],
        ),
        *moving,
    )

    one, two = from_stretch(gtok[:block_len], gtok[block_len:], place)
    one = advance(one, sums, final)
    back = one, advance(two, sums, final)
    while any(chain.pending is not None for chain in moving):
        advance((), *moving)
    grad_tokens = jnp.stack(swapped(place["seq"] % 2 == 1, back))
    if dealt:
        outputs = out_chain.value

    early_sum, late_sum, sums = early.value, final.value, sums.value
    raw_in = jnp.concatenate(
        [early_sum[:shard_rows], early_sum[shard_rows : 2 * shard_rows],
         late_sum[:, : in_weight.shape[1] - INNER]], axis=1
    )
    raw_out = early_sum[2 * shard_rows :]
    grad_norm_gain = jnp.sum(raw_in * in_weight.astype(F32), axis=1) / norm_gain.astype(F32)
    grad_gate_gain = jnp.sum(raw_out * out_weight.astype(F32), axis=1) / gate_gain.astype(F32)
    grad_skip = jnp.sum(sums[6, :INNER].reshape(HEADS, HDIM), axis=1)
    return (
        outputs[:, None],
        grad_tokens[:, None],
        raw_in,
        raw_out,
        grad_norm_gain,
        grad_gate_gain,
        sums[0:KCONV, :CHANNELS],
        sums[4, :CHANNELS],
        sums[5, :HEADS],
        sums[5, LANES : LANES + HEADS],
        grad_skip,
    )


def solution(mesh):
    in_specs = (
        P(None, "dp", "seq", None),
        P(None, "dp"),
        P(None, "dp"),
        P(None, "dp", "seq", None),
        P(BOTH, None),
        P(BOTH, None),
        P(BOTH),
        P(BOTH),
        P(),
        P(),
        P(),
        P(),
        P(),
    )
    out_specs = (
        P(None, "dp", "seq", None),
        P(None, "dp", "seq", None),
        P(BOTH, None),
        P(BOTH, None),
        P(BOTH),
        P(BOTH),
        P(),
        P(),
        P(),
        P(),
        P(),
    )
    return jax.shard_map(per_device, mesh=mesh, in_specs=in_specs, out_specs=out_specs, check_vma=False)
```
